128 devices in a mesh: dp: 8 (over y, x_hi), cent: 16 (over z, x_lo, core).
Axes of the slice: x: 4 (x_hi: 2, x_lo: 2; x = x_hi * 2 + x_lo), y: 4, z: 4, core: 2. Of those that a mesh axis runs over, the one named last changes fastest.
Arguments:
- embeddings: float32 [8192, 768], P('dp'), may hold values from -6 to 6
- centroids_one: bfloat16 [65536, 768], P('cent'), may hold values from -6 to 6
- centroids_two: bfloat16 [4096, 768], P('dp'), may hold values from -6 to 6
Outputs:
- updated_one: float32 [65536, 768], P('cent', 'dp')
- mass_one: float32 [65536], P('cent')
- updated_two: float32 [4096, 768], P('dp')
- mass_two: float32 [4096], P('dp')
The draws below stay inside these ranges and needn't reach their ends.
All inputs are finite; a program needn't handle non-finite values.
Results may differ from the reference program's by a relative error of at most 0.029.
The reference program's roundings to bfloat16 on the way count: a program that leaves them out, or rounds other values in their place, can miss the bound.
Values may be sent and summed in bfloat16 or wider, within the bound.
No kernel may reach another device: no remote copies, remote signals or barrier semaphores. Data moves between devices by JAX's collectives and lax.ppermute only.
A program may use at most 128 MiB of HBM per device.

```python
import math
import jax
import jax.numpy as jnp
from jax import lax

D = 768
K1 = 65536
K2 = 4096
N_ROWS = 8192


def draw_embeddings(key, part):
    first_key = jax.random.fold_in(key, 11)
    values = jnp.clip(jax.random.normal(first_key, (N_ROWS, D), jnp.float32), -6.0, 6.0)
    return values


def draw_centroids_one(key, part):
    first_key = jax.random.fold_in(key, 21)
    positions = jnp.arange(K1, dtype=jnp.int32).astype(jnp.float32)[:, None]
    radius = (0.7 + 0.65 * positions / K1) / math.sqrt(D)
    values = jnp.clip(jax.random.normal(first_key, (K1, D), jnp.float32), -4.0, 4.0) * radius
    return values.astype(jnp.bfloat16)


def draw_centroids_two(key, part):
    first_key = jax.random.fold_in(key, 31)
    positions = jnp.arange(K2, dtype=jnp.int32).astype(jnp.float32)[:, None]
    radius = (4.0 - 0.2 * positions / K2) / math.sqrt(D)
    values = jnp.clip(jax.random.normal(first_key, (K2, D), jnp.float32), -4.0, 4.0) * radius
    return values.astype(jnp.bfloat16)


def setup_inputs(seed: int = 0) -> dict:
    splits = jax.random.split(jax.random.key(seed), 4)
    return {
        "embeddings": draw_embeddings(jax.random.fold_in(splits[3], 71), 0),
        "centroids_one": draw_centroids_one(jax.random.fold_in(splits[3], 71), 0),
        "centroids_two": draw_centroids_two(jax.random.fold_in(splits[3], 71), 0),
    }


PRIOR = 0.5


def against(left, right):
    return lax.dot_general(left, right, (((1,), (1,)), ((), ())), preferred_element_type=jnp.float32)


def over_rows(left, right):
    return lax.dot_general(left, right, (((0,), (0,)), ((), ())), preferred_element_type=jnp.float32)


def em_update(low_points, centers):
    count_rows = low_points.shape[0]
    width = low_points.shape[1]
    centers_wide = centers.astype(jnp.float32)
    squares = jnp.sum(centers_wide * centers_wide, axis=1)
    block_size = math.gcd(count_rows, 512)
    blocks = low_points.reshape(count_rows // block_size, block_size, width)

    def advance(running, block_rows):
        numerator, mass_sum = running
        scores = 2.0 * against(block_rows, centers) - squares[None, :]
        row_top = jnp.max(scores, axis=1)
        powers = jnp.exp(scores - row_top[:, None])
        totals = jnp.sum(powers, axis=1)
        weights = (powers / totals[:, None]).astype(jnp.bfloat16)
        numerator = numerator + over_rows(weights, block_rows)
        mass_sum = mass_sum + jnp.sum(weights.astype(jnp.float32), axis=0)
        return (numerator, mass_sum), None

    start = (jnp.zeros((centers.shape[0], width), jnp.float32), jnp.zeros((centers.shape[0],), jnp.float32))
    (numerator, mass_sum), unused = lax.scan(advance, start, blocks)
    updated = (numerator + PRIOR * centers_wide) / (mass_sum[:, None] + PRIOR)
    return updated, mass_sum


def reference(embeddings, centroids_one, centroids_two):
    updated_one, mass_one = em_update(embeddings.astype(jnp.bfloat16), centroids_one)
    updated_two, mass_two = em_update(updated_one.astype(jnp.bfloat16), centroids_two)
    return (updated_one, mass_one, updated_two, mass_two)
```

```python
import jax
import jax.numpy as jnp
from jax import lax
from jax.experimental import pallas as pl
from jax.experimental.pallas import tpu as pltpu
from jax.sharding import Mesh, PartitionSpec as P

PRIOR = 0.5
BF = jnp.bfloat16
F32 = jnp.float32
D = 768
SUB = 256


def nt(left, right):
    return lax.dot_general(left, right, (((1,), (1,)), ((), ())), preferred_element_type=F32)


def nn(left, right):
    return lax.dot_general(left, right, (((1,), (0,)), ((), ())), preferred_element_type=F32)


def square_norms(block):
    wide = block.astype(F32)
    return jnp.sum(wide * wide, axis=1, keepdims=True)


def fold_rows(block, op):
    parts = [block[i : i + 8] for i in range(0, block.shape[0], 8)]
    while len(parts) > 1:
        parts = [op(parts[i], parts[i + 1]) for i in range(0, len(parts) - 1, 2)] + (
            [parts[-1]] if len(parts) % 2 else []
        )
    return parts[0]


def scores_kernel(idx_ref, x_ref, c0, c1, c2, c3, p_ref, m_ref, l_ref, norms, scores):
    cents = (c0, c1, c2, c3)

    @pl.when(pl.program_id(0) == 0)
    def _():
        for k in range(4):
            norms[pl.ds(k * 512, 512), :] = jnp.broadcast_to(square_norms(cents[k][...]), (512, 128))

    twice = x_ref[...] * 2
    top = None
    for k in range(4):
        for h in range(2):
            at = k * 512 + h * 256
            s = nt(cents[k][pl.ds(h * 256, 256), :], twice)
            n = norms[pl.ds(at, 256), :]
            s = s - jnp.concatenate([n, n], axis=1)
            scores[pl.ds(at, 256), :] = s
            t = fold_rows(s, jnp.maximum)
            top = t if top is None else jnp.maximum(top, t)
    m = jnp.max(top, axis=0, keepdims=True)
    total = None
    for at in range(0, 2048, 256):
        e = jnp.exp(scores[pl.ds(at, 256), :] - m)
        p_ref[pl.ds(at, 256), :] = e
        t = fold_rows(e, jnp.add)
        total = t if total is None else total + t
    m_ref[...] = m
    l_ref[...] = jnp.sum(total, axis=0, keepdims=True)


def scores_one(x, cents, idx):
    rows = x.shape[0]
    spec = lambda k: pl.BlockSpec((512, D), lambda i, s, k=k: (s[k], 0))
    return pl.pallas_call(
        scores_kernel,
        grid_spec=pltpu.PrefetchScalarGridSpec(
            num_scalar_prefetch=1,
            grid=(rows // SUB,),
            in_specs=[pl.BlockSpec((SUB, D), lambda i, s: (i, 0))] + [spec(k) for k in range(4)],
            out_specs=[
                pl.BlockSpec((2048, SUB), lambda i, s: (0, i)),
                pl.BlockSpec((1, SUB), lambda i, s: (0, i)),
                pl.BlockSpec((1, SUB), lambda i, s: (0, i)),
            ],
            scratch_shapes=[pltpu.VMEM((2048, 128), F32), pltpu.VMEM((2048, SUB), F32)],
        ),
        out_shape=[
            jax.ShapeDtypeStruct((2048, rows), F32),
            jax.ShapeDtypeStruct((1, rows), F32),
            jax.ShapeDtypeStruct((1, rows), F32),
        ],
        name="scores_one",
    )(idx, x, cents, cents, cents, cents)


def sums_kernel(p_ref, q_ref, f_ref, x_ref, y_ref, o_ref, mass_ref, acc, macc):
    i = pl.program_id(0)
    half = pl.num_programs(0) // 2

    @pl.when(i == 0)
    def _():
        acc[...] = jnp.zeros_like(acc)
        macc[...] = jnp.zeros_like(macc)

    def add(p, x):
        w = (p[...] * f_ref[...]).astype(BF)
        acc[...] += nn(w, x[...])
        wide = w.astype(F32)
        part = wide[:, 0:128]
        for j in range(128, wide.shape[1], 128):
            part = part + wide[:, j : j + 128]
        macc[...] += part

    @pl.when(i < half)
    def _():
        add(p_ref, x_ref)

    @pl.when(i >= half)
    def _():
        add(q_ref, y_ref)

    @pl.when(i == pl.num_programs(0) - 1)
    def _():
        o_ref[...] = acc[...].astype(o_ref.dtype)
        t = jnp.broadcast_to(jnp.sum(macc[...], axis=1, keepdims=True), (512, 128))
        mass_ref[...] = t.T[0:1, :]


def sums_one(pa, pb, factor, xa, xb, k, dtype):
    step = 512
    n = xa.shape[0] // step
    first = lambda i: jnp.minimum(i, n - 1)
    second = lambda i: jnp.maximum(i - n, 0)
    return pl.pallas_call(
        sums_kernel,
        grid=(2 * n,),
        in_specs=[
            pl.BlockSpec((512, step), lambda i: (k, first(i))),
            pl.BlockSpec((512, step), lambda i: (k, second(i))),
            pl.BlockSpec((1, step), lambda i: (0, i)),
            pl.BlockSpec((step, D), lambda i: (first(i), 0)),
            pl.BlockSpec((step, D), lambda i: (second(i), 0)),
        ],
        out_specs=[
            pl.BlockSpec((512, D), lambda i: (0, 0)),
            pl.BlockSpec((1, 512), lambda i: (0, 0)),
        ],
        scratch_shapes=[pltpu.VMEM((512, D), F32), pltpu.VMEM((512, 128), F32)],
        out_shape=[jax.ShapeDtypeStruct((512, D), dtype), jax.ShapeDtypeStruct((1, 512), F32)],
        name="sums_one",
    )(pa, pb, factor, xa, xb)


def level_two_kernel(pts_ref, ca_ref, cb_ref, oa_ref, ob_ref, ma_ref, mb_ref, scores, weights):
    pts = pts_ref[...]
    twice = pts * 2
    top = None
    for s_i, c_ref in enumerate((ca_ref, cb_ref)):
        for at in range(0, 2048, 256):
            c = c_ref[pl.ds(at, 256), :]
            s = nt(c, twice) - square_norms(c)
            scores[pl.ds(s_i * 2048 + at, 256), :] = s
            t = fold_rows(s, jnp.maximum)
            top = t if top is None else jnp.maximum(top, t)
    m = jnp.max(top, axis=0, keepdims=True)
    total = None
    for at in range(0, 4096, 256):
        e = jnp.exp(scores[pl.ds(at, 256), :] - m)
        scores[pl.ds(at, 256), :] = e
        t = fold_rows(e, jnp.add)
        total = t if total is None else total + t
    inv = 1.0 / jnp.sum(total, axis=0, keepdims=True)
    for s_i, (o_ref, m_ref) in enumerate(((oa_ref, ma_ref), (ob_ref, mb_ref))):
        for at in range(0, 2048, 256):
            w = (scores[pl.ds(s_i * 2048 + at, 256), :] * inv).astype(BF)
            o_ref[pl.ds(at, 256), :] = nn(w, pts).astype(BF)
            wide = w.astype(F32)
            part = wide[:, 0:128]
            for j in range(128, 512, 128):
                part = part + wide[:, j : j + 128]
            t = jnp.broadcast_to(jnp.sum(part, axis=1, keepdims=True), (256, 128))
            m_ref[:, pl.ds(at, 256)] = t.T[0:1, :]


def level_two(points, ca, cb):
    return pl.pallas_call(
        level_two_kernel,
        scratch_shapes=[pltpu.VMEM((4096, 512), F32), pltpu.VMEM((8, 128), F32)],
        out_shape=[
            jax.ShapeDtypeStruct((2048, D), BF),
            jax.ShapeDtypeStruct((2048, D), BF),
            jax.ShapeDtypeStruct((1, 2048), F32),
            jax.ShapeDtypeStruct((1, 2048), F32),
        ],
        name="level_two",
    )(points, ca, cb)


def shift_y(x, k):
    return lax.ppermute(x, "y", [(i, (i + k) % 4) for i in range(4)])


def shift_z(x, k):
    return lax.ppermute(x, "z", [(i, (i + k) % 4) for i in range(4)])


def flip(x, axis):
    return lax.ppermute(x, axis, [(0, 1), (1, 0)])


def flip_x(x):
    return lax.ppermute(x, ("xh", "xl"), [(0, 3), (1, 2), (2, 1), (3, 0)])


def merge(parts):
    m = parts[0][0]
    for p in parts[1:]:
        m = jnp.maximum(m, p[0])
    s = sum(p[1] * jnp.exp(p[0] - m) for p in parts)
    return jnp.stack([m, s])


def body(embeddings, cents_one, cents_two):
    y = lax.axis_index("y")
    xh = lax.axis_index("xh")
    c = lax.axis_index("c")

    mine = lax.dynamic_slice_in_dim(embeddings, c * 512, 512, 0).astype(BF)
    other = lax.dynamic_slice_in_dim(embeddings, (1 - c) * 512, 512, 0).astype(BF)
    far_mine = flip_x(mine)
    far_other = flip(far_mine, "c")
    xa = jnp.concatenate([mine, other], axis=0)
    xb = jnp.concatenate([far_mine, far_other], axis=0)

    half_two = lax.dynamic_slice_in_dim(cents_two, c * 256, 256, 0)
    same_two = jnp.concatenate([half_two] + [shift_y(half_two, k) for k in (1, 2, 3)], axis=0)
    far_two = flip_x(same_two)
    two_mine = jnp.concatenate([same_two, far_two], axis=0)
    two_theirs = flip(two_mine, "c")

    idx = xh * 4 + (y + jnp.arange(4, dtype=jnp.int32)) % 4
    idx = idx.astype(jnp.int32)
    pa, ma, la = scores_one(xa, cents_one, idx)
    pb, mb, lb = scores_one(xb, cents_one, idx)

    local = jnp.stack([jnp.concatenate([ma, mb], 0), jnp.concatenate([la, lb], 0)]).reshape(2, 2, 2, 512)
    stat = merge([local, flip(local, "c")[:, :, ::-1, :]])
    stat = merge([
        stat,
        flip(stat, "xl"),
        flip(stat, "xh")[:, ::-1],
        flip_x(stat)[:, ::-1],
    ])
    stat = merge([stat] + [shift_z(stat, k) for k in (1, 2, 3)])
    factor = (jnp.exp(local[0] - stat[0]) / stat[1]).reshape(1, 2048)

    own, own_mass = None, None
    got, masses = [], []
    for k in (2, 1, 3):
        part, mass = sums_one(pa, pb, factor, xa, xb, k, BF)
        got.append(shift_y(part, k))
        masses.append((k, mass))
    own, own_mass = sums_one(pa, pb, factor, xa, xb, 0, F32)
    mass_of = dict(masses)
    mass_of[0] = own_mass
    partial_mass = jnp.concatenate([mass_of[k] for k in range(4)], axis=0)
    totals = partial_mass
    for k in (1, 2, 3):
        totals = totals + jnp.roll(shift_y(partial_mass, k), -k, axis=0)
    far_totals = flip(totals, "xh")
    lined = lambda t: lax.dynamic_slice_in_dim(jnp.concatenate([t, t], 0), (4 - y) % 4, 4, 0)
    both = jnp.stack([lined(totals), lined(far_totals)])
    mass_one = jnp.where(xh == 0, both, both[::-1]).reshape(4096)

    block = lax.dynamic_slice_in_dim(cents_one, idx[0] * 512, 512, 0).astype(F32)
    numer = own + sum(g.astype(F32) for g in got)
    points = ((numer + PRIOR * block) / (totals[0][:, None] + PRIOR)).astype(BF)

    tall = points.T.reshape(4, 2 * 96, 512)
    tall = lax.dynamic_slice_in_dim(jnp.concatenate([tall, tall], 0), y, 4, 0)
    pieces = [tall[0]] + [shift_y(tall[k], k) for k in (1, 2, 3)]
    cols = jnp.stack(pieces).reshape(4, 2, 96, 512)
    keep = lax.dynamic_index_in_dim(cols, xh, 1, keepdims=False)
    give = lax.dynamic_index_in_dim(cols, 1 - xh, 1, keepdims=False)
    take = flip(give, "xh")
    both = jnp.stack([jnp.where(xh == 0, keep, take), jnp.where(xh == 0, take, keep)])
    order = (y - jnp.arange(4)) % 4
    both = jnp.take(both, order, axis=1)
    updated_one = both.transpose(0, 1, 3, 2).reshape(4096, 96).astype(F32)

    num_a, num_b, mass_a, mass_b = level_two(points, two_mine, two_theirs)
    num = num_a.astype(F32) + flip(num_b, "c").astype(F32)
    mass = (mass_a + flip(mass_b, "c")).reshape(8, 256)
    num = num.reshape(8, 256, D)

    def carry(values, weights):
        hi = weights.astype(BF)
        rest = weights - hi.astype(F32)
        mid = rest.astype(BF)
        low = (rest - mid.astype(F32)).astype(BF)
        row = jnp.stack([hi, mid, low]).reshape(1, D)
        return jnp.concatenate([values.astype(BF), row, jnp.zeros((15, D), BF)], axis=0)

    def split(packed):
        wide = packed.astype(F32)
        return wide[:256], jnp.sum(wide[256].reshape(3, 256), axis=0)

    def dp_move(value, j, b):
        if b == 0:
            return shift_y(value, -j)
        pairs = []
        for a in range(4):
            for h in range(2):
                for l in range(2):
                    pairs.append((a * 4 + h * 2 + l, ((a - j) % 4) * 4 + (1 - h) * 2 + (1 - l)))
        return lax.ppermute(value, ("y", "xh", "xl"), pairs)

    tot, tmass = num[0], mass[0]
    for j, b in ((2, 1), (2, 0), (1, 1), (3, 1), (0, 1), (1, 0), (3, 0)):
        v, w = split(dp_move(carry(num[b * 4 + j], mass[b * 4 + j]), j, b))
        tot, tmass = tot + v, tmass + w
    packed = carry(tot, tmass)
    for k in (2, 1, 3):
        v, w = split(shift_z(packed, k))
        tot, tmass = tot + v, tmass + w
    v, w = split(flip(carry(tot, tmass), "xl"))
    tot, tmass = tot + v, tmass + w
    fin = (tot + PRIOR * half_two.astype(F32)) / (tmass[:, None] + PRIOR)
    fin_other = flip(fin, "c")
    mass_other = flip(tmass, "c")
    low = c == 0
    updated_two = jnp.concatenate(
        [jnp.where(low, fin, fin_other), jnp.where(low, fin_other, fin)], axis=0
    )
    mass_two = jnp.concatenate(
        [jnp.where(low, tmass, mass_other), jnp.where(low, mass_other, tmass)], axis=0
    )
    return updated_one, mass_one, updated_two, mass_two


def solution(mesh):
    fine = Mesh(mesh.devices.reshape(4, 2, 4, 2, 2), ("y", "xh", "z", "xl", "c"))
    dp, cent = ("y", "xh"), ("z", "xl", "c")
    return jax.shard_map(
        body,
        mesh=fine,
        in_specs=(P(dp, None), P(cent, None), P(dp, None)),
        out_specs=(P(cent, dp), P(cent), P(dp, None), P(dp)),
        check_vma=False,
    )
```

```python
import jax
import jax.numpy as jnp
from jax import lax
from jax.experimental import pallas as pl
from jax.experimental.pallas import tpu as pltpu
from jax.sharding import Mesh, PartitionSpec as P

PRIOR = 0.5
BF = jnp.bfloat16
F32 = jnp.float32
D = 768
TALL = 208
SMEM = pl.BlockSpec(memory_space=pltpu.SMEM)
VMEM = pl.BlockSpec(memory_space=pltpu.VMEM)


def nt(left, right):
    return lax.dot_general(left, right, (((1,), (1,)), ((), ())), preferred_element_type=F32)


def nn(left, right):
    return lax.dot_general(left, right, (((1,), (0,)), ((), ())), preferred_element_type=F32)


def shape(dims, dtype):
    return jax.ShapeDtypeStruct(dims, dtype)


def cost(flops, exps=0, size=1 << 20):
    return pl.CostEstimate(flops=flops, transcendentals=exps, bytes_accessed=size)


def square_norms(block):
    wide = block.astype(F32)
    return jnp.sum(wide * wide, axis=1, keepdims=True)


def fold_rows(block, op):
    parts = [block[i : i + 8] for i in range(0, block.shape[0], 8)]
    while len(parts) > 1:
        parts = [op(parts[i], parts[i + 1]) for i in range(0, len(parts) - 1, 2)] + (
            [parts[-1]] if len(parts) % 2 else []
        )
    return parts[0]


def lane_sums(w):
    wide = w.astype(F32)
    part = wide[:, 0:128]
    for j in range(128, wide.shape[1], 128):
        part = part + wide[:, j : j + 128]
    return jnp.sum(part, axis=1, keepdims=True)


def as_row(column):
    return jnp.broadcast_to(column, (column.shape[0], 128)).T[0:1, :]


def as_column(row):
    return jnp.broadcast_to(row, (128, row.shape[1])).T[:, 0:1]


def mass_rows(row):
    t = jnp.broadcast_to(row, (16, row.shape[1]))
    hi = t.astype(BF).astype(F32)
    mid = (t - hi).astype(BF).astype(F32)
    low = t - hi - mid
    at = lax.broadcasted_iota(jnp.int32, t.shape, 0)
    return jnp.where(at == 0, hi, jnp.where(at == 1, mid, jnp.where(at == 2, low, 0.0)))


def scores_step(cents, twice, norms, p_ref, scores):
    top = None
    for k in range(4):
        for h in range(2):
            at = k * 512 + h * 256
            n = norms[pl.ds(at, 256), :]
            s = nt(cents[k][pl.ds(h * 256, 256), :], twice) - jnp.concatenate([n, n], axis=1)
            scores[pl.ds(at, 256), :] = s
            t = fold_rows(s, jnp.maximum)
            top = t if top is None else jnp.maximum(top, t)
    m = jnp.max(top, axis=0, keepdims=True)
    total = None
    for at in range(0, 2048, 256):
        e = jnp.exp(scores[pl.ds(at, 256), :] - m)
        p_ref[pl.ds(at, 256), :] = e
        t = fold_rows(e, jnp.add)
        total = t if total is None else total + t
    return m, jnp.sum(total, axis=0, keepdims=True)


def put_stats(stat_ref, row, i, m, l):
    cols = pl.ds(pl.multiple_of(lax.rem(i, 2) * 256, 256), 256)
    stat_ref[pl.ds(row, 1), cols] = m
    stat_ref[pl.ds(4 + row, 1), cols] = l


def scores_near_kernel(idx, a_ref, b_ref, c0, c1, c2, c3, p_ref, x_ref, stat_ref, norms_ref, scores):
    i = pl.program_id(0)
    cents = (c0, c1, c2, c3)

    @pl.when(i == 0)
    def _():
        stat_ref[...] = jnp.zeros_like(stat_ref)
        for k in range(4):
            for h in range(2):
                n = square_norms(cents[k][pl.ds(h * 256, 256), :])
                norms_ref[pl.ds(k * 512 + h * 256, 256), :] = jnp.broadcast_to(n, (256, 128))

    x = jnp.where(i < 2, a_ref[...], b_ref[...])
    x_ref[...] = x
    m, l = scores_step(cents, x * 2, norms_ref, p_ref, scores)
    put_stats(stat_ref, idx[4 + i // 2], i, m, l)


def scores_far_kernel(idx, a_ref, b_ref, c0, c1, c2, c3, norms_ref, near_ref, p_old, x_old, p_ref, x_ref, stat_ref, scores):
    i = pl.program_id(0)

    @pl.when(i == 0)
    def _():
        stat_ref[...] = near_ref[...]

    x = jnp.where(i < 2, a_ref[...], b_ref[...])
    x_ref[...] = x
    m, l = scores_step((c0, c1, c2, c3), x * 2, norms_ref, p_ref, scores)
    put_stats(stat_ref, idx[6 + i // 2], i, m, l)


ANY = pl.BlockSpec(memory_space=pl.ANY)
ROW_IN = [
    pl.BlockSpec((256, D), lambda i, s: (jnp.minimum(i, 1), 0)),
    pl.BlockSpec((256, D), lambda i, s: (jnp.maximum(i - 2, 0), 0)),
]
CENTS_IN = [pl.BlockSpec((512, D), lambda i, s, k=k: (s[k], 0)) for k in range(4)]
WHOLE_STAT = pl.BlockSpec((8, 512), lambda i, s: (0, 0))
WHOLE_NORMS = pl.BlockSpec((2048, 128), lambda i, s: (0, 0))


def scores_near(idx, a, b, cents):
    return pl.pallas_call(
        scores_near_kernel,
        grid_spec=pltpu.PrefetchScalarGridSpec(
            num_scalar_prefetch=1,
            grid=(4,),
            in_specs=ROW_IN + CENTS_IN,
            out_specs=[
                pl.BlockSpec((2048, 256), lambda i, s: (0, i)),
                pl.BlockSpec((256, D), lambda i, s: (i, 0)),
                WHOLE_STAT,
                WHOLE_NORMS,
            ],
            scratch_shapes=[pltpu.VMEM((2048, 256), F32)],
        ),
        out_shape=[
            shape((2048, 2048), F32),
            shape((2048, D), BF),
            shape((8, 512), F32),
            shape((2048, 128), F32),
        ],
        cost_estimate=cost(2 * 2048 * 1024 * D, 2048 * 1024),
        name="scores_near",
    )(idx, a, b, cents, cents, cents, cents)


def scores_far(idx, a, b, cents, norms, near, p, x):
    return pl.pallas_call(
        scores_far_kernel,
        grid_spec=pltpu.PrefetchScalarGridSpec(
            num_scalar_prefetch=1,
            grid=(4,),
            in_specs=ROW_IN + CENTS_IN + [WHOLE_NORMS, WHOLE_STAT, ANY, ANY],
            out_specs=[
                pl.BlockSpec((2048, 256), lambda i, s: (0, 4 + i)),
                pl.BlockSpec((256, D), lambda i, s: (4 + i, 0)),
                WHOLE_STAT,
            ],
            scratch_shapes=[pltpu.VMEM((2048, 256), F32)],
        ),
        out_shape=[shape((2048, 2048), F32), shape((2048, D), BF), shape((8, 512), F32)],
        input_output_aliases={9: 0, 10: 1},
        cost_estimate=cost(2 * 2048 * 1024 * D, 2048 * 1024),
        name="scores_far",
    )(idx, a, b, cents, cents, cents, cents, norms, near, p, x)


def merge_all(stats):
    m = stats[0][0:4]
    for t in stats[1:]:
        m = jnp.maximum(m, t[0:4])
    total = None
    for t in stats:
        part = t[4:8] * jnp.exp(t[0:4] - m)
        total = part if total is None else total + part
    return m, total


def merge_cores(local, other):
    def kernel(a, b, o_ref):
        m, total = merge_all([a[...], b[...]])
        both = jnp.concatenate([m, total], axis=0)
        for i in range(16):
            o_ref[i] = both

    return pl.pallas_call(
        kernel, in_specs=[VMEM] * 2, out_shape=shape((16, 8, 512), F32), name="merge_cores"
    )(local, other)


def merge_last(idx, stats, local):
    def kernel(idx_ref, s_ref, l_ref, f_ref, tmp):
        m, total = merge_all([s_ref[i] for i in range(16)])
        tmp[0:4, :] = jnp.exp(l_ref[0:4, :] - m) / total
        for r in range(4):
            f_ref[:, r * 512 : (r + 1) * 512] = tmp[pl.ds(idx_ref[4 + r], 1), :]

    return pl.pallas_call(
        kernel,
        in_specs=[SMEM] + [VMEM] * 2,
        scratch_shapes=[pltpu.VMEM((8, 512), F32)],
        out_shape=shape((1, 2048), F32),
        name="merge_last",
    )(idx, stats, local)


def sums_one(p, factor, x, masses, first, count, dtype):
    def kernel(p_ref, f_ref, x_ref, old_ref, o_ref, mass_ref, acc, macc):
        j, i = pl.program_id(0), pl.program_id(1)
        w = (p_ref[...] * f_ref[...]).astype(BF)
        part = nn(w, x_ref[...])
        wide = w.astype(F32)
        lanes = wide[:, 0:128]
        for at in range(128, 1024, 128):
            lanes = lanes + wide[:, at : at + 128]

        @pl.when((i == 0) & (j == 0))
        def _():
            mass_ref[...] = old_ref[...]

        @pl.when(i == 0)
        def _():
            acc[...] = part
            macc[...] = lanes

        @pl.when(i == 1)
        def _():
            o_ref[...] = (acc[...] + part).astype(o_ref.dtype)
            mass = jnp.sum(macc[...] + lanes, axis=1, keepdims=True)
            mass_ref[pl.ds(first + 2 * j, 1), :] = as_row(mass)

    return pl.pallas_call(
        kernel,
        grid=(count, 2),
        in_specs=[
            pl.BlockSpec((512, 1024), lambda j, i: (first + 2 * j, i)),
            pl.BlockSpec((1, 1024), lambda j, i: (0, i)),
            pl.BlockSpec((1024, D), lambda j, i: (i, 0)),
            pl.BlockSpec((4, 512), lambda j, i: (0, 0)),
        ],
        out_specs=[
            pl.BlockSpec((512, D), lambda j, i: (j, 0)),
            pl.BlockSpec((4, 512), lambda j, i: (0, 0)),
        ],
        scratch_shapes=[pltpu.VMEM((512, D), F32), pltpu.VMEM((512, 128), F32)],
        out_shape=[shape((512 * count, D), dtype), shape((4, 512), F32)],
        name="sums_one",
    )(p, factor, x, masses)


def finish_one(idx, own, got, cents, masses, far_masses):
    def kernel(idx_ref, own_ref, g1, g2, g3, cents_ref, m0, m1, m2, m3, pts_ref, mass_ref):
        total = m0[...]
        for k, ref in ((1, m1), (2, m2), (3, m3)):
            t = ref[...]
            total = total + jnp.concatenate([t[k:], t[:k]], axis=0)
        mass_ref[...] = total
        i = pl.program_id(0)
        column = as_column(mass_ref[0:1, pl.ds(pl.multiple_of(i * 128, 128), 128)]) + PRIOR
        num = own_ref[...] + g1[...].astype(F32) + g2[...].astype(F32) + g3[...].astype(F32)
        num = num + PRIOR * cents_ref[...].astype(F32)
        pts_ref[...] = (num / column).astype(BF)

    rows = pl.BlockSpec((128, D), lambda i, s: (i, 0))
    small = pl.BlockSpec((4, 512), lambda i, s: (0, 0))
    return pl.pallas_call(
        kernel,
        grid_spec=pltpu.PrefetchScalarGridSpec(
            num_scalar_prefetch=1,
            grid=(4,),
            in_specs=[rows] * 4 + [pl.BlockSpec((128, D), lambda i, s: (s[0] * 4 + i, 0))] + [small] * 4,
            out_specs=[rows, small],
        ),
        out_shape=[shape((512, D), BF), shape((4, 512), F32)],
        name="finish_one",
    )(idx, own, *got, cents, masses, *far_masses)


def turn_points(points):
    def kernel(p_ref, o_ref):
        o_ref[...] = p_ref[...].astype(F32).T.astype(BF)

    return pl.pallas_call(
        kernel,
        grid=(6,),
        in_specs=[pl.BlockSpec((512, 128), lambda i: (0, i))],
        out_specs=pl.BlockSpec((128, 512), lambda i: (i, 0)),
        out_shape=shape((D, 512), BF),
        name="turn_points",
    )(points)


def gather_one(place, keep, take, totals, far_totals):
    def kernel(place_ref, keep_ref, take_ref, t_ref, f_ref, o_ref, m_ref):
        y, near = place_ref[0], place_ref[1]
        for ref, half in ((keep_ref, near), (take_ref, 1 - near)):
            for k in range(4):
                start = half * 2048 + lax.rem(y + 4 - k, 4) * 512
                o_ref[:, pl.ds(pl.multiple_of(start, 512), 512)] = ref[k].astype(F32)
        for ref, half in ((t_ref, near), (f_ref, 1 - near)):
            for j in range(4):
                m_ref[pl.ds(half * 4 + lax.rem(y + j, 4), 1), :] = ref[j : j + 1, :]

    return pl.pallas_call(
        kernel,
        in_specs=[SMEM] + [VMEM] * 4,
        out_shape=[shape((96, 4096), F32), shape((8, 512), F32)],
        name="gather_one",
    )(place, keep, take, totals, far_totals)


def norms_two(two):
    def kernel(c_ref, o_ref):
        o_ref[...] = jnp.broadcast_to(square_norms(c_ref[...]), (256, 128))

    return pl.pallas_call(
        kernel,
        grid=(8,),
        in_specs=[pl.BlockSpec((256, D), lambda i: (i, 0))],
        out_specs=pl.BlockSpec((256, 128), lambda i: (i, 0)),
        out_shape=shape((2048, 128), F32),
        name="norms_two",
    )(two)


def scores_two(slots, a, b, two, norms):
    def kernel(slots_ref, a_ref, b_ref, c_ref, n_ref, p_ref, stat_ref, scores):
        i = pl.program_id(0)
        twice = jnp.where(i < 2, a_ref[...], b_ref[...]) * 2
        top = None
        for d in range(8):
            here = pl.ds(pl.multiple_of(slots_ref[d] * 256, 256), 256)
            n = n_ref[here, :]
            s = nt(c_ref[here, :], twice) - jnp.concatenate([n, n], axis=1)
            scores[pl.ds(d * 256, 256), :] = s
            t = fold_rows(s, jnp.maximum)
            top = t if top is None else jnp.maximum(top, t)
        m = jnp.max(top, axis=0, keepdims=True)
        total = None
        for at in range(0, 2048, 256):
            e = jnp.exp(scores[pl.ds(at, 256), :] - m)
            p_ref[pl.ds(at, 256), :] = e
            t = fold_rows(e, jnp.add)
            total = t if total is None else total + t
        stat_ref[0:1, :] = m
        stat_ref[1:2, :] = jnp.sum(total, axis=0, keepdims=True)

    return pl.pallas_call(
        kernel,
        grid_spec=pltpu.PrefetchScalarGridSpec(
            num_scalar_prefetch=1,
            grid=(4,),
            in_specs=ROW_IN + [pl.BlockSpec((2048, D), lambda i, s: (0, 0)), WHOLE_NORMS],
            out_specs=[
                pl.BlockSpec((2048, 256), lambda i, s: (0, i)),
                pl.BlockSpec((2, 256), lambda i, s: (0, i)),
            ],
            scratch_shapes=[pltpu.VMEM((2048, 256), F32)],
        ),
        out_shape=[shape((2048, 1024), F32), shape((2, 1024), F32)],
        cost_estimate=cost(2 * 2048 * 1024 * D, 2048 * 1024),
        name="scores_two",
    )(slots, a, b, two, norms)


def sums_two(p, stat, other, a, b):
    def kernel(p_ref, s_ref, r_ref, a_ref, b_ref, o_ref, rows, factor):
        @pl.when(pl.program_id(0) == 0)
        def _():
            rows[0:512, :] = a_ref[...]
            rows[512:1024, :] = b_ref[...]
            theirs = jnp.concatenate([r_ref[:, 512:1024], r_ref[:, 0:512]], axis=1)
            mine = s_ref[...]
            m = jnp.maximum(mine[0:1], theirs[0:1])
            near = jnp.exp(mine[0:1] - m)
            total = mine[1:2] * near + theirs[1:2] * jnp.exp(theirs[0:1] - m)
            factor[0:1, :] = near / total

        w = (p_ref[...] * factor[0:1, :]).astype(BF)
        num = nn(w, rows[...])
        packed = mass_rows(as_row(lane_sums(w)))
        for q in range(8):
            for j in range(6):
                o_ref[q, j * 32 : j * 32 + 32, :] = num[q * 32 : q * 32 + 32, j * 128 : j * 128 + 128].astype(BF)
            lanes = packed[:, (q // 4) * 128 : (q // 4) * 128 + 128]
            turn = (128 - (q % 4) * 32) % 128
            o_ref[q, 192:TALL, :] = (pltpu.roll(lanes, turn, 1) if turn else lanes).astype(BF)

    whole = lambda r, c: pl.BlockSpec((r, c), lambda i: (0, 0))
    return pl.pallas_call(
        kernel,
        grid=(8,),
        in_specs=[pl.BlockSpec((256, 1024), lambda i: (i, 0)), whole(2, 1024), whole(2, 1024), whole(512, D), whole(512, D)],
        out_specs=pl.BlockSpec((8, TALL, 128), lambda i: (i, 0, 0)),
        scratch_shapes=[pltpu.VMEM((1024, D), BF), pltpu.VMEM((8, 1024), F32)],
        out_shape=shape((64, TALL, 128), BF),
        cost_estimate=cost(2 * 2048 * 1024 * D),
        name="sums_two",
    )(p, stat, other, a, b)


def finish_two(parts, cents):
    def kernel(x_ref, c_ref, o_ref, acc):
        i = pl.program_id(0)
        total = x_ref[0].astype(F32)
        for q in range(1, 8):
            total = total + x_ref[q].astype(F32)

        @pl.when(i == 0)
        def _():
            acc[...] = total

        @pl.when(i > 0)
        def _():
            acc[...] += total

        @pl.when(i == 7)
        def _():
            mass = acc[192:193, :] + acc[193:194, :] + acc[194:195, :]
            column = as_column(mass)[0:32] + PRIOR
            packed = mass_rows(mass).astype(BF)
            for j in range(6):
                num = acc[j * 32 : j * 32 + 32, :] + PRIOR * c_ref[:, j * 128 : j * 128 + 128].astype(F32)
                new = (num / column).astype(BF)
                for q in range(8):
                    o_ref[q, j * 32 : j * 32 + 32, :] = new
            for q in range(8):
                o_ref[q, 192:TALL, :] = packed

    return pl.pallas_call(
        kernel,
        grid=(8,),
        in_specs=[
            pl.BlockSpec((8, TALL, 128), lambda i: (i, 0, 0)),
            pl.BlockSpec((32, D), lambda i: (0, 0)),
        ],
        out_specs=pl.BlockSpec((8, TALL, 128), lambda i: (0, 0, 0)),
        scratch_shapes=[pltpu.VMEM((TALL, 128), F32)],
        out_shape=shape((8, TALL, 128), BF),
        name="finish_two",
    )(parts, cents)


def gather_two(core, mine, theirs):
    def kernel(core_ref, a_ref, b_ref, o_ref, m_ref):
        lane = lax.broadcasted_iota(jnp.int32, (16, 128), 1)
        for ref, half in ((a_ref, core_ref[0]), (b_ref, 1 - core_ref[0])):
            start = pl.multiple_of(half * 256, 256)
            for q in range(8):
                for j in range(6):
                    o_ref[pl.ds(start + q * 32, 32), j * 128 : j * 128 + 128] = ref[q, j * 32 : j * 32 + 32, :].astype(F32)
            for g in range(2):
                row = None
                for r in range(4):
                    t = ref[g * 4 + r, 192:TALL, :].astype(F32)
                    t = pltpu.roll(t, r * 32, 1) if r else t
                    row = t if row is None else jnp.where(lane >= r * 32, t, row)
                m_ref[:, pl.ds(start + g * 128, 128)] = row[0:1] + row[1:2] + row[2:3]

    return pl.pallas_call(
        kernel,
        in_specs=[SMEM] + [VMEM] * 2,
        out_shape=[shape((512, D), F32), shape((1, 512), F32)],
        name="gather_two",
    )(core, mine, theirs)


def shift_y(x, k):
    return lax.ppermute(x, "y", [(i, (i + k) % 4) for i in range(4)])


def shift_z(x, k):
    return lax.ppermute(x, "z", [(i, (i + k) % 4) for i in range(4)])


def flip(x, axis):
    return lax.ppermute(x, axis, [(0, 1), (1, 0)])


def flip_x(x):
    return lax.ppermute(x, ("xh", "xl"), [(0, 3), (1, 2), (2, 1), (3, 0)])


def after(x, *others):
    return lax.optimization_barrier((x,) + others)[0]


def body(embeddings, cents_one, cents_two):
    y = lax.axis_index("y").astype(jnp.int32)
    xh = lax.axis_index("xh").astype(jnp.int32)
    z = lax.axis_index("z").astype(jnp.int32)
    xl = lax.axis_index("xl").astype(jnp.int32)
    c = lax.axis_index("c").astype(jnp.int32)
    halves = jnp.stack([xh * 2 + c, xh * 2 + 1 - c, 2 - xh * 2 + c, 3 - xh * 2 - c])
    idx = jnp.concatenate([xh * 4 + (y + jnp.arange(4, dtype=jnp.int32)) % 4, halves])
    to = jnp.arange(8, dtype=jnp.int32)
    slots = (xh ^ (to % 2)) * 4 + (y - to // 2) % 4

    mine = lax.dynamic_slice_in_dim(embeddings, c * 512, 512, 0).astype(BF)
    far_mine = flip_x(mine)
    other = lax.dynamic_slice_in_dim(embeddings, (1 - c) * 512, 512, 0).astype(BF)
    p, x, near, norms = scores_near(idx, mine, other, cents_one)
    far_mine = after(far_mine, near)
    far_other = flip(far_mine, "c")
    p, x, local = scores_far(idx, far_mine, far_other, cents_one, norms, near, p, x)

    spread = merge_cores(local, flip(local, "c"))
    stats = lax.all_to_all(spread, ("xh", "z", "xl"), 0, 0, tiled=True)

    half_two = after(lax.dynamic_slice_in_dim(cents_two, c * 256, 256, 0), spread)
    around = [shift_y(half_two, k) for k in (1, 2, 3)]

    factor = merge_last(idx, stats, local)
    masses = jnp.zeros((4, 512), F32)
    part, masses = sums_one(p, factor, x, masses, 2, 1, BF)
    same_two = jnp.concatenate([half_two] + [after(t, part) for t in around], axis=0)
    got = {2: shift_y(part, 2)}
    part, masses = sums_one(p, factor, x, masses, 1, 2, BF)
    got[1], got[3] = shift_y(part[0:512], 1), shift_y(part[512:1024], 3)
    own, masses = sums_one(p, factor, x, masses, 0, 1, F32)

    far_two = after(flip_x(same_two), masses)
    two = jnp.concatenate([same_two, far_two], axis=0)
    norms = norms_two(two)

    points, totals = finish_one(
        idx, after(own, norms), [got[k] for k in (1, 2, 3)], cents_one, masses, [shift_y(masses, k) for k in (1, 2, 3)]
    )
    their_points = flip(points, "c")
    tall = turn_points(points)
    p2, stat2 = scores_two(slots, after(points, tall), their_points, two, norms)
    other2 = flip(stat2, "c")

    cut = lambda d: lax.dynamic_slice_in_dim(tall, ((y + d) % 4) * 192, 192, 0)
    cols = jnp.stack([cut(0)] + [shift_y(cut(k), k) for k in (1, 2, 3)]).reshape(4, 2, 96, 512)
    keep = lax.dynamic_index_in_dim(cols, xh, 1, keepdims=False)
    take = flip(lax.dynamic_index_in_dim(cols, 1 - xh, 1, keepdims=False), "xh")
    far_totals = flip(totals, "xh")

    packed = sums_two(p2, stat2, other2, points, their_points)
    packed = after(packed, take, far_totals)
    parts = lax.all_to_all(packed, ("y", "xh", "z", "xl"), 0, 0, tiled=True)
    turned_one, mass_one = gather_one(jnp.stack([y, xh]), keep, take, totals, far_totals)
    rows = lax.dynamic_slice_in_dim(cents_two, c * 256 + z * 64 + xl * 32, 32, 0)
    spread = finish_two(parts, after(rows, turned_one))
    block = lax.all_to_all(spread, ("z", "xl"), 0, 0, tiled=True)
    updated_two, mass_two = gather_two(c[None], block, flip(block, "c"))
    return turned_one.T, mass_one.reshape(4096), updated_two, mass_two.reshape(512)


def solution(mesh):
    fine = Mesh(mesh.devices.reshape(4, 2, 4, 2, 2), ("y", "xh", "z", "xl", "c"))
    dp, cent = ("y", "xh"), ("z", "xl", "c")
    return jax.shard_map(
        body,
        mesh=fine,
        in_specs=(P(dp, None), P(cent, None), P(dp, None)),
        out_specs=(P(cent, dp), P(cent), P(dp, None), P(dp)),
        check_vma=False,
    )
```

```python
import jax
import jax.numpy as jnp
from jax import lax
from jax.experimental import pallas as pl
from jax.experimental.pallas import tpu as pltpu
from jax.sharding import Mesh, PartitionSpec as P

PRIOR = 0.5
BF = jnp.bfloat16
F32 = jnp.float32
D = 768
TALL = 208
SMEM = pl.BlockSpec(memory_space=pltpu.SMEM)
VMEM = pl.BlockSpec(memory_space=pltpu.VMEM)


def nt(left, right):
    return lax.dot_general(left, right, (((1,), (1,)), ((), ())), preferred_element_type=F32)


def nn(left, right):
    return lax.dot_general(left, right, (((1,), (0,)), ((), ())), preferred_element_type=F32)


def shape(dims, dtype):
    return jax.ShapeDtypeStruct(dims, dtype)


def square_norms(block):
    wide = block.astype(F32)
    return jnp.sum(wide * wide, axis=1, keepdims=True)


def fold_rows(block, op):
    parts = [block[i : i + 8] for i in range(0, block.shape[0], 8)]
    while len(parts) > 1:
        parts = [op(parts[i], parts[i + 1]) for i in range(0, len(parts) - 1, 2)] + (
            [parts[-1]] if len(parts) % 2 else []
        )
    return parts[0]


def lane_sums(w):
    wide = w.astype(F32)
    part = wide[:, 0:128]
    for j in range(128, wide.shape[1], 128):
        part = part + wide[:, j : j + 128]
    return jnp.sum(part, axis=1, keepdims=True)


def as_row(column):
    return jnp.broadcast_to(column, (column.shape[0], 128)).T[0:1, :]


def as_column(row):
    return jnp.broadcast_to(row, (128, row.shape[1])).T[:, 0:1]


def mass_rows(row):
    t = jnp.broadcast_to(row, (16, row.shape[1]))
    hi = t.astype(BF).astype(F32)
    mid = (t - hi).astype(BF).astype(F32)
    low = t - hi - mid
    at = lax.broadcasted_iota(jnp.int32, t.shape, 0)
    return jnp.where(at == 0, hi, jnp.where(at == 1, mid, jnp.where(at == 2, low, 0.0)))


def scores_step(cents, twice, norms, p_ref, scores):
    top = None
    for k in range(4):
        for h in range(2):
            at = k * 512 + h * 256
            n = norms[pl.ds(at, 256), :]
            s = nt(cents[k][pl.ds(h * 256, 256), :], twice) - jnp.concatenate([n, n], axis=1)
            scores[pl.ds(at, 256), :] = s
            t = fold_rows(s, jnp.maximum)
            top = t if top is None else jnp.maximum(top, t)
    m = jnp.max(top, axis=0, keepdims=True)
    total = None
    for at in range(0, 2048, 256):
        e = jnp.exp(scores[pl.ds(at, 256), :] - m)
        p_ref[pl.ds(at, 256), :] = e
        t = fold_rows(e, jnp.add)
        total = t if total is None else total + t
    return m, jnp.sum(total, axis=0, keepdims=True)


def put_stats(stat_ref, row, i, m, l):
    cols = pl.ds(pl.multiple_of(lax.rem(i, 2) * 256, 256), 256)
    stat_ref[pl.ds(row, 1), cols] = m
    stat_ref[pl.ds(4 + row, 1), cols] = l


def scores_near_kernel(idx, a_ref, b_ref, c0, c1, c2, c3, p_ref, x_ref, stat_ref, norms_ref, scores):
    i = pl.program_id(0)
    cents = (c0, c1, c2, c3)

    @pl.when(i == 0)
    def _():
        stat_ref[...] = jnp.zeros_like(stat_ref)
        for k in range(4):
            for h in range(2):
                n = square_norms(cents[k][pl.ds(h * 256, 256), :])
                norms_ref[pl.ds(k * 512 + h * 256, 256), :] = jnp.broadcast_to(n, (256, 128))

    x = jnp.where(i < 2, a_ref[...], b_ref[...])
    x_ref[...] = x
    m, l = scores_step(cents, x * 2, norms_ref, p_ref, scores)
    put_stats(stat_ref, idx[4 + i // 2], i, m, l)


def scores_far_kernel(idx, a_ref, b_ref, c0, c1, c2, c3, norms_ref, near_ref, p_old, x_old, p_ref, x_ref, stat_ref, scores):
    i = pl.program_id(0)

    @pl.when(i == 0)
    def _():
        stat_ref[...] = near_ref[...]

    x = jnp.where(i < 2, a_ref[...], b_ref[...])
    x_ref[...] = x
    m, l = scores_step((c0, c1, c2, c3), x * 2, norms_ref, p_ref, scores)
    put_stats(stat_ref, idx[6 + i // 2], i, m, l)


ANY = pl.BlockSpec(memory_space=pl.ANY)
ROW_IN = [
    pl.BlockSpec((256, D), lambda i, s: (jnp.minimum(i, 1), 0)),
    pl.BlockSpec((256, D), lambda i, s: (jnp.maximum(i - 2, 0), 0)),
]
CENTS_IN = [pl.BlockSpec((512, D), lambda i, s, k=k: (s[k], 0)) for k in range(4)]
WHOLE_STAT = pl.BlockSpec((8, 512), lambda i, s: (0, 0))
WHOLE_NORMS = pl.BlockSpec((2048, 128), lambda i, s: (0, 0))


def scores_near(idx, a, b, cents):
    return pl.pallas_call(
        scores_near_kernel,
        grid_spec=pltpu.PrefetchScalarGridSpec(
            num_scalar_prefetch=1,
            grid=(4,),
            in_specs=ROW_IN + CENTS_IN,
            out_specs=[
                pl.BlockSpec((2048, 256), lambda i, s: (0, i)),
                pl.BlockSpec((256, D), lambda i, s: (i, 0)),
                WHOLE_STAT,
                WHOLE_NORMS,
            ],
            scratch_shapes=[pltpu.VMEM((2048, 256), F32)],
        ),
        out_shape=[
            shape((2048, 2048), F32),
            shape((2048, D), BF),
            shape((8, 512), F32),
            shape((2048, 128), F32),
        ],
        cost_estimate=pl.CostEstimate(
            flops=2 * 2048 * 1024 * D, transcendentals=2048 * 1024, bytes_accessed=24 << 20
        ),
        name="scores_near",
    )(idx, a, b, cents, cents, cents, cents)


def scores_far(idx, a, b, cents, norms, near, p, x):
    return pl.pallas_call(
        scores_far_kernel,
        grid_spec=pltpu.PrefetchScalarGridSpec(
            num_scalar_prefetch=1,
            grid=(4,),
            in_specs=ROW_IN + CENTS_IN + [WHOLE_NORMS, WHOLE_STAT, ANY, ANY],
            out_specs=[
                pl.BlockSpec((2048, 256), lambda i, s: (0, 4 + i)),
                pl.BlockSpec((256, D), lambda i, s: (4 + i, 0)),
                WHOLE_STAT,
            ],
            scratch_shapes=[pltpu.VMEM((2048, 256), F32)],
        ),
        out_shape=[shape((2048, 2048), F32), shape((2048, D), BF), shape((8, 512), F32)],
        input_output_aliases={9: 0, 10: 1},
        name="scores_far",
    )(idx, a, b, cents, cents, cents, cents, norms, near, p, x)


def merge_all(stats):
    m = stats[0][0:4]
    for t in stats[1:]:
        m = jnp.maximum(m, t[0:4])
    total = None
    for t in stats:
        part = t[4:8] * jnp.exp(t[0:4] - m)
        total = part if total is None else total + part
    return m, total


def merge_cores(local, other):
    def kernel(a, b, o_ref):
        m, total = merge_all([a[...], b[...]])
        both = jnp.concatenate([m, total], axis=0)
        for i in range(16):
            o_ref[i] = both

    return pl.pallas_call(
        kernel, in_specs=[VMEM] * 2, out_shape=shape((16, 8, 512), F32), name="merge_cores"
    )(local, other)


def merge_last(idx, stats, local):
    def kernel(idx_ref, s_ref, l_ref, f_ref, tmp):
        m, total = merge_all([s_ref[i] for i in range(16)])
        tmp[0:4, :] = jnp.exp(l_ref[0:4, :] - m) / total
        for r in range(4):
            f_ref[:, r * 512 : (r + 1) * 512] = tmp[pl.ds(idx_ref[4 + r], 1), :]

    return pl.pallas_call(
        kernel,
        in_specs=[SMEM] + [VMEM] * 2,
        scratch_shapes=[pltpu.VMEM((8, 512), F32)],
        out_shape=shape((1, 2048), F32),
        name="merge_last",
    )(idx, stats, local)


def sums_one(p, factor, x, masses, blocks, dtype):
    first, step = blocks[0], blocks[-1] - blocks[0]

    def kernel(p_ref, f_ref, x_ref, old_ref, *refs):
        mass_ref = refs[-1]
        w = (p_ref[...] * f_ref[...]).astype(BF)
        sums = nn(w, x_ref[...])
        mass = as_row(lane_sums(w))
        for q, k in enumerate(blocks):

            @pl.when(pl.program_id(0) == q)
            def _(q=q, k=k):
                if q == 0:
                    mass_ref[...] = old_ref[...]
                refs[q][...] = sums.astype(dtype)
                mass_ref[k : k + 1, :] = mass

    return pl.pallas_call(
        kernel,
        grid=(len(blocks),),
        in_specs=[
            pl.BlockSpec((512, 2048), lambda j: (first + step * j, 0)),
            pl.BlockSpec((1, 2048), lambda j: (0, 0)),
            pl.BlockSpec((2048, D), lambda j: (0, 0)),
            pl.BlockSpec((4, 512), lambda j: (0, 0)),
        ],
        out_specs=[pl.BlockSpec((512, D), lambda j: (0, 0)) for k in blocks]
        + [pl.BlockSpec((4, 512), lambda j: (0, 0))],
        out_shape=[shape((512, D), dtype) for k in blocks] + [shape((4, 512), F32)],
        name="sums_one",
    )(p, factor, x, masses)


def finish_one(idx, own, got, cents, masses, far_masses):
    def kernel(idx_ref, own_ref, g1, g2, g3, cents_ref, m0, m1, m2, m3, pts_ref, mass_ref):
        total = m0[...]
        for k, ref in ((1, m1), (2, m2), (3, m3)):
            t = ref[...]
            total = total + jnp.concatenate([t[k:], t[:k]], axis=0)
        mass_ref[...] = total
        i = pl.program_id(0)
        column = as_column(mass_ref[0:1, pl.ds(pl.multiple_of(i * 256, 256), 256)]) + PRIOR
        num = own_ref[...] + g1[...].astype(F32) + g2[...].astype(F32) + g3[...].astype(F32)
        num = num + PRIOR * cents_ref[...].astype(F32)
        pts_ref[...] = (num / column).astype(BF)

    rows = pl.BlockSpec((256, D), lambda i, s: (i, 0))
    small = pl.BlockSpec((4, 512), lambda i, s: (0, 0))
    return pl.pallas_call(
        kernel,
        grid_spec=pltpu.PrefetchScalarGridSpec(
            num_scalar_prefetch=1,
            grid=(2,),
            in_specs=[rows] * 4 + [pl.BlockSpec((256, D), lambda i, s: (s[0] * 2 + i, 0))] + [small] * 4,
            out_specs=[rows, small],
        ),
        out_shape=[shape((512, D), BF), shape((4, 512), F32)],
        name="finish_one",
    )(idx, own, *got, cents, masses, *far_masses)


def turn_points(points):
    def kernel(p_ref, o_ref):
        for at in range(0, D, 128):
            o_ref[pl.ds(at, 128), :] = p_ref[:, pl.ds(at, 128)].astype(F32).T.astype(BF)

    return pl.pallas_call(kernel, in_specs=[VMEM], out_shape=shape((D, 512), BF), name="turn_points")(points)


def gather_one(place, keep, take, totals, far_totals):
    def kernel(place_ref, keep_ref, take_ref, t_ref, f_ref, o_ref, m_ref):
        y, near = place_ref[0], place_ref[1]
        for ref, half in ((keep_ref, near), (take_ref, 1 - near)):
            for k in range(4):
                start = half * 2048 + lax.rem(y + 4 - k, 4) * 512
                o_ref[:, pl.ds(pl.multiple_of(start, 512), 512)] = ref[k].astype(F32)
        for ref, half in ((t_ref, near), (f_ref, 1 - near)):
            for j in range(4):
                m_ref[pl.ds(half * 4 + lax.rem(y + j, 4), 1), :] = ref[j : j + 1, :]

    return pl.pallas_call(
        kernel,
        in_specs=[SMEM] + [VMEM] * 4,
        out_shape=[shape((96, 4096), F32), shape((8, 512), F32)],
        name="gather_one",
    )(place, keep, take, totals, far_totals)


def norms_two(two):
    def kernel(c_ref, o_ref):
        o_ref[...] = jnp.broadcast_to(square_norms(c_ref[...]), (1024, 128))

    return pl.pallas_call(
        kernel,
        grid=(2,),
        in_specs=[pl.BlockSpec((1024, D), lambda i: (i, 0))],
        out_specs=pl.BlockSpec((1024, 128), lambda i: (i, 0)),
        out_shape=shape((2048, 128), F32),
        name="norms_two",
    )(two)


def scores_two(slots, a, b, two, norms):
    def kernel(slots_ref, a_ref, b_ref, c_ref, n_ref, p_ref, stat_ref, scores):
        i = pl.program_id(0)
        twice = jnp.where(i < 2, a_ref[...], b_ref[...]) * 2
        top = None
        for d in range(8):
            here = pl.ds(pl.multiple_of(slots_ref[d] * 256, 256), 256)
            n = n_ref[here, :]
            s = nt(c_ref[here, :], twice) - jnp.concatenate([n, n], axis=1)
            scores[pl.ds(d * 256, 256), :] = s
            t = fold_rows(s, jnp.maximum)
            top = t if top is None else jnp.maximum(top, t)
        m = jnp.max(top, axis=0, keepdims=True)
        total = None
        for at in range(0, 2048, 256):
            e = jnp.exp(scores[pl.ds(at, 256), :] - m)
            p_ref[pl.ds(at, 256), :] = e
            t = fold_rows(e, jnp.add)
            total = t if total is None else total + t
        stat_ref[0:1, :] = m
        stat_ref[1:2, :] = jnp.sum(total, axis=0, keepdims=True)

    return pl.pallas_call(
        kernel,
        grid_spec=pltpu.PrefetchScalarGridSpec(
            num_scalar_prefetch=1,
            grid=(4,),
            in_specs=ROW_IN + [pl.BlockSpec((2048, D), lambda i, s: (0, 0)), WHOLE_NORMS],
            out_specs=[
                pl.BlockSpec((2048, 256), lambda i, s: (0, i)),
                pl.BlockSpec((2, 256), lambda i, s: (0, i)),
            ],
            scratch_shapes=[pltpu.VMEM((2048, 256), F32)],
        ),
        out_shape=[shape((2048, 1024), F32), shape((2, 1024), F32)],
        name="scores_two",
    )(slots, a, b, two, norms)


def sums_two(p, stat, other, a, b):
    def kernel(p_ref, s_ref, r_ref, a_ref, b_ref, o_ref, rows, factor):
        @pl.when(pl.program_id(0) == 0)
        def _():
            rows[0:512, :] = a_ref[...]
            rows[512:1024, :] = b_ref[...]
            theirs = jnp.concatenate([r_ref[:, 512:1024], r_ref[:, 0:512]], axis=1)
            mine = s_ref[...]
            m = jnp.maximum(mine[0:1], theirs[0:1])
            near = jnp.exp(mine[0:1] - m)
            total = mine[1:2] * near + theirs[1:2] * jnp.exp(theirs[0:1] - m)
            factor[0:1, :] = near / total

        w = (p_ref[...] * factor[0:1, :]).astype(BF)
        num = nn(w, rows[...])
        packed = mass_rows(as_row(lane_sums(w)))
        for q in range(32):
            for j in range(6):
                o_ref[q, j * 32 : j * 32 + 32, :] = num[q * 32 : q * 32 + 32, j * 128 : j * 128 + 128].astype(BF)
            lanes = packed[:, (q // 4) * 128 : (q // 4) * 128 + 128]
            turn = (128 - (q % 4) * 32) % 128
            o_ref[q, 192:TALL, :] = (pltpu.roll(lanes, turn, 1) if turn else lanes).astype(BF)

    whole = lambda r, c: pl.BlockSpec((r, c), lambda i: (0, 0))
    return pl.pallas_call(
        kernel,
        grid=(2,),
        in_specs=[pl.BlockSpec((1024, 1024), lambda i: (i, 0)), whole(2, 1024), whole(2, 1024), whole(512, D), whole(512, D)],
        out_specs=pl.BlockSpec((32, TALL, 128), lambda i: (i, 0, 0)),
        scratch_shapes=[pltpu.VMEM((1024, D), BF), pltpu.VMEM((8, 1024), F32)],
        out_shape=shape((64, TALL, 128), BF),
        name="sums_two",
    )(p, stat, other, a, b)


def finish_two(parts, cents):
    def kernel(x_ref, c_ref, o_ref, acc):
        i = pl.program_id(0)
        total = x_ref[0].astype(F32)
        for q in range(1, 16):
            total = total + x_ref[q].astype(F32)

        @pl.when(i == 0)
        def _():
            acc[...] = total

        @pl.when(i > 0)
        def _():
            acc[...] += total

        @pl.when(i == 3)
        def _():
            mass = acc[192:193, :] + acc[193:194, :] + acc[194:195, :]
            column = as_column(mass)[0:32] + PRIOR
            packed = mass_rows(mass).astype(BF)
            for j in range(6):
                num = acc[j * 32 : j * 32 + 32, :] + PRIOR * c_ref[:, j * 128 : j * 128 + 128].astype(F32)
                new = (num / column).astype(BF)
                for q in range(8):
                    o_ref[q, j * 32 : j * 32 + 32, :] = new
            for q in range(8):
                o_ref[q, 192:TALL, :] = packed

    return pl.pallas_call(
        kernel,
        grid=(4,),
        in_specs=[
            pl.BlockSpec((16, TALL, 128), lambda i: (i, 0, 0)),
            pl.BlockSpec((32, D), lambda i: (0, 0)),
        ],
        out_specs=pl.BlockSpec((8, TALL, 128), lambda i: (0, 0, 0)),
        scratch_shapes=[pltpu.VMEM((TALL, 128), F32)],
        out_shape=shape((8, TALL, 128), BF),
        name="finish_two",
    )(parts, cents)


def gather_two(core, mine, theirs):
    def kernel(core_ref, a_ref, b_ref, o_ref, m_ref):
        lane = lax.broadcasted_iota(jnp.int32, (16, 128), 1)
        for ref, half in ((a_ref, core_ref[0]), (b_ref, 1 - core_ref[0])):
            start = pl.multiple_of(half * 256, 256)
            for q in range(8):
                for j in range(6):
                    o_ref[pl.ds(start + q * 32, 32), j * 128 : j * 128 + 128] = ref[q, j * 32 : j * 32 + 32, :].astype(F32)
            for g in range(2):
                row = None
                for r in range(4):
                    t = ref[g * 4 + r, 192:TALL, :].astype(F32)
                    t = pltpu.roll(t, r * 32, 1) if r else t
                    row = t if row is None else jnp.where(lane >= r * 32, t, row)
                m_ref[:, pl.ds(start + g * 128, 128)] = row[0:1] + row[1:2] + row[2:3]

    return pl.pallas_call(
        kernel,
        in_specs=[SMEM] + [VMEM] * 2,
        out_shape=[shape((512, D), F32), shape((1, 512), F32)],
        name="gather_two",
    )(core, mine, theirs)


def shift_y(x, k):
    return lax.ppermute(x, "y", [(i, (i + k) % 4) for i in range(4)])


def shift_z(x, k):
    return lax.ppermute(x, "z", [(i, (i + k) % 4) for i in range(4)])


def flip(x, axis):
    return lax.ppermute(x, axis, [(0, 1), (1, 0)])


def flip_x(x):
    return lax.ppermute(x, ("xh", "xl"), [(0, 3), (1, 2), (2, 1), (3, 0)])


def after(x, *others):
    return lax.optimization_barrier((x,) + others)[0]


def body(embeddings, cents_one, cents_two):
    y = lax.axis_index("y").astype(jnp.int32)
    xh = lax.axis_index("xh").astype(jnp.int32)
    z = lax.axis_index("z").astype(jnp.int32)
    xl = lax.axis_index("xl").astype(jnp.int32)
    c = lax.axis_index("c").astype(jnp.int32)
    halves = jnp.stack([xh * 2 + c, xh * 2 + 1 - c, 2 - xh * 2 + c, 3 - xh * 2 - c])
    idx = jnp.concatenate([xh * 4 + (y + jnp.arange(4, dtype=jnp.int32)) % 4, halves])
    to = jnp.arange(8, dtype=jnp.int32)
    slots = (xh ^ (to % 2)) * 4 + (y - to // 2) % 4

    mine = lax.dynamic_slice_in_dim(embeddings, c * 512, 512, 0).astype(BF)
    far_mine = flip_x(mine)
    half_two = lax.dynamic_slice_in_dim(cents_two, c * 256, 256, 0)
    around = [shift_y(half_two, k) for k in (1, 2, 3)]

    other = lax.dynamic_slice_in_dim(embeddings, (1 - c) * 512, 512, 0).astype(BF)
    p, x, near, norms = scores_near(idx, mine, other, cents_one)
    far_mine = after(far_mine, near, around[0], around[2])
    far_other = flip(far_mine, "c")
    p, x, local = scores_far(idx, far_mine, far_other, cents_one, norms, near, p, x)

    spread = merge_cores(local, flip(local, "c"))
    stats = lax.all_to_all(spread, ("xh", "z", "xl"), 0, 0, tiled=True)
    factor = merge_last(idx, stats, local)

    masses = jnp.zeros((4, 512), F32)
    part, masses = sums_one(p, factor, x, masses, (2,), BF)
    got = {2: shift_y(part, 2)}
    part1, part3, masses = sums_one(p, factor, x, masses, (1, 3), BF)
    got[1], got[3] = shift_y(part1, 1), shift_y(part3, 3)
    own, masses = sums_one(p, factor, x, after(masses, got[2]), (0,), F32)

    same_two = jnp.concatenate([half_two] + [after(t, part) for t in around], axis=0)
    far_two = after(flip_x(same_two), masses)
    two = jnp.concatenate([same_two, far_two], axis=0)
    norms = norms_two(two)

    points, totals = finish_one(
        idx, after(own, norms), [got[k] for k in (1, 2, 3)], cents_one, masses, [shift_y(masses, k) for k in (1, 2, 3)]
    )
    their_points = flip(points, "c")
    p2, stat2 = scores_two(slots, points, their_points, two, norms)
    packed = sums_two(p2, stat2, flip(stat2, "c"), points, their_points)
    parts = lax.all_to_all(packed, ("y", "xh", "z", "xl"), 0, 0, tiled=True)

    late_points, late_totals = lax.optimization_barrier((points, totals, packed))[0:2]
    tall = turn_points(late_points)
    cut = lambda d: lax.dynamic_slice_in_dim(tall, ((y + d) % 4) * 192, 192, 0)
    cols = jnp.stack([cut(0)] + [shift_y(cut(k), k) for k in (1, 2, 3)]).reshape(4, 2, 96, 512)
    keep = lax.dynamic_index_in_dim(cols, xh, 1, keepdims=False)
    take = flip(lax.dynamic_index_in_dim(cols, 1 - xh, 1, keepdims=False), "xh")
    turned_one, mass_one = gather_one(jnp.stack([y, xh]), keep, take, late_totals, flip(late_totals, "xh"))

    rows = lax.dynamic_slice_in_dim(cents_two, c * 256 + z * 64 + xl * 32, 32, 0)
    spread = finish_two(parts, after(rows, turned_one))
    block = lax.all_to_all(spread, ("z", "xl"), 0, 0, tiled=True)
    updated_two, mass_two = gather_two(c[None], block, flip(block, "c"))
    return turned_one.T, mass_one.reshape(4096), updated_two, mass_two.reshape(512)


def solution(mesh):
    fine = Mesh(mesh.devices.reshape(4, 2, 4, 2, 2), ("y", "xh", "z", "xl", "c"))
    dp, cent = ("y", "xh"), ("z", "xl", "c")
    return jax.shard_map(
        body,
        mesh=fine,
        in_specs=(P(dp, None), P(cent, None), P(dp, None)),
        out_specs=(P(cent, dp), P(cent), P(dp, None), P(dp)),
        check_vma=False,
    )
```

```python
import jax
import jax.numpy as jnp
from jax import lax
from jax.experimental import pallas as pl
from jax.experimental.pallas import tpu as pltpu
from jax.sharding import Mesh, PartitionSpec as P

PRIOR = 0.5
BF = jnp.bfloat16
F32 = jnp.float32
D = 768
TALL = 208
SMEM = pl.BlockSpec(memory_space=pltpu.SMEM)
VMEM = pl.BlockSpec(memory_space=pltpu.VMEM)


def nt(left, right):
    return lax.dot_general(left, right, (((1,), (1,)), ((), ())), preferred_element_type=F32)


def nn(left, right):
    return lax.dot_general(left, right, (((1,), (0,)), ((), ())), preferred_element_type=F32)


def shape(dims, dtype):
    return jax.ShapeDtypeStruct(dims, dtype)


def square_norms(block):
    wide = block.astype(F32)
    return jnp.sum(wide * wide, axis=1, keepdims=True)


def fold_rows(block, op):
    parts = [block[i : i + 8] for i in range(0, block.shape[0], 8)]
    while len(parts) > 1:
        parts = [op(parts[i], parts[i + 1]) for i in range(0, len(parts) - 1, 2)] + (
            [parts[-1]] if len(parts) % 2 else []
        )
    return parts[0]


def lane_sums(w):
    wide = w.astype(F32)
    part = wide[:, 0:128]
    for j in range(128, wide.shape[1], 128):
        part = part + wide[:, j : j + 128]
    return jnp.sum(part, axis=1, keepdims=True)


def as_row(column):
    return jnp.broadcast_to(column, (column.shape[0], 128)).T[0:1, :]


def as_column(row):
    return jnp.broadcast_to(row, (128, row.shape[1])).T[:, 0:1]


def mass_rows(row):
    t = jnp.broadcast_to(row, (16, row.shape[1]))
    hi = t.astype(BF).astype(F32)
    mid = (t - hi).astype(BF).astype(F32)
    low = t - hi - mid
    at = lax.broadcasted_iota(jnp.int32, t.shape, 0)
    return jnp.where(at == 0, hi, jnp.where(at == 1, mid, jnp.where(at == 2, low, 0.0)))


def scores_step(cents, twice, norms, p_ref, scores):
    top = None
    for k in range(4):
        for h in range(2):
            at = k * 512 + h * 256
            n = norms[pl.ds(at, 256), :]
            s = nt(cents[k][pl.ds(h * 256, 256), :], twice) - jnp.concatenate([n, n], axis=1)
            scores[pl.ds(at, 256), :] = s
            t = fold_rows(s, jnp.maximum)
            top = t if top is None else jnp.maximum(top, t)
    m = jnp.max(top, axis=0, keepdims=True)
    total = None
    for at in range(0, 2048, 256):
        e = jnp.exp(scores[pl.ds(at, 256), :] - m)
        p_ref[pl.ds(at, 256), :] = e
        t = fold_rows(e, jnp.add)
        total = t if total is None else total + t
    return m, jnp.sum(total, axis=0, keepdims=True)


def put_stats(stat_ref, row, i, m, l):
    cols = pl.ds(pl.multiple_of(lax.rem(i, 2) * 256, 256), 256)
    stat_ref[pl.ds(row, 1), cols] = m
    stat_ref[pl.ds(4 + row, 1), cols] = l


def scores_near_kernel(idx, e_ref, c0, c1, c2, c3, p_ref, x_ref, stat_ref, norms_ref, scores):
    i = pl.program_id(0)
    cents = (c0, c1, c2, c3)

    @pl.when(i == 0)
    def _():
        stat_ref[...] = jnp.zeros_like(stat_ref)
        for k in range(4):
            for h in range(2):
                n = square_norms(cents[k][pl.ds(h * 256, 256), :])
                norms_ref[pl.ds(k * 512 + h * 256, 256), :] = jnp.broadcast_to(n, (256, 128))

    x = e_ref[...].astype(BF)
    x_ref[...] = x
    m, l = scores_step(cents, x * 2, norms_ref, p_ref, scores)
    put_stats(stat_ref, idx[4 + i // 2], i, m, l)


def scores_far_kernel(idx, a_ref, b_ref, c0, c1, c2, c3, norms_ref, near_ref, p_old, x_old, p_ref, x_ref, stat_ref, scores):
    i = pl.program_id(0)

    @pl.when(i == 0)
    def _():
        stat_ref[...] = near_ref[...]

    x = jnp.where(i < 2, a_ref[...], b_ref[...])
    x_ref[...] = x
    m, l = scores_step((c0, c1, c2, c3), x * 2, norms_ref, p_ref, scores)
    put_stats(stat_ref, idx[6 + i // 2], i, m, l)


ANY = pl.BlockSpec(memory_space=pl.ANY)
ROW_IN = [
    pl.BlockSpec((256, D), lambda i, s: (jnp.minimum(i, 1), 0)),
    pl.BlockSpec((256, D), lambda i, s: (jnp.maximum(i - 2, 0), 0)),
]
CENTS_IN = [pl.BlockSpec((512, D), lambda i, s, k=k: (s[k], 0)) for k in range(4)]
WHOLE_STAT = pl.BlockSpec((8, 512), lambda i, s: (0, 0))
WHOLE_NORMS = pl.BlockSpec((2048, 128), lambda i, s: (0, 0))


def scores_near(idx, embeddings, cents):
    return pl.pallas_call(
        scores_near_kernel,
        grid_spec=pltpu.PrefetchScalarGridSpec(
            num_scalar_prefetch=1,
            grid=(4,),
            in_specs=[pl.BlockSpec((256, D), lambda i, s: (s[8 + i // 2] * 2 + i % 2, 0))] + CENTS_IN,
            out_specs=[
                pl.BlockSpec((2048, 256), lambda i, s: (0, i)),
                pl.BlockSpec((256, D), lambda i, s: (i, 0)),
                WHOLE_STAT,
                WHOLE_NORMS,
            ],
            scratch_shapes=[pltpu.VMEM((2048, 256), F32)],
        ),
        out_shape=[
            shape((2048, 2048), F32),
            shape((2048, D), BF),
            shape((8, 512), F32),
            shape((2048, 128), F32),
        ],
        cost_estimate=pl.CostEstimate(
            flops=2 * 2048 * 1024 * D, transcendentals=2048 * 1024, bytes_accessed=24 << 20
        ),
        name="scores_near",
    )(idx, embeddings, cents, cents, cents, cents)


def scores_far(idx, a, b, cents, norms, near, p, x):
    return pl.pallas_call(
        scores_far_kernel,
        grid_spec=pltpu.PrefetchScalarGridSpec(
            num_scalar_prefetch=1,
            grid=(4,),
            in_specs=ROW_IN + CENTS_IN + [WHOLE_NORMS, WHOLE_STAT, ANY, ANY],
            out_specs=[
                pl.BlockSpec((2048, 256), lambda i, s: (0, 4 + i)),
                pl.BlockSpec((256, D), lambda i, s: (4 + i, 0)),
                WHOLE_STAT,
            ],
            scratch_shapes=[pltpu.VMEM((2048, 256), F32)],
        ),
        out_shape=[shape((2048, 2048), F32), shape((2048, D), BF), shape((8, 512), F32)],
        input_output_aliases={9: 0, 10: 1},
        name="scores_far",
    )(idx, a, b, cents, cents, cents, cents, norms, near, p, x)


def merge_all(stats):
    m = stats[0][0:4]
    for t in stats[1:]:
        m = jnp.maximum(m, t[0:4])
    total = None
    for t in stats:
        part = t[4:8] * jnp.exp(t[0:4] - m)
        total = part if total is None else total + part
    return m, total


def merge_cores(local, other):
    def kernel(a, b, o_ref):
        m, total = merge_all([a[...], b[...]])
        both = jnp.concatenate([m, total], axis=0)
        for i in range(16):
            o_ref[i] = both

    return pl.pallas_call(
        kernel, in_specs=[VMEM] * 2, out_shape=shape((16, 8, 512), F32), name="merge_cores"
    )(local, other)


def merge_last(idx, stats, local):
    def kernel(idx_ref, s_ref, l_ref, f_ref, tmp):
        m, total = merge_all([s_ref[i] for i in range(16)])
        tmp[0:4, :] = jnp.exp(l_ref[0:4, :] - m) / total
        for r in range(4):
            f_ref[:, r * 512 : (r + 1) * 512] = tmp[pl.ds(idx_ref[4 + r], 1), :]

    return pl.pallas_call(
        kernel,
        in_specs=[SMEM] + [VMEM] * 2,
        scratch_shapes=[pltpu.VMEM((8, 512), F32)],
        out_shape=shape((1, 2048), F32),
        name="merge_last",
    )(idx, stats, local)


def sums_one(p, factor, x, masses, blocks, dtype):
    first, step = blocks[0], blocks[-1] - blocks[0]

    def kernel(p_ref, f_ref, x_ref, old_ref, *refs):
        mass_ref = refs[-1]
        w = (p_ref[...] * f_ref[...]).astype(BF)
        sums = nn(w, x_ref[...])
        mass = as_row(lane_sums(w))
        for q, k in enumerate(blocks):

            @pl.when(pl.program_id(0) == q)
            def _(q=q, k=k):
                if q == 0:
                    mass_ref[...] = old_ref[...]
                refs[q][...] = sums.astype(dtype)
                mass_ref[k : k + 1, :] = mass

    return pl.pallas_call(
        kernel,
        grid=(len(blocks),),
        in_specs=[
            pl.BlockSpec((512, 2048), lambda j: (first + step * j, 0)),
            pl.BlockSpec((1, 2048), lambda j: (0, 0)),
            pl.BlockSpec((2048, D), lambda j: (0, 0)),
            pl.BlockSpec((4, 512), lambda j: (0, 0)),
        ],
        out_specs=[pl.BlockSpec((512, D), lambda j: (0, 0)) for k in blocks]
        + [pl.BlockSpec((4, 512), lambda j: (0, 0))],
        out_shape=[shape((512, D), dtype) for k in blocks] + [shape((4, 512), F32)],
        name="sums_one",
    )(p, factor, x, masses)


def finish_one(idx, own, got, cents, masses, far_masses):
    def kernel(idx_ref, own_ref, g1, g2, g3, cents_ref, m0, m1, m2, m3, pts_ref, mass_ref):
        total = m0[...]
        for k, ref in ((1, m1), (2, m2), (3, m3)):
            t = ref[...]
            total = total + jnp.concatenate([t[k:], t[:k]], axis=0)
        mass_ref[...] = total
        i = pl.program_id(0)
        column = as_column(mass_ref[0:1, pl.ds(pl.multiple_of(i * 256, 256), 256)]) + PRIOR
        num = own_ref[...] + g1[...].astype(F32) + g2[...].astype(F32) + g3[...].astype(F32)
        num = num + PRIOR * cents_ref[...].astype(F32)
        pts_ref[...] = (num / column).astype(BF)

    rows = pl.BlockSpec((256, D), lambda i, s: (i, 0))
    small = pl.BlockSpec((4, 512), lambda i, s: (0, 0))
    return pl.pallas_call(
        kernel,
        grid_spec=pltpu.PrefetchScalarGridSpec(
            num_scalar_prefetch=1,
            grid=(2,),
            in_specs=[rows] * 4 + [pl.BlockSpec((256, D), lambda i, s: (s[0] * 2 + i, 0))] + [small] * 4,
            out_specs=[rows, small],
        ),
        out_shape=[shape((512, D), BF), shape((4, 512), F32)],
        name="finish_one",
    )(idx, own, *got, cents, masses, *far_masses)


def turn_points(points, totals):
    def kernel(p_ref, t_ref, o_ref, tall):
        for at in range(0, D, 128):
            tall[pl.ds(at, 128), :] = p_ref[:, pl.ds(at, 128)].astype(F32).T.astype(BF)
        packed = mass_rows(t_ref[0:1, :]).astype(BF)
        for d in range(8):
            o_ref[d, 0:96, :] = tall[pl.ds(d * 96, 96), :]
            o_ref[d, 96:112, :] = packed

    return pl.pallas_call(
        kernel,
        in_specs=[VMEM] * 2,
        scratch_shapes=[pltpu.VMEM((D, 512), BF)],
        out_shape=shape((8, 112, 512), BF),
        cost_estimate=pl.CostEstimate(flops=0, transcendentals=0, bytes_accessed=24 << 20),
        name="turn_points",
    )(points, totals)


def gather_one(parts):
    def kernel(x_ref, o_ref, m_ref):
        for s in range(8):
            block = (s % 2) * 4 + s // 2
            o_ref[:, block * 512 : block * 512 + 512] = x_ref[s, 0:96, :].astype(F32)
            t = x_ref[s, 96:112, :].astype(F32)
            m_ref[block : block + 1, :] = t[0:1] + t[1:2] + t[2:3]

    return pl.pallas_call(
        kernel,
        in_specs=[VMEM],
        out_shape=[shape((96, 4096), F32), shape((8, 512), F32)],
        name="gather_one",
    )(parts)


def join_near(blocks):
    def kernel(a, b, c, d, o_ref, n_ref):
        for at, ref in zip(range(0, 1024, 256), (a, b, c, d)):
            block = ref[...]
            o_ref[pl.ds(at, 256), :] = block
            n_ref[pl.ds(at, 256), :] = jnp.broadcast_to(square_norms(block), (256, 128))

    return pl.pallas_call(
        kernel,
        in_specs=[VMEM] * 4,
        out_shape=[shape((1024, D), BF), shape((1024, 128), F32)],
        name="join_near",
    )(*blocks)


def norms_far(block):
    def kernel(c_ref, o_ref):
        o_ref[...] = jnp.broadcast_to(square_norms(c_ref[...]), (1024, 128))

    return pl.pallas_call(
        kernel, in_specs=[VMEM], out_shape=shape((1024, 128), F32), name="norms_far"
    )(block)


def scores_two(places, a, b, near, far, near_norms, far_norms):
    def kernel(places_ref, a_ref, b_ref, near_ref, far_ref, nn_ref, fn_ref, p_ref, stat_ref, scores):
        i = pl.program_id(0)
        twice = jnp.where(i < 2, a_ref[...], b_ref[...]) * 2
        top = None
        for slot in range(8):
            c_ref, n_ref = ((near_ref, nn_ref), (far_ref, fn_ref))[slot // 4]
            here = pl.ds((slot % 4) * 256, 256)
            n = n_ref[here, :]
            s = nt(c_ref[here, :], twice) - jnp.concatenate([n, n], axis=1)
            scores[pl.ds(slot * 256, 256), :] = s
            t = fold_rows(s, jnp.maximum)
            top = t if top is None else jnp.maximum(top, t)
        m = jnp.max(top, axis=0, keepdims=True)
        total = None
        for slot in range(8):
            e = jnp.exp(scores[pl.ds(slot * 256, 256), :] - m)
            p_ref[pl.ds(pl.multiple_of(places_ref[slot] * 256, 256), 256), :] = e
            t = fold_rows(e, jnp.add)
            total = t if total is None else total + t
        stat_ref[0:1, :] = m
        stat_ref[1:2, :] = jnp.sum(total, axis=0, keepdims=True)

    return pl.pallas_call(
        kernel,
        grid_spec=pltpu.PrefetchScalarGridSpec(
            num_scalar_prefetch=1,
            grid=(4,),
            in_specs=ROW_IN
            + [pl.BlockSpec((1024, D), lambda i, s: (0, 0))] * 2
            + [pl.BlockSpec((1024, 128), lambda i, s: (0, 0))] * 2,
            out_specs=[
                pl.BlockSpec((2048, 256), lambda i, s: (0, i)),
                pl.BlockSpec((2, 256), lambda i, s: (0, i)),
            ],
            scratch_shapes=[pltpu.VMEM((2048, 256), F32)],
        ),
        out_shape=[shape((2048, 1024), F32), shape((2, 1024), F32)],
        name="scores_two",
    )(places, a, b, near, far, near_norms, far_norms)


def sums_two(p, stat, other, a, b):
    def kernel(p_ref, s_ref, r_ref, a_ref, b_ref, o_ref, rows, factor):
        @pl.when(pl.program_id(0) == 0)
        def _():
            rows[0:512, :] = a_ref[...]
            rows[512:1024, :] = b_ref[...]
            theirs = jnp.concatenate([r_ref[:, 512:1024], r_ref[:, 0:512]], axis=1)
            mine = s_ref[...]
            m = jnp.maximum(mine[0:1], theirs[0:1])
            near = jnp.exp(mine[0:1] - m)
            total = mine[1:2] * near + theirs[1:2] * jnp.exp(theirs[0:1] - m)
            factor[0:1, :] = near / total

        w = (p_ref[...] * factor[0:1, :]).astype(BF)
        num = nn(w, rows[...])
        packed = mass_rows(as_row(lane_sums(w)))
        for q in range(32):
            for j in range(6):
                o_ref[q, j * 32 : j * 32 + 32, :] = num[q * 32 : q * 32 + 32, j * 128 : j * 128 + 128].astype(BF)
            lanes = packed[:, (q // 4) * 128 : (q // 4) * 128 + 128]
            turn = (128 - (q % 4) * 32) % 128
            o_ref[q, 192:TALL, :] = (pltpu.roll(lanes, turn, 1) if turn else lanes).astype(BF)

    whole = lambda r, c: pl.BlockSpec((r, c), lambda i: (0, 0))
    return pl.pallas_call(
        kernel,
        grid=(2,),
        in_specs=[pl.BlockSpec((1024, 1024), lambda i: (i, 0)), whole(2, 1024), whole(2, 1024), whole(512, D), whole(512, D)],
        out_specs=pl.BlockSpec((32, TALL, 128), lambda i: (i, 0, 0)),
        scratch_shapes=[pltpu.VMEM((1024, D), BF), pltpu.VMEM((8, 1024), F32)],
        out_shape=shape((64, TALL, 128), BF),
        name="sums_two",
    )(p, stat, other, a, b)


def finish_two(total, cents):
    def kernel(x_ref, c_ref, o_ref):
        mass = x_ref[192:193, :] + x_ref[193:194, :] + x_ref[194:195, :]
        column = as_column(mass)[0:32] + PRIOR
        packed = mass_rows(mass).astype(BF)
        for j in range(6):
            num = x_ref[j * 32 : j * 32 + 32, :] + PRIOR * c_ref[:, j * 128 : j * 128 + 128].astype(F32)
            new = (num / column).astype(BF)
            for q in range(8):
                o_ref[q, j * 32 : j * 32 + 32, :] = new
        for q in range(8):
            o_ref[q, 192:TALL, :] = packed

    return pl.pallas_call(
        kernel, in_specs=[VMEM] * 2, out_shape=shape((8, TALL, 128), BF), name="finish_two"
    )(total, cents)


def gather_two(core, mine, theirs):
    def kernel(core_ref, a_ref, b_ref, o_ref, m_ref):
        lane = lax.broadcasted_iota(jnp.int32, (16, 128), 1)
        for ref, half in ((a_ref, core_ref[0]), (b_ref, 1 - core_ref[0])):
            start = pl.multiple_of(half * 256, 256)
            for q in range(8):
                for j in range(6):
                    o_ref[pl.ds(start + q * 32, 32), j * 128 : j * 128 + 128] = ref[q, j * 32 : j * 32 + 32, :].astype(F32)
            for g in range(2):
                row = None
                for r in range(4):
                    t = ref[g * 4 + r, 192:TALL, :].astype(F32)
                    t = pltpu.roll(t, r * 32, 1) if r else t
                    row = t if row is None else jnp.where(lane >= r * 32, t, row)
                m_ref[:, pl.ds(start + g * 128, 128)] = row[0:1] + row[1:2] + row[2:3]

    return pl.pallas_call(
        kernel,
        in_specs=[SMEM] + [VMEM] * 2,
        out_shape=[shape((512, D), F32), shape((1, 512), F32)],
        name="gather_two",
    )(core, mine, theirs)


def shift_y(x, k):
    return lax.ppermute(x, "y", [(i, (i + k) % 4) for i in range(4)])


def shift_z(x, k):
    return lax.ppermute(x, "z", [(i, (i + k) % 4) for i in range(4)])


def flip(x, axis):
    return lax.ppermute(x, axis, [(0, 1), (1, 0)])


def flip_x(x):
    return lax.ppermute(x, ("xh", "xl"), [(0, 3), (1, 2), (2, 1), (3, 0)])


def after(x, *others):
    return lax.optimization_barrier((x,) + others)[0]


def body(embeddings, cents_one, cents_two):
    y = lax.axis_index("y").astype(jnp.int32)
    xh = lax.axis_index("xh").astype(jnp.int32)
    z = lax.axis_index("z").astype(jnp.int32)
    xl = lax.axis_index("xl").astype(jnp.int32)
    c = lax.axis_index("c").astype(jnp.int32)
    halves = jnp.stack([xh * 2 + c, xh * 2 + 1 - c, 2 - xh * 2 + c, 3 - xh * 2 - c])
    idx = jnp.concatenate([xh * 4 + (y + jnp.arange(4, dtype=jnp.int32)) % 4, halves, jnp.stack([c, 1 - c])])
    slot = jnp.arange(8, dtype=jnp.int32)
    places = (y - slot) % 4 * 2 + (xh ^ (slot // 4))

    mine = lax.dynamic_slice_in_dim(embeddings, c * 512, 512, 0).astype(BF)
    far_mine = flip_x(mine)
    half_two = lax.dynamic_slice_in_dim(cents_two, c * 256, 256, 0)
    around = [shift_y(half_two, k) for k in (1, 2, 3)]

    p, x, near, norms = scores_near(idx, embeddings, cents_one)
    far_mine = after(far_mine, near, around[0], around[2])
    far_other = flip(far_mine, "c")
    p, x, local = scores_far(idx, far_mine, far_other, cents_one, norms, near, p, x)

    spread = merge_cores(local, flip(local, "c"))
    stats = lax.all_to_all(spread, ("xh", "z", "xl"), 0, 0, tiled=True)
    near_two, near_norms = join_near([after(half_two, spread)] + around)
    factor = merge_last(idx, stats, after(local, near_norms))

    masses = jnp.zeros((4, 512), F32)
    part, masses = sums_one(p, factor, x, masses, (2,), BF)
    got = {2: shift_y(part, 2)}
    part1, part3, masses = sums_one(p, factor, x, masses, (1, 3), BF)
    got[1], got[3] = shift_y(part1, 1), shift_y(part3, 3)
    own, masses = sums_one(p, factor, x, after(masses, got[2]), (0,), F32)

    far_two = after(flip_x(after(near_two, part)), masses)
    far_norms = norms_far(far_two)

    points, totals = finish_one(
        idx, after(own, far_norms), [got[k] for k in (1, 2, 3)], cents_one, masses, [shift_y(masses, k) for k in (1, 2, 3)]
    )
    their_points = flip(points, "c")
    tall = turn_points(points, totals)
    columns = lax.all_to_all(tall, ("y", "xh"), 0, 0, tiled=True)
    p2, stat2 = scores_two(places, after(points, tall), their_points, near_two, far_two, near_norms, far_norms)
    packed = sums_two(p2, stat2, flip(stat2, "c"), points, their_points)
    parts = lax.all_to_all(after(packed, columns), ("y", "xh", "z", "xl"), 0, 0, tiled=True)
    turned_one, mass_one = gather_one(columns)
    total = jnp.sum(parts.astype(F32), axis=0)
    rows = lax.dynamic_slice_in_dim(cents_two, c * 256 + z * 64 + xl * 32, 32, 0)
    spread = finish_two(total, after(rows, turned_one))
    block = lax.all_to_all(spread, ("z", "xl"), 0, 0, tiled=True)
    updated_two, mass_two = gather_two(c[None], block, flip(block, "c"))
    return turned_one.T, mass_one.reshape(4096), updated_two, mass_two.reshape(512)


def solution(mesh):
    fine = Mesh(mesh.devices.reshape(4, 2, 4, 2, 2), ("y", "xh", "z", "xl", "c"))
    dp, cent = ("y", "xh"), ("z", "xl", "c")
    return jax.shard_map(
        body,
        mesh=fine,
        in_specs=(P(dp, None), P(cent, None), P(dp, None)),
        out_specs=(P(cent, dp), P(cent), P(dp, None), P(dp)),
        check_vma=False,
    )
```

```python
import jax
import jax.numpy as jnp
from jax import lax
from jax.experimental import pallas as pl
from jax.experimental.pallas import tpu as pltpu
from jax.sharding import Mesh, PartitionSpec as P

PRIOR = 0.5
BF = jnp.bfloat16
F32 = jnp.float32
D = 768
TALL = 208
SMEM = pl.BlockSpec(memory_space=pltpu.SMEM)
VMEM = pl.BlockSpec(memory_space=pltpu.VMEM)


def nt(left, right):
    return lax.dot_general(left, right, (((1,), (1,)), ((), ())), preferred_element_type=F32)


def nn(left, right):
    return lax.dot_general(left, right, (((1,), (0,)), ((), ())), preferred_element_type=F32)


def shape(dims, dtype):
    return jax.ShapeDtypeStruct(dims, dtype)


def square_norms(block):
    wide = block.astype(F32)
    return jnp.sum(wide * wide, axis=1, keepdims=True)


def fold_rows(block, op):
    parts = [block[i : i + 8] for i in range(0, block.shape[0], 8)]
    while len(parts) > 1:
        parts = [op(parts[i], parts[i + 1]) for i in range(0, len(parts) - 1, 2)] + (
            [parts[-1]] if len(parts) % 2 else []
        )
    return parts[0]


def lane_sums(w):
    wide = w.astype(F32)
    part = wide[:, 0:128]
    for j in range(128, wide.shape[1], 128):
        part = part + wide[:, j : j + 128]
    return jnp.sum(part, axis=1, keepdims=True)


def as_row(column):
    return jnp.broadcast_to(column, (column.shape[0], 128)).T[0:1, :]


def as_column(row):
    return jnp.broadcast_to(row, (128, row.shape[1])).T[:, 0:1]


def mass_rows(row):
    t = jnp.broadcast_to(row, (16, row.shape[1]))
    hi = t.astype(BF).astype(F32)
    mid = (t - hi).astype(BF).astype(F32)
    low = t - hi - mid
    at = lax.broadcasted_iota(jnp.int32, t.shape, 0)
    return jnp.where(at == 0, hi, jnp.where(at == 1, mid, jnp.where(at == 2, low, 0.0)))


def scores_step(cents, twice, norms, p_ref, scores):
    top = None
    for k in range(4):
        for h in range(2):
            at = k * 512 + h * 256
            n = norms[pl.ds(at, 256), :]
            s = nt(cents[k][pl.ds(h * 256, 256), :], twice) - jnp.concatenate([n, n], axis=1)
            scores[pl.ds(at, 256), :] = s
            t = fold_rows(s, jnp.maximum)
            top = t if top is None else jnp.maximum(top, t)
    m = jnp.max(top, axis=0, keepdims=True)
    total = None
    for at in range(0, 2048, 256):
        e = jnp.exp(scores[pl.ds(at, 256), :] - m)
        p_ref[pl.ds(at, 256), :] = e
        t = fold_rows(e, jnp.add)
        total = t if total is None else total + t
    return m, jnp.sum(total, axis=0, keepdims=True)


def put_stats(stat_ref, row, i, m, l):
    cols = pl.ds(pl.multiple_of(lax.rem(i, 2) * 256, 256), 256)
    stat_ref[pl.ds(row, 1), cols] = m
    stat_ref[pl.ds(4 + row, 1), cols] = l


def scores_near_kernel(idx, e_ref, c0, c1, c2, c3, p_ref, x_ref, stat_ref, norms_ref, scores):
    i = pl.program_id(0)
    cents = (c0, c1, c2, c3)

    @pl.when(i == 0)
    def _():
        stat_ref[...] = jnp.zeros_like(stat_ref)
        for k in range(4):
            for h in range(2):
                n = square_norms(cents[k][pl.ds(h * 256, 256), :])
                norms_ref[pl.ds(k * 512 + h * 256, 256), :] = jnp.broadcast_to(n, (256, 128))

    x = e_ref[...].astype(BF)
    x_ref[...] = x
    m, l = scores_step(cents, x * 2, norms_ref, p_ref, scores)
    put_stats(stat_ref, idx[4 + i // 2], i, m, l)


def scores_far_kernel(idx, a_ref, b_ref, c0, c1, c2, c3, norms_ref, near_ref, p_old, x_old, p_ref, x_ref, stat_ref, scores):
    i = pl.program_id(0)

    @pl.when(i == 0)
    def _():
        stat_ref[...] = near_ref[...]

    x = jnp.where(i < 2, a_ref[...], b_ref[...])
    x_ref[...] = x
    m, l = scores_step((c0, c1, c2, c3), x * 2, norms_ref, p_ref, scores)
    put_stats(stat_ref, idx[6 + i // 2], i, m, l)


ANY = pl.BlockSpec(memory_space=pl.ANY)
ROW_IN = [
    pl.BlockSpec((256, D), lambda i, s: (jnp.minimum(i, 1), 0)),
    pl.BlockSpec((256, D), lambda i, s: (jnp.maximum(i - 2, 0), 0)),
]
CENTS_IN = [pl.BlockSpec((512, D), lambda i, s, k=k: (s[k], 0)) for k in range(4)]
WHOLE_STAT = pl.BlockSpec((8, 512), lambda i, s: (0, 0))
WHOLE_NORMS = pl.BlockSpec((2048, 128), lambda i, s: (0, 0))


def scores_near(idx, embeddings, cents):
    return pl.pallas_call(
        scores_near_kernel,
        grid_spec=pltpu.PrefetchScalarGridSpec(
            num_scalar_prefetch=1,
            grid=(4,),
            in_specs=[pl.BlockSpec((256, D), lambda i, s: (s[8 + i // 2] * 2 + i % 2, 0))] + CENTS_IN,
            out_specs=[
                pl.BlockSpec((2048, 256), lambda i, s: (0, i)),
                pl.BlockSpec((256, D), lambda i, s: (i, 0)),
                WHOLE_STAT,
                WHOLE_NORMS,
            ],
            scratch_shapes=[pltpu.VMEM((2048, 256), F32)],
        ),
        out_shape=[
            shape((2048, 2048), F32),
            shape((2048, D), BF),
            shape((8, 512), F32),
            shape((2048, 128), F32),
        ],
        cost_estimate=pl.CostEstimate(
            flops=2 * 2048 * 1024 * D, transcendentals=2048 * 1024, bytes_accessed=24 << 20
        ),
        name="scores_near",
    )(idx, embeddings, cents, cents, cents, cents)


def scores_far(idx, a, b, cents, norms, near, p, x):
    return pl.pallas_call(
        scores_far_kernel,
        grid_spec=pltpu.PrefetchScalarGridSpec(
            num_scalar_prefetch=1,
            grid=(4,),
            in_specs=ROW_IN + CENTS_IN + [WHOLE_NORMS, WHOLE_STAT, ANY, ANY],
            out_specs=[
                pl.BlockSpec((2048, 256), lambda i, s: (0, 4 + i)),
                pl.BlockSpec((256, D), lambda i, s: (4 + i, 0)),
                WHOLE_STAT,
            ],
            scratch_shapes=[pltpu.VMEM((2048, 256), F32)],
        ),
        out_shape=[shape((2048, 2048), F32), shape((2048, D), BF), shape((8, 512), F32)],
        input_output_aliases={9: 0, 10: 1},
        name="scores_far",
    )(idx, a, b, cents, cents, cents, cents, norms, near, p, x)


def merge_all(stats):
    m = stats[0][0:4]
    for t in stats[1:]:
        m = jnp.maximum(m, t[0:4])
    total = None
    for t in stats:
        part = t[4:8] * jnp.exp(t[0:4] - m)
        total = part if total is None else total + part
    return m, total


def merge_cores(local, other):
    def kernel(a, b, o_ref):
        m, total = merge_all([a[...], b[...]])
        both = jnp.concatenate([m, total], axis=0)
        for i in range(16):
            o_ref[i] = both

    return pl.pallas_call(
        kernel, in_specs=[VMEM] * 2, out_shape=shape((16, 8, 512), F32), name="merge_cores"
    )(local, other)


def merge_last(idx, stats, local):
    def kernel(idx_ref, s_ref, l_ref, f_ref, tmp):
        m, total = merge_all([s_ref[i] for i in range(16)])
        tmp[0:4, :] = jnp.exp(l_ref[0:4, :] - m) / total
        for r in range(4):
            f_ref[:, r * 512 : (r + 1) * 512] = tmp[pl.ds(idx_ref[4 + r], 1), :]

    return pl.pallas_call(
        kernel,
        in_specs=[SMEM] + [VMEM] * 2,
        scratch_shapes=[pltpu.VMEM((8, 512), F32)],
        out_shape=shape((1, 2048), F32),
        name="merge_last",
    )(idx, stats, local)


def sums_far(p, factor, x, half):
    def kernel(p_ref, f_ref, x_ref, *refs):
        w = (p_ref[...] * f_ref[...]).astype(BF)
        sums = nn(w, x_ref[...]).astype(BF)
        packed = mass_rows(as_row(lane_sums(w))).astype(BF)
        for q in range(3):

            @pl.when(pl.program_id(0) == q)
            def _(q=q):
                refs[q][0:256, :] = sums
                refs[q][256:272, 0:256] = packed
                refs[q][256:272, 256:D] = jnp.zeros((16, D - 256), BF)

    return pl.pallas_call(
        kernel,
        grid=(3,),
        in_specs=[
            pl.BlockSpec((256, 2048), lambda j: ((2 - j + 3 * (j // 2)) * 2 + half, 0)),
            pl.BlockSpec((1, 2048), lambda j: (0, 0)),
            pl.BlockSpec((2048, D), lambda j: (0, 0)),
        ],
        out_specs=[pl.BlockSpec((272, D), lambda j: (0, 0))] * 3,
        out_shape=[shape((272, D), BF)] * 3,
        name="sums_far",
    )(p, factor, x)


def sums_own(p, factor, x):
    def kernel(p_ref, f_ref, x_ref, o_ref, m_ref):
        w = (p_ref[...] * f_ref[...]).astype(BF)
        o_ref[...] = nn(w, x_ref[...])
        m_ref[...] = as_row(lane_sums(w))

    return pl.pallas_call(
        kernel,
        grid=(1,),
        in_specs=[
            pl.BlockSpec((512, 2048), lambda j: (0, 0)),
            pl.BlockSpec((1, 2048), lambda j: (0, 0)),
            pl.BlockSpec((2048, D), lambda j: (0, 0)),
        ],
        out_specs=[pl.BlockSpec((512, D), lambda j: (0, 0)), pl.BlockSpec((1, 512), lambda j: (0, 0))],
        out_shape=[shape((512, D), F32), shape((1, 512), F32)],
        name="sums_own",
    )(p, factor, x)


def finish_one(idx, own, own_mass, got, cents, half):
    def kernel(idx_ref, own_ref, m_ref, g1, g2, g3, cents_ref, pts_ref, mass_ref):
        total = m_ref[...]
        num = own_ref[...] + PRIOR * cents_ref[...].astype(F32)
        for g in (g1, g2, g3):
            extra = g[256:272, 0:256].astype(F32)
            total = total + (extra[0:1] + extra[1:2] + extra[2:3])
            num = num + g[0:256, :].astype(F32)
        mass_ref[...] = total
        pts_ref[...] = (num / (as_column(total) + PRIOR)).astype(BF)

    return pl.pallas_call(
        kernel,
        grid_spec=pltpu.PrefetchScalarGridSpec(
            num_scalar_prefetch=1,
            grid=(1,),
            in_specs=[
                pl.BlockSpec((256, D), lambda i, s: (half, 0)),
                pl.BlockSpec((1, 256), lambda i, s: (0, half)),
            ]
            + [pl.BlockSpec((272, D), lambda i, s: (0, 0))] * 3
            + [pl.BlockSpec((256, D), lambda i, s: (s[0] * 2 + half, 0))],
            out_specs=[pl.BlockSpec((256, D), lambda i, s: (0, 0)), pl.BlockSpec((1, 256), lambda i, s: (0, 0))],
        ),
        out_shape=[shape((256, D), BF), shape((1, 256), F32)],
        name="finish_one",
    )(idx, own, own_mass, *got, cents)


def turn_points(points, masses):
    def kernel(p0, p1, m0, m1, o_ref, tall):
        for h, p_ref in enumerate((p0, p1)):
            for at in range(0, D, 128):
                tall[pl.ds(at, 128), h * 256 : h * 256 + 256] = p_ref[:, pl.ds(at, 128)].astype(F32).T.astype(BF)
        packed = mass_rows(jnp.concatenate([m0[...], m1[...]], axis=1)).astype(BF)
        for d in range(8):
            o_ref[d, 0:96, :] = tall[pl.ds(d * 96, 96), :]
            o_ref[d, 96:112, :] = packed

    return pl.pallas_call(
        kernel,
        in_specs=[VMEM] * 4,
        scratch_shapes=[pltpu.VMEM((D, 512), BF)],
        out_shape=shape((8, 112, 512), BF),
        name="turn_points",
    )(*points, *masses)


def gather_one(parts):
    def kernel(x_ref, o_ref, m_ref):
        for s in range(8):
            block = (s % 2) * 4 + s // 2
            o_ref[:, block * 512 : block * 512 + 512] = x_ref[s, 0:96, :].astype(F32)
            t = x_ref[s, 96:112, :].astype(F32)
            m_ref[block : block + 1, :] = t[0:1] + t[1:2] + t[2:3]

    return pl.pallas_call(
        kernel,
        in_specs=[VMEM],
        out_shape=[shape((96, 4096), F32), shape((8, 512), F32)],
        name="gather_one",
    )(parts)


def join_two(a, b):
    def kernel(a_ref, b_ref, o_ref, n_ref):
        for at, ref in ((0, a_ref), (256, b_ref)):
            block = ref[...]
            o_ref[at : at + 256, :] = block
            n_ref[at : at + 256, :] = jnp.broadcast_to(square_norms(block), (256, 128))

    return pl.pallas_call(
        kernel,
        in_specs=[VMEM] * 2,
        out_shape=[shape((512, D), BF), shape((512, 128), F32)],
        name="join_two",
    )(a, b)


def norms_of(block):
    def kernel(c_ref, n_ref):
        n_ref[...] = jnp.broadcast_to(square_norms(c_ref[...]), (512, 128))

    return pl.pallas_call(
        kernel, in_specs=[VMEM], out_shape=shape((512, 128), F32), name="norms_of"
    )(block)


def scores_two(places, own, theirs, two, norms, half, old=()):
    def kernel(places_ref, a_ref, b_ref, *refs):
        cents, ns = refs[0:4], refs[4:8]
        p_ref, stat_ref, scores = refs[-3:]
        i = pl.program_id(0)
        twice = jnp.where(i == 0, a_ref[...], b_ref[...]) * 2
        top = None
        for slot in range(8):
            here = pl.ds((slot % 2) * 256, 256)
            n = ns[slot // 2][here, :]
            s = nt(cents[slot // 2][here, :], twice) - jnp.concatenate([n, n], axis=1)
            scores[pl.ds(slot * 256, 256), :] = s
            t = fold_rows(s, jnp.maximum)
            top = t if top is None else jnp.maximum(top, t)
        m = jnp.max(top, axis=0, keepdims=True)
        total = None
        for slot in range(8):
            e = jnp.exp(scores[pl.ds(slot * 256, 256), :] - m)
            p_ref[pl.ds(pl.multiple_of(places_ref[slot] * 256, 256), 256), :] = e
            t = fold_rows(e, jnp.add)
            total = t if total is None else total + t

        @pl.when(i == 0)
        def _():
            stat_ref[...] = refs[9][...] if old else jnp.zeros_like(stat_ref)

        cols = pl.ds(pl.multiple_of((half * 2 + i) * 256, 256), 256)
        stat_ref[0:1, cols] = m
        stat_ref[1:2, cols] = jnp.sum(total, axis=0, keepdims=True)

    whole = lambda r, c: pl.BlockSpec((r, c), lambda i, s: (0, 0))
    return pl.pallas_call(
        kernel,
        grid_spec=pltpu.PrefetchScalarGridSpec(
            num_scalar_prefetch=1,
            grid=(2,),
            in_specs=[whole(256, D)] * 2 + [whole(512, D)] * 4 + [whole(512, 128)] * 4
            + ([ANY, whole(2, 1024)] if old else []),
            out_specs=[pl.BlockSpec((2048, 256), lambda i, s: (0, half * 2 + i)), whole(2, 1024)],
            scratch_shapes=[pltpu.VMEM((2048, 256), F32)],
        ),
        out_shape=[shape((2048, 1024), F32), shape((2, 1024), F32)],
        input_output_aliases={11: 0} if old else {},
        name="scores_two",
    )(places, own, theirs, *two, *norms, *old)


def sums_two(p, stat, other, points):
    def kernel(p_ref, s_ref, r_ref, x0, x1, x2, x3, o_ref, rows, factor):
        @pl.when(pl.program_id(0) == 0)
        def _():
            for at, ref in zip(range(0, 1024, 256), (x0, x1, x2, x3)):
                rows[at : at + 256, :] = ref[...]
            theirs = jnp.concatenate([r_ref[:, at : at + 256] for at in (256, 0, 768, 512)], axis=1)
            mine = s_ref[...]
            m = jnp.maximum(mine[0:1], theirs[0:1])
            near = jnp.exp(mine[0:1] - m)
            total = mine[1:2] * near + theirs[1:2] * jnp.exp(theirs[0:1] - m)
            factor[0:1, :] = near / total

        w = (p_ref[...] * factor[0:1, :]).astype(BF)
        num = nn(w, rows[...])
        packed = mass_rows(as_row(lane_sums(w)))
        for q in range(32):
            for j in range(6):
                o_ref[q, j * 32 : j * 32 + 32, :] = num[q * 32 : q * 32 + 32, j * 128 : j * 128 + 128].astype(BF)
            lanes = packed[:, (q // 4) * 128 : (q // 4) * 128 + 128]
            turn = (128 - (q % 4) * 32) % 128
            o_ref[q, 192:TALL, :] = (pltpu.roll(lanes, turn, 1) if turn else lanes).astype(BF)

    whole = lambda r, c: pl.BlockSpec((r, c), lambda i: (0, 0))
    return pl.pallas_call(
        kernel,
        grid=(2,),
        in_specs=[pl.BlockSpec((1024, 1024), lambda i: (i, 0)), whole(2, 1024), whole(2, 1024)] + [whole(256, D)] * 4,
        out_specs=pl.BlockSpec((32, TALL, 128), lambda i: (i, 0, 0)),
        scratch_shapes=[pltpu.VMEM((1024, D), BF), pltpu.VMEM((8, 1024), F32)],
        out_shape=shape((64, TALL, 128), BF),
        name="sums_two",
    )(p, stat, other, *points)


def finish_two(total, cents):
    def kernel(x_ref, c_ref, o_ref):
        mass = x_ref[192:193, :] + x_ref[193:194, :] + x_ref[194:195, :]
        column = as_column(mass)[0:32] + PRIOR
        packed = mass_rows(mass).astype(BF)
        for j in range(6):
            num = x_ref[j * 32 : j * 32 + 32, :] + PRIOR * c_ref[:, j * 128 : j * 128 + 128].astype(F32)
            new = (num / column).astype(BF)
            for q in range(8):
                o_ref[q, j * 32 : j * 32 + 32, :] = new
        for q in range(8):
            o_ref[q, 192:TALL, :] = packed

    return pl.pallas_call(
        kernel, in_specs=[VMEM] * 2, out_shape=shape((8, TALL, 128), BF), name="finish_two"
    )(total, cents)


def gather_two(core, mine, theirs):
    def kernel(core_ref, a_ref, b_ref, o_ref, m_ref):
        lane = lax.broadcasted_iota(jnp.int32, (16, 128), 1)
        for ref, half in ((a_ref, core_ref[0]), (b_ref, 1 - core_ref[0])):
            start = pl.multiple_of(half * 256, 256)
            for q in range(8):
                for j in range(6):
                    o_ref[pl.ds(start + q * 32, 32), j * 128 : j * 128 + 128] = ref[q, j * 32 : j * 32 + 32, :].astype(F32)
            for g in range(2):
                row = None
                for r in range(4):
                    t = ref[g * 4 + r, 192:TALL, :].astype(F32)
                    t = pltpu.roll(t, r * 32, 1) if r else t
                    row = t if row is None else jnp.where(lane >= r * 32, t, row)
                m_ref[:, pl.ds(start + g * 128, 128)] = row[0:1] + row[1:2] + row[2:3]

    return pl.pallas_call(
        kernel,
        in_specs=[SMEM] + [VMEM] * 2,
        out_shape=[shape((512, D), F32), shape((1, 512), F32)],
        name="gather_two",
    )(core, mine, theirs)


def shift_y(x, k):
    return lax.ppermute(x, "y", [(i, (i + k) % 4) for i in range(4)])


def shift_z(x, k):
    return lax.ppermute(x, "z", [(i, (i + k) % 4) for i in range(4)])


def flip(x, axis):
    return lax.ppermute(x, axis, [(0, 1), (1, 0)])


def flip_x(x):
    return lax.ppermute(x, ("xh", "xl"), [(0, 3), (1, 2), (2, 1), (3, 0)])


def after(x, *others):
    return lax.optimization_barrier((x,) + others)[0]


def body(embeddings, cents_one, cents_two):
    y = lax.axis_index("y").astype(jnp.int32)
    xh = lax.axis_index("xh").astype(jnp.int32)
    z = lax.axis_index("z").astype(jnp.int32)
    xl = lax.axis_index("xl").astype(jnp.int32)
    c = lax.axis_index("c").astype(jnp.int32)
    halves = jnp.stack([xh * 2 + c, xh * 2 + 1 - c, 2 - xh * 2 + c, 3 - xh * 2 - c])
    idx = jnp.concatenate([xh * 4 + (y + jnp.arange(4, dtype=jnp.int32)) % 4, halves, jnp.stack([c, 1 - c])])
    slot = jnp.arange(8, dtype=jnp.int32)
    places = (y - slot) % 4 * 2 + (xh ^ (slot // 4))

    mine = lax.dynamic_slice_in_dim(embeddings, c * 512, 512, 0).astype(BF)
    far_mine = flip_x(mine)
    half_two = lax.dynamic_slice_in_dim(cents_two, c * 256, 256, 0)
    around = [shift_y(half_two, k) for k in (1, 2, 3)]

    p, x, near, norms = scores_near(idx, embeddings, cents_one)
    near_a, norms_a = join_two(after(half_two, near), around[0])
    far_mine = after(far_mine, near, norms_a, around[2])
    far_other = flip(far_mine, "c")
    far_a = flip_x(after(near_a, far_mine))
    p, x, local = scores_far(idx, far_mine, far_other, cents_one, norms, near, p, x)

    spread = merge_cores(local, flip(local, "c"))
    stats = lax.all_to_all(spread, ("xh", "z", "xl"), 0, 0, tiled=True)
    near_b, norms_b = join_two(after(around[1], spread), around[2])
    norms_c = norms_of(after(far_a, spread))
    factor = merge_last(idx, stats, after(local, norms_b, norms_c))

    parts_0 = sums_far(p, factor, x, 0)
    got_0 = [shift_y(part, k) for part, k in zip(parts_0, (2, 1, 3))]
    far_b = flip_x(after(near_b, parts_0[0]))
    parts_1 = sums_far(p, after(factor, parts_0[0]), x, 1)
    own, own_mass = sums_own(p, after(factor, parts_1[0]), x)
    got_1 = [shift_y(parts_1[0], 2)] + [shift_y(after(part, own_mass), k) for part, k in zip(parts_1[1:], (1, 3))]
    two = (near_a, near_b, far_a, far_b)
    norms_two = (norms_a, norms_b, norms_c, norms_of(after(far_b, own_mass)))

    points_0, mass_0 = finish_one(idx, own, own_mass, got_0, cents_one, 0)
    theirs_0 = flip(points_0, "c")
    old = scores_two(places, points_0, theirs_0, two, norms_two, 0)
    points_1, mass_1 = finish_one(idx, own, after(own_mass, old[1]), got_1, cents_one, 1)
    theirs_1 = flip(points_1, "c")
    tall = turn_points((points_0, points_1), (mass_0, mass_1))
    columns = lax.all_to_all(tall, ("y", "xh"), 0, 0, tiled=True)
    p2, stat2 = scores_two(places, after(points_1, tall), theirs_1, two, norms_two, 1, tuple(old))
    packed = sums_two(p2, stat2, flip(stat2, "c"), (points_0, theirs_0, points_1, theirs_1))
    parts = lax.all_to_all(after(packed, columns), ("y", "xh", "z", "xl"), 0, 0, tiled=True)
    turned_one, mass_one = gather_one(columns)
    total = jnp.sum(parts.astype(F32), axis=0)
    rows = lax.dynamic_slice_in_dim(cents_two, c * 256 + z * 64 + xl * 32, 32, 0)
    spread = finish_two(total, after(rows, turned_one))
    block = lax.all_to_all(spread, ("z", "xl"), 0, 0, tiled=True)
    updated_two, mass_two = gather_two(c[None], block, flip(block, "c"))
    return turned_one.T, mass_one.reshape(4096), updated_two, mass_two.reshape(512)


def solution(mesh):
    fine = Mesh(mesh.devices.reshape(4, 2, 4, 2, 2), ("y", "xh", "z", "xl", "c"))
    dp, cent = ("y", "xh"), ("z", "xl", "c")
    return jax.shard_map(
        body,
        mesh=fine,
        in_specs=(P(dp, None), P(cent, None), P(dp, None)),
        out_specs=(P(cent, dp), P(cent), P(dp, None), P(dp)),
        check_vma=False,
    )
```

```python
import jax
import jax.numpy as jnp
from jax import lax
from jax.experimental import pallas as pl
from jax.experimental.pallas import tpu as pltpu
from jax.sharding import Mesh, PartitionSpec as P

PRIOR = 0.5
BF = jnp.bfloat16
F32 = jnp.float32
D = 768
TALL = 208
SMEM = pl.BlockSpec(memory_space=pltpu.SMEM)
VMEM = pl.BlockSpec(memory_space=pltpu.VMEM)


def nt(left, right):
    return lax.dot_general(left, right, (((1,), (1,)), ((), ())), preferred_element_type=F32)


def nn(left, right):
    return lax.dot_general(left, right, (((1,), (0,)), ((), ())), preferred_element_type=F32)


def shape(dims, dtype):
    return jax.ShapeDtypeStruct(dims, dtype)


def square_norms(block):
    wide = block.astype(F32)
    return jnp.sum(wide * wide, axis=1, keepdims=True)


def fold_rows(block, op):
    parts = [block[i : i + 8] for i in range(0, block.shape[0], 8)]
    while len(parts) > 1:
        parts = [op(parts[i], parts[i + 1]) for i in range(0, len(parts) - 1, 2)] + (
            [parts[-1]] if len(parts) % 2 else []
        )
    return parts[0]


def lane_sums(w):
    wide = w.astype(F32)
    part = wide[:, 0:128]
    for j in range(128, wide.shape[1], 128):
        part = part + wide[:, j : j + 128]
    return jnp.sum(part, axis=1, keepdims=True)


def as_row(column):
    return jnp.broadcast_to(column, (column.shape[0], 128)).T[0:1, :]


def as_column(row):
    return jnp.broadcast_to(row, (128, row.shape[1])).T[:, 0:1]


def mass_rows(row):
    t = jnp.broadcast_to(row, (16, row.shape[1]))
    hi = t.astype(BF).astype(F32)
    mid = (t - hi).astype(BF).astype(F32)
    low = t - hi - mid
    at = lax.broadcasted_iota(jnp.int32, t.shape, 0)
    return jnp.where(at == 0, hi, jnp.where(at == 1, mid, jnp.where(at == 2, low, 0.0)))


def scores_step(cents, twice, norms, p_ref, scores):
    top = None
    for k in range(4):
        for h in range(2):
            at = k * 512 + h * 256
            n = norms[pl.ds(at, 256), :]
            s = nt(cents[k][pl.ds(h * 256, 256), :], twice) - jnp.concatenate([n, n], axis=1)
            scores[pl.ds(at, 256), :] = s
            t = fold_rows(s, jnp.maximum)
            top = t if top is None else jnp.maximum(top, t)
    m = jnp.max(top, axis=0, keepdims=True)
    total = None
    for at in range(0, 2048, 256):
        e = jnp.exp(scores[pl.ds(at, 256), :] - m)
        p_ref[pl.ds(at, 256), :] = e
        t = fold_rows(e, jnp.add)
        total = t if total is None else total + t
    return m, jnp.sum(total, axis=0, keepdims=True)


def put_stats(stat_ref, row, i, m, l):
    cols = pl.ds(pl.multiple_of(lax.rem(i, 2) * 256, 256), 256)
    stat_ref[pl.ds(row, 1), cols] = m
    stat_ref[pl.ds(4 + row, 1), cols] = l


def scores_near_kernel(idx, e_ref, c0, c1, c2, c3, p_ref, x_ref, stat_ref, norms_ref, scores):
    i = pl.program_id(0)
    cents = (c0, c1, c2, c3)

    @pl.when(i == 0)
    def _():
        stat_ref[...] = jnp.zeros_like(stat_ref)
        for k in range(4):
            for h in range(2):
                n = square_norms(cents[k][pl.ds(h * 256, 256), :])
                norms_ref[pl.ds(k * 512 + h * 256, 256), :] = jnp.broadcast_to(n, (256, 128))

    x = e_ref[...].astype(BF)
    x_ref[...] = x
    m, l = scores_step(cents, x * 2, norms_ref, p_ref, scores)
    put_stats(stat_ref, idx[4 + i // 2], i, m, l)


def scores_far_kernel(idx, a_ref, b_ref, c0, c1, c2, c3, norms_ref, near_ref, p_old, x_old, p_ref, x_ref, stat_ref, scores):
    i = pl.program_id(0)

    @pl.when(i == 0)
    def _():
        stat_ref[...] = near_ref[...]

    x = jnp.where(i < 2, a_ref[...], b_ref[...])
    x_ref[...] = x
    m, l = scores_step((c0, c1, c2, c3), x * 2, norms_ref, p_ref, scores)
    put_stats(stat_ref, idx[6 + i // 2], i, m, l)


ANY = pl.BlockSpec(memory_space=pl.ANY)
ROW_IN = [
    pl.BlockSpec((256, D), lambda i, s: (jnp.minimum(i, 1), 0)),
    pl.BlockSpec((256, D), lambda i, s: (jnp.maximum(i - 2, 0), 0)),
]
CENTS_IN = [pl.BlockSpec((512, D), lambda i, s, k=k: (s[k], 0)) for k in range(4)]
WHOLE_STAT = pl.BlockSpec((8, 512), lambda i, s: (0, 0))
WHOLE_NORMS = pl.BlockSpec((2048, 128), lambda i, s: (0, 0))


def scores_near(idx, embeddings, cents):
    return pl.pallas_call(
        scores_near_kernel,
        grid_spec=pltpu.PrefetchScalarGridSpec(
            num_scalar_prefetch=1,
            grid=(4,),
            in_specs=[pl.BlockSpec((256, D), lambda i, s: (s[8 + i // 2] * 2 + i % 2, 0))] + CENTS_IN,
            out_specs=[
                pl.BlockSpec((2048, 256), lambda i, s: (0, i)),
                pl.BlockSpec((256, D), lambda i, s: (i, 0)),
                WHOLE_STAT,
                WHOLE_NORMS,
            ],
            scratch_shapes=[pltpu.VMEM((2048, 256), F32)],
        ),
        out_shape=[
            shape((2048, 2048), F32),
            shape((2048, D), BF),
            shape((8, 512), F32),
            shape((2048, 128), F32),
        ],
        cost_estimate=pl.CostEstimate(
            flops=2 * 2048 * 1024 * D, transcendentals=2048 * 1024, bytes_accessed=24 << 20
        ),
        name="scores_near",
    )(idx, embeddings, cents, cents, cents, cents)


def scores_far(idx, a, b, cents, norms, near, p, x):
    return pl.pallas_call(
        scores_far_kernel,
        grid_spec=pltpu.PrefetchScalarGridSpec(
            num_scalar_prefetch=1,
            grid=(4,),
            in_specs=ROW_IN + CENTS_IN + [WHOLE_NORMS, WHOLE_STAT, ANY, ANY],
            out_specs=[
                pl.BlockSpec((2048, 256), lambda i, s: (0, 4 + i)),
                pl.BlockSpec((256, D), lambda i, s: (4 + i, 0)),
                WHOLE_STAT,
            ],
            scratch_shapes=[pltpu.VMEM((2048, 256), F32)],
        ),
        out_shape=[shape((2048, 2048), F32), shape((2048, D), BF), shape((8, 512), F32)],
        input_output_aliases={9: 0, 10: 1},
        name="scores_far",
    )(idx, a, b, cents, cents, cents, cents, norms, near, p, x)


def merge_all(stats):
    m = stats[0][0:4]
    for t in stats[1:]:
        m = jnp.maximum(m, t[0:4])
    total = None
    for t in stats:
        part = t[4:8] * jnp.exp(t[0:4] - m)
        total = part if total is None else total + part
    return m, total


def merge_cores(local, other):
    def kernel(a, b, o_ref):
        m, total = merge_all([a[...], b[...]])
        both = jnp.concatenate([m, total], axis=0)
        for i in range(16):
            o_ref[i] = both

    return pl.pallas_call(
        kernel, in_specs=[VMEM] * 2, out_shape=shape((16, 8, 512), F32), name="merge_cores"
    )(local, other)


def merge_last(idx, stats, local):
    def kernel(idx_ref, s_ref, l_ref, f_ref, tmp):
        m, total = merge_all([s_ref[i] for i in range(16)])
        tmp[0:4, :] = jnp.exp(l_ref[0:4, :] - m) / total
        for r in range(4):
            f_ref[:, r * 512 : (r + 1) * 512] = tmp[pl.ds(idx_ref[4 + r], 1), :]

    return pl.pallas_call(
        kernel,
        in_specs=[SMEM] + [VMEM] * 2,
        scratch_shapes=[pltpu.VMEM((8, 512), F32)],
        out_shape=shape((1, 2048), F32),
        name="merge_last",
    )(idx, stats, local)


def sums_far(p, factor, x, half):
    def kernel(p_ref, f_ref, x_ref, *refs):
        w = (p_ref[...] * f_ref[...]).astype(BF)
        sums = nn(w, x_ref[...]).astype(BF)
        packed = mass_rows(as_row(lane_sums(w))).astype(BF)
        for q in range(3):

            @pl.when(pl.program_id(0) == q)
            def _(q=q):
                refs[q][0:256, :] = sums
                refs[q][256:272, 0:256] = packed
                refs[q][256:272, 256:D] = jnp.zeros((16, D - 256), BF)

    return pl.pallas_call(
        kernel,
        grid=(3,),
        in_specs=[
            pl.BlockSpec((256, 2048), lambda j: ((2 - j + 3 * (j // 2)) * 2 + half, 0)),
            pl.BlockSpec((1, 2048), lambda j: (0, 0)),
            pl.BlockSpec((2048, D), lambda j: (0, 0)),
        ],
        out_specs=[pl.BlockSpec((272, D), lambda j: (0, 0))] * 3,
        out_shape=[shape((272, D), BF)] * 3,
        name="sums_far",
    )(p, factor, x)


def sums_rest(p, factor, x):
    def kernel(p_ref, f_ref, x_ref, g2, g1, g3, own_ref, m_ref):
        w = (p_ref[...] * f_ref[...]).astype(BF)
        sums = nn(w, x_ref[...])
        mass = as_row(lane_sums(w))
        j = pl.program_id(0)
        for q, ref in enumerate((g2, g1, g3)):

            @pl.when(j == q)
            def _(ref=ref):
                ref[0:256, :] = sums.astype(BF)
                ref[256:272, 0:256] = mass_rows(mass).astype(BF)
                ref[256:272, 256:D] = jnp.zeros((16, D - 256), BF)

        @pl.when(j >= 3)
        def _():
            own_ref[...] = sums
            m_ref[...] = mass

    return pl.pallas_call(
        kernel,
        grid=(5,),
        in_specs=[
            pl.BlockSpec((256, 2048), lambda j: (jnp.where(j < 3, (2 - j + 3 * (j // 2)) * 2 + 1, j - 3), 0)),
            pl.BlockSpec((1, 2048), lambda j: (0, 0)),
            pl.BlockSpec((2048, D), lambda j: (0, 0)),
        ],
        out_specs=[pl.BlockSpec((272, D), lambda j: (0, 0))] * 3
        + [
            pl.BlockSpec((256, D), lambda j: (jnp.maximum(j - 3, 0), 0)),
            pl.BlockSpec((1, 256), lambda j: (0, jnp.maximum(j - 3, 0))),
        ],
        out_shape=[shape((272, D), BF)] * 3 + [shape((512, D), F32), shape((1, 512), F32)],
        name="sums_rest",
    )(p, factor, x)


def finish_one(idx, own, own_mass, got, cents, half):
    def kernel(idx_ref, own_ref, m_ref, g1, g2, g3, cents_ref, pts_ref, mass_ref):
        total = m_ref[...]
        num = own_ref[...] + PRIOR * cents_ref[...].astype(F32)
        for g in (g1, g2, g3):
            extra = g[256:272, 0:256].astype(F32)
            total = total + (extra[0:1] + extra[1:2] + extra[2:3])
            num = num + g[0:256, :].astype(F32)
        mass_ref[...] = total
        pts_ref[...] = (num / (as_column(total) + PRIOR)).astype(BF)

    return pl.pallas_call(
        kernel,
        grid_spec=pltpu.PrefetchScalarGridSpec(
            num_scalar_prefetch=1,
            grid=(1,),
            in_specs=[
                pl.BlockSpec((256, D), lambda i, s: (half, 0)),
                pl.BlockSpec((1, 256), lambda i, s: (0, half)),
            ]
            + [pl.BlockSpec((272, D), lambda i, s: (0, 0))] * 3
            + [pl.BlockSpec((256, D), lambda i, s: (s[0] * 2 + half, 0))],
            out_specs=[pl.BlockSpec((256, D), lambda i, s: (0, 0)), pl.BlockSpec((1, 256), lambda i, s: (0, 0))],
        ),
        out_shape=[shape((256, D), BF), shape((1, 256), F32)],
        name="finish_one",
    )(idx, own, own_mass, *got, cents)


def turn_points(owners, points, masses):
    def kernel(owners_ref, p0, p1, m0, m1, *refs):
        tall = refs[8]
        for h, p_ref in enumerate((p0, p1)):
            for at in range(0, D, 128):
                tall[pl.ds(at, 128), h * 256 : h * 256 + 256] = p_ref[:, pl.ds(at, 128)].astype(F32).T.astype(BF)
        packed = mass_rows(jnp.concatenate([m0[...], m1[...]], axis=1)).astype(BF)
        for r in range(8):
            refs[r][0:96, :] = tall[pl.ds(pl.multiple_of(owners_ref[r] * 96, 32), 96), :]
            refs[r][96:112, :] = packed

    return pl.pallas_call(
        kernel,
        in_specs=[SMEM] + [VMEM] * 4,
        scratch_shapes=[pltpu.VMEM((D, 512), BF)],
        out_shape=[shape((112, 512), BF)] * 8,
        name="turn_points",
    )(owners, *points, *masses)


def gather_one(sources, pieces):
    def kernel(sources_ref, *refs):
        o_ref, m_ref = refs[8:]
        for r in range(8):
            block = sources_ref[r]
            o_ref[:, pl.ds(pl.multiple_of(block * 512, 512), 512)] = refs[r][0:96, :].astype(F32)
            t = refs[r][96:112, :].astype(F32)
            m_ref[pl.ds(block, 1), :] = t[0:1] + t[1:2] + t[2:3]

    return pl.pallas_call(
        kernel,
        in_specs=[SMEM] + [VMEM] * 8,
        out_shape=[shape((96, 4096), F32), shape((8, 512), F32)],
        name="gather_one",
    )(sources, *pieces)


def join_two(a, b):
    def kernel(a_ref, b_ref, o_ref, n_ref):
        for at, ref in ((0, a_ref), (256, b_ref)):
            block = ref[...]
            o_ref[at : at + 256, :] = block
            n_ref[at : at + 256, :] = jnp.broadcast_to(square_norms(block), (256, 128))

    return pl.pallas_call(
        kernel,
        in_specs=[VMEM] * 2,
        out_shape=[shape((512, D), BF), shape((512, 128), F32)],
        name="join_two",
    )(a, b)


def norms_of(block):
    def kernel(c_ref, n_ref):
        n_ref[...] = jnp.broadcast_to(square_norms(c_ref[...]), (512, 128))

    return pl.pallas_call(
        kernel, in_specs=[VMEM], out_shape=shape((512, 128), F32), name="norms_of"
    )(block)


def scores_two(places, own, theirs, two, norms, half, old=()):
    def kernel(places_ref, a_ref, b_ref, *refs):
        cents, ns = refs[0:4], refs[4:8]
        p_ref, stat_ref, scores = refs[-3:]
        i = pl.program_id(0)
        twice = jnp.where(i == 0, a_ref[...], b_ref[...]) * 2
        top = None
        for slot in range(8):
            here = pl.ds((slot % 2) * 256, 256)
            n = ns[slot // 2][here, :]
            s = nt(cents[slot // 2][here, :], twice) - jnp.concatenate([n, n], axis=1)
            scores[pl.ds(slot * 256, 256), :] = s
            t = fold_rows(s, jnp.maximum)
            top = t if top is None else jnp.maximum(top, t)
        m = jnp.max(top, axis=0, keepdims=True)
        total = None
        for slot in range(8):
            e = jnp.exp(scores[pl.ds(slot * 256, 256), :] - m)
            p_ref[pl.ds(pl.multiple_of(places_ref[slot] * 256, 256), 256), :] = e
            t = fold_rows(e, jnp.add)
            total = t if total is None else total + t

        @pl.when(i == 0)
        def _():
            stat_ref[...] = refs[9][...] if old else jnp.zeros_like(stat_ref)

        cols = pl.ds(pl.multiple_of((half * 2 + i) * 256, 256), 256)
        stat_ref[0:1, cols] = m
        stat_ref[1:2, cols] = jnp.sum(total, axis=0, keepdims=True)

    whole = lambda r, c: pl.BlockSpec((r, c), lambda i, s: (0, 0))
    return pl.pallas_call(
        kernel,
        grid_spec=pltpu.PrefetchScalarGridSpec(
            num_scalar_prefetch=1,
            grid=(2,),
            in_specs=[whole(256, D)] * 2 + [whole(512, D)] * 4 + [whole(512, 128)] * 4
            + ([ANY, whole(2, 1024)] if old else []),
            out_specs=[pl.BlockSpec((2048, 256), lambda i, s: (0, half * 2 + i)), whole(2, 1024)],
            scratch_shapes=[pltpu.VMEM((2048, 256), F32)],
        ),
        out_shape=[shape((2048, 1024), F32), shape((2, 1024), F32)],
        input_output_aliases={11: 0} if old else {},
        name="scores_two",
    )(places, own, theirs, *two, *norms, *old)


def sums_two(p, stat, other, points):
    def kernel(p_ref, s_ref, r_ref, x0, x1, x2, x3, o_ref, rows, factor):
        @pl.when(pl.program_id(0) == 0)
        def _():
            for at, ref in zip(range(0, 1024, 256), (x0, x1, x2, x3)):
                rows[at : at + 256, :] = ref[...]
            theirs = jnp.concatenate([r_ref[:, at : at + 256] for at in (256, 0, 768, 512)], axis=1)
            mine = s_ref[...]
            m = jnp.maximum(mine[0:1], theirs[0:1])
            near = jnp.exp(mine[0:1] - m)
            total = mine[1:2] * near + theirs[1:2] * jnp.exp(theirs[0:1] - m)
            factor[0:1, :] = near / total

        w = (p_ref[...] * factor[0:1, :]).astype(BF)
        num = nn(w, rows[...])
        packed = mass_rows(as_row(lane_sums(w)))
        for q in range(32):
            for j in range(6):
                o_ref[q, j * 32 : j * 32 + 32, :] = num[q * 32 : q * 32 + 32, j * 128 : j * 128 + 128].astype(BF)
            lanes = packed[:, (q // 4) * 128 : (q // 4) * 128 + 128]
            turn = (128 - (q % 4) * 32) % 128
            o_ref[q, 192:TALL, :] = (pltpu.roll(lanes, turn, 1) if turn else lanes).astype(BF)

    whole = lambda r, c: pl.BlockSpec((r, c), lambda i: (0, 0))
    return pl.pallas_call(
        kernel,
        grid=(2,),
        in_specs=[pl.BlockSpec((1024, 1024), lambda i: (i, 0)), whole(2, 1024), whole(2, 1024)] + [whole(256, D)] * 4,
        out_specs=pl.BlockSpec((32, TALL, 128), lambda i: (i, 0, 0)),
        scratch_shapes=[pltpu.VMEM((1024, D), BF), pltpu.VMEM((8, 1024), F32)],
        out_shape=shape((64, TALL, 128), BF),
        name="sums_two",
    )(p, stat, other, *points)


def finish_two(total, cents):
    def kernel(x_ref, c_ref, o_ref):
        mass = x_ref[192:193, :] + x_ref[193:194, :] + x_ref[194:195, :]
        column = as_column(mass)[0:32] + PRIOR
        packed = mass_rows(mass).astype(BF)
        for j in range(6):
            num = x_ref[j * 32 : j * 32 + 32, :] + PRIOR * c_ref[:, j * 128 : j * 128 + 128].astype(F32)
            new = (num / column).astype(BF)
            for q in range(8):
                o_ref[q, j * 32 : j * 32 + 32, :] = new
        for q in range(8):
            o_ref[q, 192:TALL, :] = packed

    return pl.pallas_call(
        kernel, in_specs=[VMEM] * 2, out_shape=shape((8, TALL, 128), BF), name="finish_two"
    )(total, cents)


def gather_two(core, mine, theirs):
    def kernel(core_ref, a_ref, b_ref, o_ref, m_ref):
        lane = lax.broadcasted_iota(jnp.int32, (16, 128), 1)
        for ref, half in ((a_ref, core_ref[0]), (b_ref, 1 - core_ref[0])):
            start = pl.multiple_of(half * 256, 256)
            for q in range(8):
                for j in range(6):
                    o_ref[pl.ds(start + q * 32, 32), j * 128 : j * 128 + 128] = ref[q, j * 32 : j * 32 + 32, :].astype(F32)
            for g in range(2):
                row = None
                for r in range(4):
                    t = ref[g * 4 + r, 192:TALL, :].astype(F32)
                    t = pltpu.roll(t, r * 32, 1) if r else t
                    row = t if row is None else jnp.where(lane >= r * 32, t, row)
                m_ref[:, pl.ds(start + g * 128, 128)] = row[0:1] + row[1:2] + row[2:3]

    return pl.pallas_call(
        kernel,
        in_specs=[SMEM] + [VMEM] * 2,
        out_shape=[shape((512, D), F32), shape((1, 512), F32)],
        name="gather_two",
    )(core, mine, theirs)


def shift_y(x, k):
    return lax.ppermute(x, "y", [(i, (i + k) % 4) for i in range(4)])


def shift_z(x, k):
    return lax.ppermute(x, "z", [(i, (i + k) % 4) for i in range(4)])


def flip(x, axis):
    return lax.ppermute(x, axis, [(0, 1), (1, 0)])


def flip_x(x):
    return lax.ppermute(x, ("xh", "xl"), [(0, 3), (1, 2), (2, 1), (3, 0)])


def after(x, *others):
    return lax.optimization_barrier((x,) + others)[0]


def body(embeddings, cents_one, cents_two):
    y = lax.axis_index("y").astype(jnp.int32)
    xh = lax.axis_index("xh").astype(jnp.int32)
    z = lax.axis_index("z").astype(jnp.int32)
    xl = lax.axis_index("xl").astype(jnp.int32)
    c = lax.axis_index("c").astype(jnp.int32)
    halves = jnp.stack([xh * 2 + c, xh * 2 + 1 - c, 2 - xh * 2 + c, 3 - xh * 2 - c])
    idx = jnp.concatenate([xh * 4 + (y + jnp.arange(4, dtype=jnp.int32)) % 4, halves, jnp.stack([c, 1 - c])])
    slot = jnp.arange(8, dtype=jnp.int32)
    places = (y - slot) % 4 * 2 + (xh ^ (slot // 4))

    mine = lax.dynamic_slice_in_dim(embeddings, c * 512, 512, 0).astype(BF)
    far_mine = flip_x(mine)
    half_two = lax.dynamic_slice_in_dim(cents_two, c * 256, 256, 0)
    around = [shift_y(half_two, k) for k in (1, 2, 3)]

    p, x, near, norms = scores_near(idx, embeddings, cents_one)
    near_a, norms_a = join_two(after(half_two, near), around[0])
    far_mine = after(far_mine, near, norms_a, around[2])
    far_other = flip(far_mine, "c")
    far_a = flip_x(after(near_a, far_mine))
    p, x, local = scores_far(idx, far_mine, far_other, cents_one, norms, near, p, x)

    spread = merge_cores(local, flip(local, "c"))
    stats = lax.all_to_all(spread, ("xh", "z", "xl"), 0, 0, tiled=True)
    near_b, norms_b = join_two(after(around[1], spread), around[2])
    norms_c = norms_of(after(far_a, spread))
    factor = merge_last(idx, stats, after(local, norms_b, norms_c))

    parts_0 = sums_far(p, factor, x, 0)
    got_0 = [shift_y(part, k) for part, k in zip(parts_0, (2, 1, 3))]
    far_b = flip_x(after(near_b, parts_0[0]))
    *parts_1, own, own_mass = sums_rest(p, after(factor, parts_0[0]), x)
    got_1 = [shift_y(part, k) for part, k in zip(parts_1, (2, 1, 3))]
    two = (near_a, near_b, far_a, far_b)
    norms_two = (norms_a, norms_b, norms_c, norms_of(after(far_b, own_mass)))

    points_0, mass_0 = finish_one(idx, own, own_mass, got_0, cents_one, 0)
    theirs_0 = flip(points_0, "c")
    old = scores_two(places, points_0, theirs_0, two, norms_two, 0)
    points_1, mass_1 = finish_one(idx, own, after(own_mass, old[1]), got_1, cents_one, 1)
    theirs_1 = flip(points_1, "c")
    p2, stat2 = scores_two(places, points_1, theirs_1, two, norms_two, 1, tuple(old))
    packed = sums_two(p2, stat2, flip(stat2, "c"), (points_0, theirs_0, points_1, theirs_1))
    parts = lax.all_to_all(packed, ("y", "xh", "z", "xl"), 0, 0, tiled=True)
    late_0, late_1 = after(points_0, packed), after(points_1, packed)
    owners = (y + slot) % 4 * 2 + (xh ^ (slot // 4))
    sources = (y - slot) % 4 + (xh ^ (slot // 4)) * 4
    tall = turn_points(owners, (late_0, late_1), (mass_0, mass_1))
    pieces = [tall[0]]
    for r in range(1, 8):
        pairs = [(a * 2 + h, (a + r) % 4 * 2 + (h ^ (r // 4))) for a in range(4) for h in range(2)]
        pieces.append(lax.ppermute(tall[r], ("y", "xh"), pairs))
    turned_one, mass_one = gather_one(sources, pieces)
    total = jnp.sum(after(parts, tall[0]).astype(F32), axis=0)
    rows = lax.dynamic_slice_in_dim(cents_two, c * 256 + z * 64 + xl * 32, 32, 0)
    spread = finish_two(total, after(rows, *pieces[1:5]))
    block = after(lax.all_to_all(spread, ("z", "xl"), 0, 0, tiled=True), *pieces[5:])
    updated_two, mass_two = gather_two(after(c[None], turned_one), block, flip(block, "c"))
    return turned_one.T, mass_one.reshape(4096), updated_two, mass_two.reshape(512)


def solution(mesh):
    fine = Mesh(mesh.devices.reshape(4, 2, 4, 2, 2), ("y", "xh", "z", "xl", "c"))
    dp, cent = ("y", "xh"), ("z", "xl", "c")
    return jax.shard_map(
        body,
        mesh=fine,
        in_specs=(P(dp, None), P(cent, None), P(dp, None)),
        out_specs=(P(cent, dp), P(cent), P(dp, None), P(dp)),
        check_vma=False,
    )
```

```python
import jax
import jax.numpy as jnp
from jax import lax
from jax.experimental import pallas as pl
from jax.experimental.pallas import tpu as pltpu
from jax.sharding import Mesh, PartitionSpec as P

PRIOR = 0.5
BF = jnp.bfloat16
F32 = jnp.float32
D = 768
TALL = 208
SMEM = pl.BlockSpec(memory_space=pltpu.SMEM)
VMEM = pl.BlockSpec(memory_space=pltpu.VMEM)


def nt(left, right):
    return lax.dot_general(left, right, (((1,), (1,)), ((), ())), preferred_element_type=F32)


def nn(left, right):
    return lax.dot_general(left, right, (((1,), (0,)), ((), ())), preferred_element_type=F32)


def shape(dims, dtype):
    return jax.ShapeDtypeStruct(dims, dtype)


def square_norms(block):
    wide = block.astype(F32)
    return jnp.sum(wide * wide, axis=1, keepdims=True)


def fold_rows(block, op):
    parts = [block[i : i + 8] for i in range(0, block.shape[0], 8)]
    while len(parts) > 1:
        parts = [op(parts[i], parts[i + 1]) for i in range(0, len(parts) - 1, 2)] + (
            [parts[-1]] if len(parts) % 2 else []
        )
    return parts[0]


def lane_sums(w):
    wide = w.astype(F32)
    part = wide[:, 0:128]
    for j in range(128, wide.shape[1], 128):
        part = part + wide[:, j : j + 128]
    return jnp.sum(part, axis=1, keepdims=True)


def as_row(column):
    return jnp.broadcast_to(column, (column.shape[0], 128)).T[0:1, :]


def as_column(row):
    return jnp.broadcast_to(row, (128, row.shape[1])).T[:, 0:1]


def mass_rows(row):
    t = jnp.broadcast_to(row, (16, row.shape[1]))
    hi = t.astype(BF).astype(F32)
    mid = (t - hi).astype(BF).astype(F32)
    low = t - hi - mid
    at = lax.broadcasted_iota(jnp.int32, t.shape, 0)
    return jnp.where(at == 0, hi, jnp.where(at == 1, mid, jnp.where(at == 2, low, 0.0)))


def scores_step(cents, twice, norms, p_ref, scores):
    top = None
    for k in range(4):
        for h in range(2):
            at = k * 512 + h * 256
            n = norms[pl.ds(at, 256), :]
            s = nt(cents[k][pl.ds(h * 256, 256), :], twice) - jnp.concatenate([n, n], axis=1)
            scores[pl.ds(at, 256), :] = s
            t = fold_rows(s, jnp.maximum)
            top = t if top is None else jnp.maximum(top, t)
    m = jnp.max(top, axis=0, keepdims=True)
    total = None
    for at in range(0, 2048, 256):
        e = jnp.exp(scores[pl.ds(at, 256), :] - m)
        p_ref[pl.ds(at, 256), :] = e
        t = fold_rows(e, jnp.add)
        total = t if total is None else total + t
    return m, jnp.sum(total, axis=0, keepdims=True)


def put_stats(stat_ref, row, i, m, l):
    cols = pl.ds(pl.multiple_of(lax.rem(i, 2) * 256, 256), 256)
    stat_ref[pl.ds(row, 1), cols] = m
    stat_ref[pl.ds(4 + row, 1), cols] = l


def scores_near_kernel(idx, e_ref, c0, c1, c2, c3, p_ref, x_ref, stat_ref, norms_ref, scores):
    i = pl.program_id(0)
    cents = (c0, c1, c2, c3)

    @pl.when(i == 0)
    def _():
        stat_ref[...] = jnp.zeros_like(stat_ref)
        for k in range(4):
            for h in range(2):
                n = square_norms(cents[k][pl.ds(h * 256, 256), :])
                norms_ref[pl.ds(k * 512 + h * 256, 256), :] = jnp.broadcast_to(n, (256, 128))

    x = e_ref[...].astype(BF)
    x_ref[...] = x
    m, l = scores_step(cents, x * 2, norms_ref, p_ref, scores)
    put_stats(stat_ref, idx[4 + i // 2], i, m, l)


def scores_far_kernel(idx, a_ref, b_ref, c0, c1, c2, c3, norms_ref, near_ref, p_old, x_old, p_ref, x_ref, stat_ref, scores):
    i = pl.program_id(0)

    @pl.when(i == 0)
    def _():
        stat_ref[...] = near_ref[...]

    x = jnp.where(i < 2, a_ref[...], b_ref[...])
    x_ref[...] = x
    m, l = scores_step((c0, c1, c2, c3), x * 2, norms_ref, p_ref, scores)
    put_stats(stat_ref, idx[6 + i // 2], i, m, l)


ANY = pl.BlockSpec(memory_space=pl.ANY)
ROW_IN = [
    pl.BlockSpec((256, D), lambda i, s: (jnp.minimum(i, 1), 0)),
    pl.BlockSpec((256, D), lambda i, s: (jnp.maximum(i - 2, 0), 0)),
]
CENTS_IN = [pl.BlockSpec((512, D), lambda i, s, k=k: (s[k], 0)) for k in range(4)]
WHOLE_STAT = pl.BlockSpec((8, 512), lambda i, s: (0, 0))
WHOLE_NORMS = pl.BlockSpec((2048, 128), lambda i, s: (0, 0))


def scores_near(idx, embeddings, cents):
    return pl.pallas_call(
        scores_near_kernel,
        grid_spec=pltpu.PrefetchScalarGridSpec(
            num_scalar_prefetch=1,
            grid=(4,),
            in_specs=[pl.BlockSpec((256, D), lambda i, s: (s[8 + i // 2] * 2 + i % 2, 0))] + CENTS_IN,
            out_specs=[
                pl.BlockSpec((2048, 256), lambda i, s: (0, i)),
                pl.BlockSpec((256, D), lambda i, s: (i, 0)),
                WHOLE_STAT,
                WHOLE_NORMS,
            ],
            scratch_shapes=[pltpu.VMEM((2048, 256), F32)],
        ),
        out_shape=[
            shape((2048, 2048), F32),
            shape((2048, D), BF),
            shape((8, 512), F32),
            shape((2048, 128), F32),
        ],
        cost_estimate=pl.CostEstimate(
            flops=2 * 2048 * 1024 * D, transcendentals=2048 * 1024, bytes_accessed=24 << 20
        ),
        name="scores_near",
    )(idx, embeddings, cents, cents, cents, cents)


def scores_far(idx, a, b, cents, norms, near, p, x):
    return pl.pallas_call(
        scores_far_kernel,
        grid_spec=pltpu.PrefetchScalarGridSpec(
            num_scalar_prefetch=1,
            grid=(4,),
            in_specs=ROW_IN + CENTS_IN + [WHOLE_NORMS, WHOLE_STAT, ANY, ANY],
            out_specs=[
                pl.BlockSpec((2048, 256), lambda i, s: (0, 4 + i)),
                pl.BlockSpec((256, D), lambda i, s: (4 + i, 0)),
                WHOLE_STAT,
            ],
            scratch_shapes=[pltpu.VMEM((2048, 256), F32)],
        ),
        out_shape=[shape((2048, 2048), F32), shape((2048, D), BF), shape((8, 512), F32)],
        input_output_aliases={9: 0, 10: 1},
        name="scores_far",
    )(idx, a, b, cents, cents, cents, cents, norms, near, p, x)


def merge_all(stats):
    m = stats[0][0:4]
    for t in stats[1:]:
        m = jnp.maximum(m, t[0:4])
    total = None
    for t in stats:
        part = t[4:8] * jnp.exp(t[0:4] - m)
        total = part if total is None else total + part
    return m, total


def merge_cores(local, other):
    def kernel(a, b, o_ref):
        m, total = merge_all([a[...], b[...]])
        both = jnp.concatenate([m, total], axis=0)
        for i in range(16):
            o_ref[i] = both

    return pl.pallas_call(
        kernel, in_specs=[VMEM] * 2, out_shape=shape((16, 8, 512), F32), name="merge_cores"
    )(local, other)


def merge_last(idx, stats, local):
    def kernel(idx_ref, s_ref, l_ref, f_ref, tmp):
        m, total = merge_all([s_ref[i] for i in range(16)])
        tmp[0:4, :] = jnp.exp(l_ref[0:4, :] - m) / total
        for r in range(4):
            f_ref[:, r * 512 : (r + 1) * 512] = tmp[pl.ds(idx_ref[4 + r], 1), :]

    return pl.pallas_call(
        kernel,
        in_specs=[SMEM] + [VMEM] * 2,
        scratch_shapes=[pltpu.VMEM((8, 512), F32)],
        out_shape=shape((1, 2048), F32),
        name="merge_last",
    )(idx, stats, local)


def sums_far(p, factor, x, half):
    def kernel(p_ref, f_ref, x_ref, *refs):
        w = (p_ref[...] * f_ref[...]).astype(BF)
        sums = nn(w, x_ref[...]).astype(BF)
        packed = mass_rows(as_row(lane_sums(w))).astype(BF)
        for q in range(3):

            @pl.when(pl.program_id(0) == q)
            def _(q=q):
                refs[q][0:256, :] = sums
                refs[q][256:272, 0:256] = packed
                refs[q][256:272, 256:D] = jnp.zeros((16, D - 256), BF)

    return pl.pallas_call(
        kernel,
        grid=(3,),
        in_specs=[
            pl.BlockSpec((256, 2048), lambda j: ((2 - j + 3 * (j // 2)) * 2 + half, 0)),
            pl.BlockSpec((1, 2048), lambda j: (0, 0)),
            pl.BlockSpec((2048, D), lambda j: (0, 0)),
        ],
        out_specs=[pl.BlockSpec((272, D), lambda j: (0, 0))] * 3,
        out_shape=[shape((272, D), BF)] * 3,
        name="sums_far",
    )(p, factor, x)


def sums_rest(p, factor, x):
    def kernel(p_ref, f_ref, x_ref, g2, g1, g3, own_ref, m_ref):
        w = (p_ref[...] * f_ref[...]).astype(BF)
        sums = nn(w, x_ref[...])
        mass = as_row(lane_sums(w))
        j = pl.program_id(0)
        for q, ref in enumerate((g2, g1, g3)):

            @pl.when(j == q)
            def _(ref=ref):
                ref[0:256, :] = sums.astype(BF)
                ref[256:272, 0:256] = mass_rows(mass).astype(BF)
                ref[256:272, 256:D] = jnp.zeros((16, D - 256), BF)

        @pl.when(j >= 3)
        def _():
            own_ref[...] = sums
            m_ref[...] = mass

    return pl.pallas_call(
        kernel,
        grid=(5,),
        in_specs=[
            pl.BlockSpec((256, 2048), lambda j: (jnp.where(j < 3, (2 - j + 3 * (j // 2)) * 2 + 1, j - 3), 0)),
            pl.BlockSpec((1, 2048), lambda j: (0, 0)),
            pl.BlockSpec((2048, D), lambda j: (0, 0)),
        ],
        out_specs=[pl.BlockSpec((272, D), lambda j: (0, 0))] * 3
        + [
            pl.BlockSpec((256, D), lambda j: (jnp.maximum(j - 3, 0), 0)),
            pl.BlockSpec((1, 256), lambda j: (0, jnp.maximum(j - 3, 0))),
        ],
        out_shape=[shape((272, D), BF)] * 3 + [shape((512, D), F32), shape((1, 512), F32)],
        name="sums_rest",
    )(p, factor, x)


def finish_one(idx, own, own_mass, got, cents, half):
    def kernel(idx_ref, own_ref, m_ref, g1, g2, g3, cents_ref, pts_ref, mass_ref):
        total = m_ref[...]
        num = own_ref[...] + PRIOR * cents_ref[...].astype(F32)
        for g in (g1, g2, g3):
            extra = g[256:272, 0:256].astype(F32)
            total = total + (extra[0:1] + extra[1:2] + extra[2:3])
            num = num + g[0:256, :].astype(F32)
        mass_ref[...] = total
        pts_ref[...] = (num / (as_column(total) + PRIOR)).astype(BF)

    return pl.pallas_call(
        kernel,
        grid_spec=pltpu.PrefetchScalarGridSpec(
            num_scalar_prefetch=1,
            grid=(1,),
            in_specs=[
                pl.BlockSpec((256, D), lambda i, s: (half, 0)),
                pl.BlockSpec((1, 256), lambda i, s: (0, half)),
            ]
            + [pl.BlockSpec((272, D), lambda i, s: (0, 0))] * 3
            + [pl.BlockSpec((256, D), lambda i, s: (s[0] * 2 + half, 0))],
            out_specs=[pl.BlockSpec((256, D), lambda i, s: (0, 0)), pl.BlockSpec((1, 256), lambda i, s: (0, 0))],
        ),
        out_shape=[shape((256, D), BF), shape((1, 256), F32)],
        name="finish_one",
    )(idx, own, own_mass, *got, cents)


def turn_points(owners, points, masses):
    def kernel(owners_ref, p0, p1, m0, m1, keep_ref, give_ref, tall):
        for h, p_ref in enumerate((p0, p1)):
            for at in range(0, D, 128):
                tall[pl.ds(at, 128), h * 256 : h * 256 + 256] = p_ref[:, pl.ds(at, 128)].astype(F32).T.astype(BF)
        packed = mass_rows(jnp.concatenate([m0[...], m1[...]], axis=1)).astype(BF)
        for r in range(8):
            ref = (keep_ref, give_ref)[r // 4]
            ref[r % 4, 0:96, :] = tall[pl.ds(pl.multiple_of(owners_ref[r] * 96, 32), 96), :]
            ref[r % 4, 96:112, :] = packed

    return pl.pallas_call(
        kernel,
        in_specs=[SMEM] + [VMEM] * 4,
        scratch_shapes=[pltpu.VMEM((D, 512), BF)],
        out_shape=[shape((4, 112, 512), BF)] * 2,
        name="turn_points",
    )(owners, *points, *masses)


def pair_pieces(keep, take):
    def kernel(k_ref, t_ref, *refs):
        for k, ref in enumerate(refs, 1):
            ref[0] = k_ref[k]
            ref[1] = t_ref[k]

    return pl.pallas_call(
        kernel, in_specs=[VMEM] * 2, out_shape=[shape((2, 112, 512), BF)] * 3, name="pair_pieces"
    )(keep, take)


def gather_one(sources, keep, take, pieces):
    def kernel(sources_ref, k_ref, t_ref, r1, r2, r3, o_ref, m_ref):
        for r in range(8):
            b, k = r // 4, r % 4
            piece = (r1, r2, r3)[k - 1].at[b] if k else (k_ref, t_ref)[b].at[0]
            block = sources_ref[r]
            o_ref[:, pl.ds(pl.multiple_of(block * 512, 512), 512)] = piece[0:96, :].astype(F32)
            t = piece[96:112, :].astype(F32)
            m_ref[pl.ds(block, 1), :] = t[0:1] + t[1:2] + t[2:3]

    return pl.pallas_call(
        kernel,
        in_specs=[SMEM] + [VMEM] * 5,
        out_shape=[shape((96, 4096), F32), shape((8, 512), F32)],
        name="gather_one",
    )(sources, keep, take, *pieces)


def join_two(a, b, rows):
    def kernel(a_ref, b_ref, o_ref, n_ref):
        if rows > 512:
            o_ref[512:rows, 512:D] = jnp.zeros((rows - 512, D - 512), BF)
        for at, ref in ((0, a_ref), (256, b_ref)):
            block = ref[...]
            n = square_norms(block)
            o_ref[at : at + 256, :] = block
            n_ref[at : at + 256, :] = jnp.broadcast_to(n, (256, 128))
            if rows > 512:
                o_ref[512:rows, at : at + 256] = mass_rows(as_row(n)).astype(BF)

    return pl.pallas_call(
        kernel,
        in_specs=[VMEM] * 2,
        out_shape=[shape((rows, D), BF), shape((512, 128), F32)],
        name="join_two",
    )(a, b)


def norms_of(block):
    def kernel(c_ref, n_ref):
        n_ref[...] = jnp.broadcast_to(square_norms(c_ref[...]), (512, 128))

    return pl.pallas_call(
        kernel, in_specs=[VMEM], out_shape=shape((512, 128), F32), name="norms_of"
    )(block)


def scores_two(places, own, theirs, two, norms, half, old=()):
    def kernel(places_ref, a_ref, b_ref, *refs):
        cents, ns = refs[0:4], (*refs[4:7], refs[-1])
        p_ref, stat_ref, scores, far_norms = refs[-4:]
        i = pl.program_id(0)

        @pl.when(i == 0)
        def _():
            row = cents[3][512:528, 0:512].astype(F32)
            row = row[0:1] + row[1:2] + row[2:3]
            far_norms[...] = jnp.broadcast_to(row, (128, 512)).T

        twice = jnp.where(i == 0, a_ref[...], b_ref[...]) * 2
        top = None
        for slot in range(8):
            here = pl.ds((slot % 2) * 256, 256)
            n = ns[slot // 2][here, :]
            s = nt(cents[slot // 2][here, :], twice) - jnp.concatenate([n, n], axis=1)
            scores[pl.ds(slot * 256, 256), :] = s
            t = fold_rows(s, jnp.maximum)
            top = t if top is None else jnp.maximum(top, t)
        m = jnp.max(top, axis=0, keepdims=True)
        total = None
        for slot in range(8):
            e = jnp.exp(scores[pl.ds(slot * 256, 256), :] - m)
            p_ref[pl.ds(pl.multiple_of(places_ref[slot] * 256, 256), 256), :] = e
            t = fold_rows(e, jnp.add)
            total = t if total is None else total + t

        @pl.when(i == 0)
        def _():
            stat_ref[...] = refs[8][...] if old else jnp.zeros_like(stat_ref)

        cols = pl.ds(pl.multiple_of((half * 2 + i) * 256, 256), 256)
        stat_ref[0:1, cols] = m
        stat_ref[1:2, cols] = jnp.sum(total, axis=0, keepdims=True)

    whole = lambda r, c: pl.BlockSpec((r, c), lambda i, s: (0, 0))
    return pl.pallas_call(
        kernel,
        grid_spec=pltpu.PrefetchScalarGridSpec(
            num_scalar_prefetch=1,
            grid=(2,),
            in_specs=[whole(256, D)] * 2 + [whole(t.shape[0], D) for t in two] + [whole(512, 128)] * 3
            + ([ANY, whole(2, 1024)] if old else []),
            out_specs=[pl.BlockSpec((2048, 256), lambda i, s: (0, half * 2 + i)), whole(2, 1024)],
            scratch_shapes=[pltpu.VMEM((2048, 256), F32), pltpu.VMEM((512, 128), F32)],
        ),
        out_shape=[shape((2048, 1024), F32), shape((2, 1024), F32)],
        input_output_aliases={10: 0} if old else {},
        name="scores_two",
    )(places, own, theirs, *two, *norms, *old)


def sums_two(p, stat, other, points):
    def kernel(p_ref, s_ref, r_ref, x0, x1, x2, x3, o_ref, rows, factor):
        @pl.when(pl.program_id(0) == 0)
        def _():
            for at, ref in zip(range(0, 1024, 256), (x0, x1, x2, x3)):
                rows[at : at + 256, :] = ref[...]
            theirs = jnp.concatenate([r_ref[:, at : at + 256] for at in (256, 0, 768, 512)], axis=1)
            mine = s_ref[...]
            m = jnp.maximum(mine[0:1], theirs[0:1])
            near = jnp.exp(mine[0:1] - m)
            total = mine[1:2] * near + theirs[1:2] * jnp.exp(theirs[0:1] - m)
            factor[0:1, :] = near / total

        w = (p_ref[...] * factor[0:1, :]).astype(BF)
        num = nn(w, rows[...])
        packed = mass_rows(as_row(lane_sums(w)))
        for q in range(32):
            for j in range(6):
                o_ref[q, j * 32 : j * 32 + 32, :] = num[q * 32 : q * 32 + 32, j * 128 : j * 128 + 128].astype(BF)
            lanes = packed[:, (q // 4) * 128 : (q // 4) * 128 + 128]
            turn = (128 - (q % 4) * 32) % 128
            o_ref[q, 192:TALL, :] = (pltpu.roll(lanes, turn, 1) if turn else lanes).astype(BF)

    whole = lambda r, c: pl.BlockSpec((r, c), lambda i: (0, 0))
    return pl.pallas_call(
        kernel,
        grid=(2,),
        in_specs=[pl.BlockSpec((1024, 1024), lambda i: (i, 0)), whole(2, 1024), whole(2, 1024)] + [whole(256, D)] * 4,
        out_specs=pl.BlockSpec((32, TALL, 128), lambda i: (i, 0, 0)),
        scratch_shapes=[pltpu.VMEM((1024, D), BF), pltpu.VMEM((8, 1024), F32)],
        out_shape=shape((64, TALL, 128), BF),
        name="sums_two",
    )(p, stat, other, *points)


def finish_two(total, cents):
    def kernel(x_ref, c_ref, o_ref):
        mass = x_ref[192:193, :] + x_ref[193:194, :] + x_ref[194:195, :]
        column = as_column(mass)[0:32] + PRIOR
        packed = mass_rows(mass).astype(BF)
        for j in range(6):
            num = x_ref[j * 32 : j * 32 + 32, :] + PRIOR * c_ref[:, j * 128 : j * 128 + 128].astype(F32)
            new = (num / column).astype(BF)
            for q in range(8):
                o_ref[q, j * 32 : j * 32 + 32, :] = new
        for q in range(8):
            o_ref[q, 192:TALL, :] = packed

    return pl.pallas_call(
        kernel, in_specs=[VMEM] * 2, out_shape=shape((8, TALL, 128), BF), name="finish_two"
    )(total, cents)


def gather_two(core, mine, theirs):
    def kernel(core_ref, a_ref, b_ref, o_ref, m_ref):
        lane = lax.broadcasted_iota(jnp.int32, (16, 128), 1)
        for ref, half in ((a_ref, core_ref[0]), (b_ref, 1 - core_ref[0])):
            start = pl.multiple_of(half * 256, 256)
            for q in range(8):
                for j in range(6):
                    o_ref[pl.ds(start + q * 32, 32), j * 128 : j * 128 + 128] = ref[q, j * 32 : j * 32 + 32, :].astype(F32)
            for g in range(2):
                row = None
                for r in range(4):
                    t = ref[g * 4 + r, 192:TALL, :].astype(F32)
                    t = pltpu.roll(t, r * 32, 1) if r else t
                    row = t if row is None else jnp.where(lane >= r * 32, t, row)
                m_ref[:, pl.ds(start + g * 128, 128)] = row[0:1] + row[1:2] + row[2:3]

    return pl.pallas_call(
        kernel,
        in_specs=[SMEM] + [VMEM] * 2,
        out_shape=[shape((512, D), F32), shape((1, 512), F32)],
        name="gather_two",
    )(core, mine, theirs)


def shift_y(x, k):
    return lax.ppermute(x, "y", [(i, (i + k) % 4) for i in range(4)])


def shift_z(x, k):
    return lax.ppermute(x, "z", [(i, (i + k) % 4) for i in range(4)])


def flip(x, axis):
    return lax.ppermute(x, axis, [(0, 1), (1, 0)])


def flip_x(x):
    return lax.ppermute(x, ("xh", "xl"), [(0, 3), (1, 2), (2, 1), (3, 0)])


def after(x, *others):
    return lax.optimization_barrier((x,) + others)[0]


def body(embeddings, cents_one, cents_two):
    y = lax.axis_index("y").astype(jnp.int32)
    xh = lax.axis_index("xh").astype(jnp.int32)
    z = lax.axis_index("z").astype(jnp.int32)
    xl = lax.axis_index("xl").astype(jnp.int32)
    c = lax.axis_index("c").astype(jnp.int32)
    halves = jnp.stack([xh * 2 + c, xh * 2 + 1 - c, 2 - xh * 2 + c, 3 - xh * 2 - c])
    idx = jnp.concatenate([xh * 4 + (y + jnp.arange(4, dtype=jnp.int32)) % 4, halves, jnp.stack([c, 1 - c])])
    slot = jnp.arange(8, dtype=jnp.int32)
    places = (y - slot) % 4 * 2 + (xh ^ (slot // 4))

    mine = lax.dynamic_slice_in_dim(embeddings, c * 512, 512, 0).astype(BF)
    far_mine = flip_x(mine)
    half_two = lax.dynamic_slice_in_dim(cents_two, c * 256, 256, 0)
    around = [shift_y(half_two, k) for k in (1, 2, 3)]

    p, x, near, norms = scores_near(idx, embeddings, cents_one)
    near_a, norms_a = join_two(after(half_two, near), around[0], 512)
    far_mine = after(far_mine, near, norms_a, around[2])
    far_other = flip(far_mine, "c")
    far_a = flip_x(after(near_a, far_mine))
    p, x, local = scores_far(idx, far_mine, far_other, cents_one, norms, near, p, x)

    spread = merge_cores(local, flip(local, "c"))
    stats = lax.all_to_all(spread, ("xh", "z", "xl"), 0, 0, tiled=True)
    near_b, norms_b = join_two(after(around[1], spread), around[2], 528)
    norms_c = norms_of(after(far_a, spread))
    factor = merge_last(idx, stats, after(local, norms_b, norms_c))

    parts_0 = sums_far(p, factor, x, 0)
    got_0 = [shift_y(part, k) for part, k in zip(parts_0, (2, 1, 3))]
    far_b = flip_x(after(near_b, parts_0[0]))
    *parts_1, own, own_mass = sums_rest(p, after(factor, parts_0[0]), x)
    got_1 = [shift_y(part, k) for part, k in zip(parts_1, (2, 1, 3))]
    two = (near_a, near_b, far_a, far_b)
    norms_two = (norms_a, norms_b, norms_c)

    points_0, mass_0 = finish_one(idx, own, own_mass, got_0, cents_one, 0)
    theirs_0 = flip(points_0, "c")
    old = scores_two(places, points_0, theirs_0, two, norms_two, 0)
    points_1, mass_1 = finish_one(idx, own, after(own_mass, old[1]), got_1, cents_one, 1)
    theirs_1 = flip(points_1, "c")
    owners = (y + slot) % 4 * 2 + (xh ^ (slot // 4))
    sources = (y - slot) % 4 + (xh ^ (slot // 4)) * 4
    keep, give = turn_points(owners, (points_0, points_1), (mass_0, mass_1))
    take = flip(give, "xh")

    p2, stat2 = scores_two(places, after(points_1, give), theirs_1, two, norms_two, 1, tuple(old))
    packed = sums_two(p2, stat2, flip(stat2, "c"), (points_0, theirs_0, points_1, theirs_1))
    packed = after(packed, take)
    parts = lax.all_to_all(packed, ("y", "xh", "z", "xl"), 0, 0, tiled=True)
    pairs = pair_pieces(after(keep, packed), take)
    pieces = [shift_y(t, k) for t, k in zip(pairs, (1, 2, 3))]
    turned_one, mass_one = gather_one(sources, keep, take, pieces)
    total = jnp.sum(after(parts, pairs[0]).astype(F32), axis=0)
    rows = lax.dynamic_slice_in_dim(cents_two, c * 256 + z * 64 + xl * 32, 32, 0)
    spread = finish_two(total, after(rows, *pieces))
    block = after(lax.all_to_all(spread, ("z", "xl"), 0, 0, tiled=True), turned_one)
    updated_two, mass_two = gather_two(c[None], block, flip(block, "c"))
    return turned_one.T, mass_one.reshape(4096), updated_two, mass_two.reshape(512)


def solution(mesh):
    fine = Mesh(mesh.devices.reshape(4, 2, 4, 2, 2), ("y", "xh", "z", "xl", "c"))
    dp, cent = ("y", "xh"), ("z", "xl", "c")
    return jax.shard_map(
        body,
        mesh=fine,
        in_specs=(P(dp, None), P(cent, None), P(dp, None)),
        out_specs=(P(cent, dp), P(cent), P(dp, None), P(dp)),
        check_vma=False,
    )
```

```python
import jax
import jax.numpy as jnp
from jax import lax
from jax.experimental import pallas as pl
from jax.experimental.pallas import tpu as pltpu
from jax.sharding import Mesh, PartitionSpec as P

PRIOR = 0.5
BF = jnp.bfloat16
F32 = jnp.float32
D = 768
TALL = 208
SMEM = pl.BlockSpec(memory_space=pltpu.SMEM)
VMEM = pl.BlockSpec(memory_space=pltpu.VMEM)


def nt(left, right):
    return lax.dot_general(left, right, (((1,), (1,)), ((), ())), preferred_element_type=F32)


def nn(left, right):
    return lax.dot_general(left, right, (((1,), (0,)), ((), ())), preferred_element_type=F32)


def shape(dims, dtype):
    return jax.ShapeDtypeStruct(dims, dtype)


def square_norms(block):
    wide = block.astype(F32)
    return jnp.sum(wide * wide, axis=1, keepdims=True)


def fold_rows(block, op):
    parts = [block[i : i + 8] for i in range(0, block.shape[0], 8)]
    while len(parts) > 1:
        parts = [op(parts[i], parts[i + 1]) for i in range(0, len(parts) - 1, 2)] + (
            [parts[-1]] if len(parts) % 2 else []
        )
    return parts[0]


def lane_sums(w):
    wide = w.astype(F32)
    part = wide[:, 0:128]
    for j in range(128, wide.shape[1], 128):
        part = part + wide[:, j : j + 128]
    return jnp.sum(part, axis=1, keepdims=True)


def as_row(column):
    return jnp.broadcast_to(column, (column.shape[0], 128)).T[0:1, :]


def as_column(row):
    return jnp.broadcast_to(row, (128, row.shape[1])).T[:, 0:1]


def mass_rows(row):
    t = jnp.broadcast_to(row, (16, row.shape[1]))
    hi = t.astype(BF).astype(F32)
    mid = (t - hi).astype(BF).astype(F32)
    low = t - hi - mid
    at = lax.broadcasted_iota(jnp.int32, t.shape, 0)
    return jnp.where(at == 0, hi, jnp.where(at == 1, mid, jnp.where(at == 2, low, 0.0)))


def scores_step(cents, twice, norms, p_ref, scores):
    top = None
    for k in range(4):
        for h in range(2):
            at = k * 512 + h * 256
            n = norms[pl.ds(at, 256), :]
            s = nt(cents[k][pl.ds(h * 256, 256), :], twice) - jnp.concatenate([n, n], axis=1)
            scores[pl.ds(at, 256), :] = s
            t = fold_rows(s, jnp.maximum)
            top = t if top is None else jnp.maximum(top, t)
    m = jnp.max(top, axis=0, keepdims=True)
    total = None
    for at in range(0, 2048, 256):
        e = jnp.exp(scores[pl.ds(at, 256), :] - m)
        p_ref[pl.ds(at, 256), :] = e
        t = fold_rows(e, jnp.add)
        total = t if total is None else total + t
    return m, jnp.sum(total, axis=0, keepdims=True)


def put_stats(stat_ref, row, i, m, l):
    cols = pl.ds(pl.multiple_of(lax.rem(i, 2) * 256, 256), 256)
    stat_ref[pl.ds(row, 1), cols] = m
    stat_ref[pl.ds(4 + row, 1), cols] = l


def scores_near_kernel(idx, e_ref, c0, c1, c2, c3, p_ref, x_ref, stat_ref, norms_ref, scores):
    i = pl.program_id(0)
    cents = (c0, c1, c2, c3)

    @pl.when(i == 0)
    def _():
        stat_ref[...] = jnp.zeros_like(stat_ref)
        for k in range(4):
            for h in range(2):
                n = square_norms(cents[k][pl.ds(h * 256, 256), :])
                norms_ref[pl.ds(k * 512 + h * 256, 256), :] = jnp.broadcast_to(n, (256, 128))

    x = e_ref[...].astype(BF)
    x_ref[...] = x
    m, l = scores_step(cents, x * 2, norms_ref, p_ref, scores)
    put_stats(stat_ref, idx[4 + i // 2], i, m, l)


def scores_far_kernel(idx, a_ref, b_ref, c0, c1, c2, c3, norms_ref, near_ref, p_old, x_old, p_ref, x_ref, stat_ref, scores):
    i = pl.program_id(0)

    @pl.when(i == 0)
    def _():
        stat_ref[...] = near_ref[...]

    x = jnp.where(i < 2, a_ref[...], b_ref[...])
    x_ref[...] = x
    m, l = scores_step((c0, c1, c2, c3), x * 2, norms_ref, p_ref, scores)
    put_stats(stat_ref, idx[6 + i // 2], i, m, l)


ANY = pl.BlockSpec(memory_space=pl.ANY)
ROW_IN = [
    pl.BlockSpec((256, D), lambda i, s: (jnp.minimum(i, 1), 0)),
    pl.BlockSpec((256, D), lambda i, s: (jnp.maximum(i - 2, 0), 0)),
]
CENTS_IN = [pl.BlockSpec((512, D), lambda i, s, k=k: (s[k], 0)) for k in range(4)]
WHOLE_STAT = pl.BlockSpec((8, 512), lambda i, s: (0, 0))
WHOLE_NORMS = pl.BlockSpec((2048, 128), lambda i, s: (0, 0))


def scores_near(idx, embeddings, cents):
    return pl.pallas_call(
        scores_near_kernel,
        grid_spec=pltpu.PrefetchScalarGridSpec(
            num_scalar_prefetch=1,
            grid=(4,),
            in_specs=[pl.BlockSpec((256, D), lambda i, s: (s[8 + i // 2] * 2 + i % 2, 0))] + CENTS_IN,
            out_specs=[
                pl.BlockSpec((2048, 256), lambda i, s: (0, i)),
                pl.BlockSpec((256, D), lambda i, s: (i, 0)),
                WHOLE_STAT,
                WHOLE_NORMS,
            ],
            scratch_shapes=[pltpu.VMEM((2048, 256), F32)],
        ),
        out_shape=[
            shape((2048, 2048), F32),
            shape((2048, D), BF),
            shape((8, 512), F32),
            shape((2048, 128), F32),
        ],
        cost_estimate=pl.CostEstimate(
            flops=2 * 2048 * 1024 * D, transcendentals=2048 * 1024, bytes_accessed=24 << 20
        ),
        name="scores_near",
    )(idx, embeddings, cents, cents, cents, cents)


def scores_far(idx, a, b, cents, norms, near, p, x):
    return pl.pallas_call(
        scores_far_kernel,
        grid_spec=pltpu.PrefetchScalarGridSpec(
            num_scalar_prefetch=1,
            grid=(4,),
            in_specs=ROW_IN + CENTS_IN + [WHOLE_NORMS, WHOLE_STAT, ANY, ANY],
            out_specs=[
                pl.BlockSpec((2048, 256), lambda i, s: (0, 4 + i)),
                pl.BlockSpec((256, D), lambda i, s: (4 + i, 0)),
                WHOLE_STAT,
            ],
            scratch_shapes=[pltpu.VMEM((2048, 256), F32)],
        ),
        out_shape=[shape((2048, 2048), F32), shape((2048, D), BF), shape((8, 512), F32)],
        input_output_aliases={9: 0, 10: 1},
        name="scores_far",
    )(idx, a, b, cents, cents, cents, cents, norms, near, p, x)


def merge_all(stats):
    m = stats[0][0:4]
    for t in stats[1:]:
        m = jnp.maximum(m, t[0:4])
    total = None
    for t in stats:
        part = t[4:8] * jnp.exp(t[0:4] - m)
        total = part if total is None else total + part
    return m, total


def merge_cores(local, other):
    def kernel(a, b, o_ref):
        m, total = merge_all([a[...], b[...]])
        both = jnp.concatenate([m, total], axis=0)
        for i in range(16):
            o_ref[i] = both

    return pl.pallas_call(
        kernel, in_specs=[VMEM] * 2, out_shape=shape((16, 8, 512), F32), name="merge_cores"
    )(local, other)


def merge_last(idx, stats, local):
    def kernel(idx_ref, s_ref, l_ref, f_ref, tmp):
        m, total = merge_all([s_ref[i] for i in range(16)])
        tmp[0:4, :] = jnp.exp(l_ref[0:4, :] - m) / total
        for r in range(4):
            f_ref[:, r * 512 : (r + 1) * 512] = tmp[pl.ds(idx_ref[4 + r], 1), :]

    return pl.pallas_call(
        kernel,
        in_specs=[SMEM] + [VMEM] * 2,
        scratch_shapes=[pltpu.VMEM((8, 512), F32)],
        out_shape=shape((1, 2048), F32),
        name="merge_last",
    )(idx, stats, local)


def sums_far(p, factor, x, blocks, half):
    first, step = blocks[0], blocks[-1] - blocks[0]

    def kernel(p_ref, f_ref, x_ref, *refs):
        w = (p_ref[...] * f_ref[...]).astype(BF)
        sums = nn(w, x_ref[...]).astype(BF)
        packed = mass_rows(as_row(lane_sums(w))).astype(BF)
        for q in range(len(blocks)):

            @pl.when(pl.program_id(0) == q)
            def _(q=q):
                refs[q][0:256, :] = sums
                refs[q][256:272, 0:256] = packed
                refs[q][256:272, 256:D] = jnp.zeros((16, D - 256), BF)

    return pl.pallas_call(
        kernel,
        grid=(len(blocks),),
        in_specs=[
            pl.BlockSpec((256, 2048), lambda j: ((first + step * j) * 2 + half, 0)),
            pl.BlockSpec((1, 2048), lambda j: (0, 0)),
            pl.BlockSpec((2048, D), lambda j: (0, 0)),
        ],
        out_specs=[pl.BlockSpec((272, D), lambda j: (0, 0)) for k in blocks],
        out_shape=[shape((272, D), BF) for k in blocks],
        name="sums_far",
    )(p, factor, x)


def sums_rest(p, factor, x):
    def kernel(p_ref, f_ref, x_ref, g2, g1, g3, own_ref, m_ref):
        w = (p_ref[...] * f_ref[...]).astype(BF)
        sums = nn(w, x_ref[...])
        mass = as_row(lane_sums(w))
        j = pl.program_id(0)
        for q, ref in enumerate((g2, g1, g3)):

            @pl.when(j == q)
            def _(ref=ref):
                ref[0:256, :] = sums.astype(BF)
                ref[256:272, 0:256] = mass_rows(mass).astype(BF)
                ref[256:272, 256:D] = jnp.zeros((16, D - 256), BF)

        @pl.when(j >= 3)
        def _():
            own_ref[...] = sums
            m_ref[...] = mass

    return pl.pallas_call(
        kernel,
        grid=(5,),
        in_specs=[
            pl.BlockSpec((256, 2048), lambda j: (jnp.where(j < 3, (2 - j + 3 * (j // 2)) * 2 + 1, j - 3), 0)),
            pl.BlockSpec((1, 2048), lambda j: (0, 0)),
            pl.BlockSpec((2048, D), lambda j: (0, 0)),
        ],
        out_specs=[pl.BlockSpec((272, D), lambda j: (0, 0))] * 3
        + [
            pl.BlockSpec((256, D), lambda j: (jnp.maximum(j - 3, 0), 0)),
            pl.BlockSpec((1, 256), lambda j: (0, jnp.maximum(j - 3, 0))),
        ],
        out_shape=[shape((272, D), BF)] * 3 + [shape((512, D), F32), shape((1, 512), F32)],
        name="sums_rest",
    )(p, factor, x)


def finish_one(idx, own, own_mass, got, cents, half):
    def kernel(idx_ref, own_ref, m_ref, g1, g2, g3, cents_ref, pts_ref, mass_ref):
        total = m_ref[...]
        num = own_ref[...] + PRIOR * cents_ref[...].astype(F32)
        for g in (g1, g2, g3):
            extra = g[256:272, 0:256].astype(F32)
            total = total + (extra[0:1] + extra[1:2] + extra[2:3])
            num = num + g[0:256, :].astype(F32)
        mass_ref[...] = total
        pts_ref[...] = (num / (as_column(total) + PRIOR)).astype(BF)

    return pl.pallas_call(
        kernel,
        grid_spec=pltpu.PrefetchScalarGridSpec(
            num_scalar_prefetch=1,
            grid=(1,),
            in_specs=[
                pl.BlockSpec((256, D), lambda i, s: (half, 0)),
                pl.BlockSpec((1, 256), lambda i, s: (0, half)),
            ]
            + [pl.BlockSpec((272, D), lambda i, s: (0, 0))] * 3
            + [pl.BlockSpec((256, D), lambda i, s: (s[0] * 2 + half, 0))],
            out_specs=[pl.BlockSpec((256, D), lambda i, s: (0, 0)), pl.BlockSpec((1, 256), lambda i, s: (0, 0))],
        ),
        out_shape=[shape((256, D), BF), shape((1, 256), F32)],
        name="finish_one",
    )(idx, own, own_mass, *got, cents)


def turn_points(owners, points, masses):
    def kernel(owners_ref, p0, p1, m0, m1, keep_ref, give_ref, tall):
        for h, p_ref in enumerate((p0, p1)):
            for at in range(0, D, 128):
                tall[pl.ds(at, 128), h * 256 : h * 256 + 256] = p_ref[:, pl.ds(at, 128)].astype(F32).T.astype(BF)
        packed = mass_rows(jnp.concatenate([m0[...], m1[...]], axis=1)).astype(BF)
        for r in range(8):
            ref = (keep_ref, give_ref)[r // 4]
            ref[r % 4, 0:96, :] = tall[pl.ds(pl.multiple_of(owners_ref[r] * 96, 32), 96), :]
            ref[r % 4, 96:112, :] = packed

    return pl.pallas_call(
        kernel,
        in_specs=[SMEM] + [VMEM] * 4,
        scratch_shapes=[pltpu.VMEM((D, 512), BF)],
        out_shape=[shape((4, 112, 512), BF)] * 2,
        name="turn_points",
    )(owners, *points, *masses)


def pair_pieces(keep, take):
    def kernel(k_ref, t_ref, *refs):
        for k, ref in enumerate(refs, 1):
            ref[0] = k_ref[k]
            ref[1] = t_ref[k]

    return pl.pallas_call(
        kernel, in_specs=[VMEM] * 2, out_shape=[shape((2, 112, 512), BF)] * 3, name="pair_pieces"
    )(keep, take)


def gather_one(sources, keep, take, pieces):
    def kernel(sources_ref, k_ref, t_ref, r1, r2, r3, o_ref, m_ref):
        for r in range(8):
            b, k = r // 4, r % 4
            piece = (r1, r2, r3)[k - 1].at[b] if k else (k_ref, t_ref)[b].at[0]
            block = sources_ref[r]
            o_ref[:, pl.ds(pl.multiple_of(block * 512, 512), 512)] = piece[0:96, :].astype(F32)
            t = piece[96:112, :].astype(F32)
            m_ref[pl.ds(block, 1), :] = t[0:1] + t[1:2] + t[2:3]

    return pl.pallas_call(
        kernel,
        in_specs=[SMEM] + [VMEM] * 5,
        out_shape=[shape((96, 4096), F32), shape((8, 512), F32)],
        name="gather_one",
    )(sources, keep, take, *pieces)


def join_two(a, b, rows):
    def kernel(a_ref, b_ref, o_ref, n_ref):
        if rows > 512:
            o_ref[512:rows, 512:D] = jnp.zeros((rows - 512, D - 512), BF)
        for at, ref in ((0, a_ref), (256, b_ref)):
            block = ref[...]
            n = square_norms(block)
            o_ref[at : at + 256, :] = block
            n_ref[at : at + 256, :] = jnp.broadcast_to(n, (256, 128))
            if rows > 512:
                o_ref[512:rows, at : at + 256] = mass_rows(as_row(n)).astype(BF)

    return pl.pallas_call(
        kernel,
        in_specs=[VMEM] * 2,
        out_shape=[shape((rows, D), BF), shape((512, 128), F32)],
        name="join_two",
    )(a, b)


def norms_of(block):
    def kernel(c_ref, n_ref):
        n_ref[...] = jnp.broadcast_to(square_norms(c_ref[...]), (512, 128))

    return pl.pallas_call(
        kernel, in_specs=[VMEM], out_shape=shape((512, 128), F32), name="norms_of"
    )(block)


def scores_two(places, own, theirs, two, norms, half, old=()):
    def kernel(places_ref, a_ref, b_ref, *refs):
        cents, ns = refs[0:4], (*refs[4:7], refs[-1])
        p_ref, stat_ref, scores, far_norms = refs[-4:]
        i = pl.program_id(0)

        @pl.when(i == 0)
        def _():
            row = cents[3][512:528, 0:512].astype(F32)
            row = row[0:1] + row[1:2] + row[2:3]
            far_norms[...] = jnp.broadcast_to(row, (128, 512)).T

        twice = jnp.where(i == 0, a_ref[...], b_ref[...]) * 2
        top = None
        for slot in range(8):
            here = pl.ds((slot % 2) * 256, 256)
            n = ns[slot // 2][here, :]
            s = nt(cents[slot // 2][here, :], twice) - jnp.concatenate([n, n], axis=1)
            scores[pl.ds(slot * 256, 256), :] = s
            t = fold_rows(s, jnp.maximum)
            top = t if top is None else jnp.maximum(top, t)
        m = jnp.max(top, axis=0, keepdims=True)
        total = None
        for slot in range(8):
            e = jnp.exp(scores[pl.ds(slot * 256, 256), :] - m)
            p_ref[pl.ds(pl.multiple_of(places_ref[slot] * 256, 256), 256), :] = e
            t = fold_rows(e, jnp.add)
            total = t if total is None else total + t

        @pl.when(i == 0)
        def _():
            stat_ref[...] = refs[8][...] if old else jnp.zeros_like(stat_ref)

        cols = pl.ds(pl.multiple_of((half * 2 + i) * 256, 256), 256)
        stat_ref[0:1, cols] = m
        stat_ref[1:2, cols] = jnp.sum(total, axis=0, keepdims=True)

    whole = lambda r, c: pl.BlockSpec((r, c), lambda i, s: (0, 0))
    return pl.pallas_call(
        kernel,
        grid_spec=pltpu.PrefetchScalarGridSpec(
            num_scalar_prefetch=1,
            grid=(2,),
            in_specs=[whole(256, D)] * 2 + [whole(t.shape[0], D) for t in two] + [whole(512, 128)] * 3
            + ([ANY, whole(2, 1024)] if old else []),
            out_specs=[pl.BlockSpec((2048, 256), lambda i, s: (0, half * 2 + i)), whole(2, 1024)],
            scratch_shapes=[pltpu.VMEM((2048, 256), F32), pltpu.VMEM((512, 128), F32)],
        ),
        out_shape=[shape((2048, 1024), F32), shape((2, 1024), F32)],
        input_output_aliases={10: 0} if old else {},
        name="scores_two",
    )(places, own, theirs, *two, *norms, *old)


def sums_two(p, stat, other, points):
    def kernel(p_ref, s_ref, r_ref, x0, x1, x2, x3, o_ref, rows, factor):
        @pl.when(pl.program_id(0) == 0)
        def _():
            for at, ref in zip(range(0, 1024, 256), (x0, x1, x2, x3)):
                rows[at : at + 256, :] = ref[...]
            theirs = jnp.concatenate([r_ref[:, at : at + 256] for at in (256, 0, 768, 512)], axis=1)
            mine = s_ref[...]
            m = jnp.maximum(mine[0:1], theirs[0:1])
            near = jnp.exp(mine[0:1] - m)
            total = mine[1:2] * near + theirs[1:2] * jnp.exp(theirs[0:1] - m)
            factor[0:1, :] = near / total

        w = (p_ref[...] * factor[0:1, :]).astype(BF)
        num = nn(w, rows[...])
        packed = mass_rows(as_row(lane_sums(w)))
        for q in range(32):
            for j in range(6):
                o_ref[q, j * 32 : j * 32 + 32, :] = num[q * 32 : q * 32 + 32, j * 128 : j * 128 + 128].astype(BF)
            lanes = packed[:, (q // 4) * 128 : (q // 4) * 128 + 128]
            turn = (128 - (q % 4) * 32) % 128
            o_ref[q, 192:TALL, :] = (pltpu.roll(lanes, turn, 1) if turn else lanes).astype(BF)

    whole = lambda r, c: pl.BlockSpec((r, c), lambda i: (0, 0))
    return pl.pallas_call(
        kernel,
        grid=(2,),
        in_specs=[pl.BlockSpec((1024, 1024), lambda i: (i, 0)), whole(2, 1024), whole(2, 1024)] + [whole(256, D)] * 4,
        out_specs=pl.BlockSpec((32, TALL, 128), lambda i: (i, 0, 0)),
        scratch_shapes=[pltpu.VMEM((1024, D), BF), pltpu.VMEM((8, 1024), F32)],
        out_shape=shape((64, TALL, 128), BF),
        name="sums_two",
    )(p, stat, other, *points)


def finish_two(total, cents):
    def kernel(x_ref, c_ref, o_ref):
        mass = x_ref[192:193, :] + x_ref[193:194, :] + x_ref[194:195, :]
        column = as_column(mass)[0:32] + PRIOR
        packed = mass_rows(mass).astype(BF)
        for j in range(6):
            num = x_ref[j * 32 : j * 32 + 32, :] + PRIOR * c_ref[:, j * 128 : j * 128 + 128].astype(F32)
            new = (num / column).astype(BF)
            for q in range(8):
                o_ref[q, j * 32 : j * 32 + 32, :] = new
        for q in range(8):
            o_ref[q, 192:TALL, :] = packed

    return pl.pallas_call(
        kernel, in_specs=[VMEM] * 2, out_shape=shape((8, TALL, 128), BF), name="finish_two"
    )(total, cents)


def gather_two(core, mine, theirs):
    def kernel(core_ref, a_ref, b_ref, o_ref, m_ref):
        lane = lax.broadcasted_iota(jnp.int32, (16, 128), 1)
        for ref, half in ((a_ref, core_ref[0]), (b_ref, 1 - core_ref[0])):
            start = pl.multiple_of(half * 256, 256)
            for q in range(8):
                for j in range(6):
                    o_ref[pl.ds(start + q * 32, 32), j * 128 : j * 128 + 128] = ref[q, j * 32 : j * 32 + 32, :].astype(F32)
            for g in range(2):
                row = None
                for r in range(4):
                    t = ref[g * 4 + r, 192:TALL, :].astype(F32)
                    t = pltpu.roll(t, r * 32, 1) if r else t
                    row = t if row is None else jnp.where(lane >= r * 32, t, row)
                m_ref[:, pl.ds(start + g * 128, 128)] = row[0:1] + row[1:2] + row[2:3]

    return pl.pallas_call(
        kernel,
        in_specs=[SMEM] + [VMEM] * 2,
        out_shape=[shape((512, D), F32), shape((1, 512), F32)],
        name="gather_two",
    )(core, mine, theirs)


def shift_y(x, k):
    return lax.ppermute(x, "y", [(i, (i + k) % 4) for i in range(4)])


def shift_z(x, k):
    return lax.ppermute(x, "z", [(i, (i + k) % 4) for i in range(4)])


def flip(x, axis):
    return lax.ppermute(x, axis, [(0, 1), (1, 0)])


def flip_x(x):
    return lax.ppermute(x, ("xh", "xl"), [(0, 3), (1, 2), (2, 1), (3, 0)])


def after(x, *others):
    return lax.optimization_barrier((x,) + others)[0]


def body(embeddings, cents_one, cents_two):
    y = lax.axis_index("y").astype(jnp.int32)
    xh = lax.axis_index("xh").astype(jnp.int32)
    z = lax.axis_index("z").astype(jnp.int32)
    xl = lax.axis_index("xl").astype(jnp.int32)
    c = lax.axis_index("c").astype(jnp.int32)
    halves = jnp.stack([xh * 2 + c, xh * 2 + 1 - c, 2 - xh * 2 + c, 3 - xh * 2 - c])
    idx = jnp.concatenate([xh * 4 + (y + jnp.arange(4, dtype=jnp.int32)) % 4, halves, jnp.stack([c, 1 - c])])
    slot = jnp.arange(8, dtype=jnp.int32)
    places = (y - slot) % 4 * 2 + (xh ^ (slot // 4))

    mine = lax.dynamic_slice_in_dim(embeddings, c * 512, 512, 0).astype(BF)
    far_mine = flip_x(mine)
    half_two = lax.dynamic_slice_in_dim(cents_two, c * 256, 256, 0)
    around = [shift_y(half_two, k) for k in (1, 2, 3)]

    p, x, near, norms = scores_near(idx, embeddings, cents_one)
    near_a, norms_a = join_two(after(half_two, near), around[0], 512)
    far_mine = after(far_mine, near, norms_a, around[2])
    far_other = flip(far_mine, "c")
    far_a = flip_x(after(near_a, far_mine))
    p, x, local = scores_far(idx, far_mine, far_other, cents_one, norms, near, p, x)

    spread = merge_cores(local, flip(local, "c"))
    stats = lax.all_to_all(spread, ("xh", "z", "xl"), 0, 0, tiled=True)
    near_b, norms_b = join_two(after(around[1], spread), around[2], 528)
    norms_c = norms_of(after(far_a, spread))
    factor = merge_last(idx, stats, after(local, norms_b, norms_c))

    parts_0 = sums_far(p, factor, x, (2,), 0)
    parts_0 += sums_far(p, after(factor, parts_0[0]), x, (1, 3), 0)
    got_0 = [shift_y(part, k) for part, k in zip(parts_0, (2, 1, 3))]
    far_b = flip_x(after(near_b, parts_0[1]))
    *parts_1, own, own_mass = sums_rest(p, after(factor, parts_0[1]), x)
    got_1 = [shift_y(part, k) for part, k in zip(parts_1, (2, 1, 3))]
    two = (near_a, near_b, far_a, far_b)
    norms_two = (norms_a, norms_b, norms_c)

    points_0, mass_0 = finish_one(idx, own, own_mass, got_0, cents_one, 0)
    theirs_0 = flip(points_0, "c")
    old = scores_two(places, points_0, theirs_0, two, norms_two, 0)
    points_1, mass_1 = finish_one(idx, own, after(own_mass, old[1]), got_1, cents_one, 1)
    theirs_1 = flip(points_1, "c")
    owners = (y + slot) % 4 * 2 + (xh ^ (slot // 4))
    sources = (y - slot) % 4 + (xh ^ (slot // 4)) * 4
    keep, give = turn_points(owners, (points_0, points_1), (mass_0, mass_1))
    take = flip(give, "xh")

    p2, stat2 = scores_two(places, after(points_1, give), theirs_1, two, norms_two, 1, tuple(old))
    packed = sums_two(p2, stat2, flip(stat2, "c"), (points_0, theirs_0, points_1, theirs_1))
    packed = after(packed, take)
    parts = lax.all_to_all(packed, ("y", "xh", "z", "xl"), 0, 0, tiled=True)
    pairs = pair_pieces(after(keep, packed), take)
    total = jnp.sum(after(parts, pairs[0]).astype(F32), axis=0)
    rows = lax.dynamic_slice_in_dim(cents_two, c * 256 + z * 64 + xl * 32, 32, 0)
    spread = finish_two(total, rows)
    pieces = [shift_y(after(t, spread), k) for t, k in zip(pairs, (1, 2, 3))]
    turned_one, mass_one = gather_one(sources, keep, take, pieces)
    block = after(lax.all_to_all(spread, ("z", "xl"), 0, 0, tiled=True), *pieces)
    updated_two, mass_two = gather_two(c[None], block, flip(block, "c"))
    return turned_one.T, mass_one.reshape(4096), updated_two, mass_two.reshape(512)


def solution(mesh):
    fine = Mesh(mesh.devices.reshape(4, 2, 4, 2, 2), ("y", "xh", "z", "xl", "c"))
    dp, cent = ("y", "xh"), ("z", "xl", "c")
    return jax.shard_map(
        body,
        mesh=fine,
        in_specs=(P(dp, None), P(cent, None), P(dp, None)),
        out_specs=(P(cent, dp), P(cent), P(dp, None), P(dp)),
        check_vma=False,
    )
```

```python
import jax
import jax.numpy as jnp
from jax import lax
from jax.experimental import pallas as pl
from jax.experimental.pallas import tpu as pltpu
from jax.sharding import Mesh, PartitionSpec as P

PRIOR = 0.5
BF = jnp.bfloat16
F32 = jnp.float32
D = 768
TALL = 208
SMEM = pl.BlockSpec(memory_space=pltpu.SMEM)
VMEM = pl.BlockSpec(memory_space=pltpu.VMEM)


def nt(left, right):
    return lax.dot_general(left, right, (((1,), (1,)), ((), ())), preferred_element_type=F32)


def nn(left, right):
    return lax.dot_general(left, right, (((1,), (0,)), ((), ())), preferred_element_type=F32)


def shape(dims, dtype):
    return jax.ShapeDtypeStruct(dims, dtype)


def square_norms(block):
    wide = block.astype(F32)
    return jnp.sum(wide * wide, axis=1, keepdims=True)


def fold_rows(block, op):
    parts = [block[i : i + 8] for i in range(0, block.shape[0], 8)]
    while len(parts) > 1:
        parts = [op(parts[i], parts[i + 1]) for i in range(0, len(parts) - 1, 2)] + (
            [parts[-1]] if len(parts) % 2 else []
        )
    return parts[0]


def lane_sums(w):
    wide = w.astype(F32)
    part = wide[:, 0:128]
    for j in range(128, wide.shape[1], 128):
        part = part + wide[:, j : j + 128]
    return jnp.sum(part, axis=1, keepdims=True)


def as_row(column):
    return jnp.broadcast_to(column, (column.shape[0], 128)).T[0:1, :]


def as_column(row):
    return jnp.broadcast_to(row, (128, row.shape[1])).T[:, 0:1]


def mass_rows(row):
    t = jnp.broadcast_to(row, (16, row.shape[1]))
    hi = t.astype(BF).astype(F32)
    mid = (t - hi).astype(BF).astype(F32)
    low = t - hi - mid
    at = lax.broadcasted_iota(jnp.int32, t.shape, 0)
    return jnp.where(at == 0, hi, jnp.where(at == 1, mid, jnp.where(at == 2, low, 0.0)))


def scores_step(cents, twice, norms, p_ref, scores):
    top = None
    for k in range(4):
        for h in range(2):
            at = k * 512 + h * 256
            n = norms[pl.ds(at, 256), :]
            s = nt(cents[k][pl.ds(h * 256, 256), :], twice) - jnp.concatenate([n, n], axis=1)
            scores[pl.ds(at, 256), :] = s
            t = fold_rows(s, jnp.maximum)
            top = t if top is None else jnp.maximum(top, t)
    m = jnp.max(top, axis=0, keepdims=True)
    total = None
    for at in range(0, 2048, 256):
        e = jnp.exp(scores[pl.ds(at, 256), :] - m)
        p_ref[pl.ds(at, 256), :] = e
        t = fold_rows(e, jnp.add)
        total = t if total is None else total + t
    return m, jnp.sum(total, axis=0, keepdims=True)


def put_stats(stat_ref, row, i, m, l):
    cols = pl.ds(pl.multiple_of(lax.rem(i, 2) * 256, 256), 256)
    stat_ref[pl.ds(row, 1), cols] = m
    stat_ref[pl.ds(4 + row, 1), cols] = l


def scores_near_kernel(idx, e_ref, c0, c1, c2, c3, p_ref, x_ref, stat_ref, norms_ref, scores):
    i = pl.program_id(0)
    cents = (c0, c1, c2, c3)

    @pl.when(i == 0)
    def _():
        stat_ref[...] = jnp.zeros_like(stat_ref)
        for k in range(4):
            for h in range(2):
                n = square_norms(cents[k][pl.ds(h * 256, 256), :])
                norms_ref[pl.ds(k * 512 + h * 256, 256), :] = jnp.broadcast_to(n, (256, 128))

    x = e_ref[...].astype(BF)
    x_ref[...] = x
    m, l = scores_step(cents, x * 2, norms_ref, p_ref, scores)
    put_stats(stat_ref, idx[4 + i // 2], i, m, l)


def scores_far_kernel(idx, a_ref, b_ref, c0, c1, c2, c3, norms_ref, near_ref, p_old, x_old, p_ref, x_ref, stat_ref, scores):
    i = pl.program_id(0)

    @pl.when(i == 0)
    def _():
        stat_ref[...] = near_ref[...]

    x = jnp.where(i < 2, a_ref[...], b_ref[...])
    x_ref[...] = x
    m, l = scores_step((c0, c1, c2, c3), x * 2, norms_ref, p_ref, scores)
    put_stats(stat_ref, idx[6 + i // 2], i, m, l)


ANY = pl.BlockSpec(memory_space=pl.ANY)
ROW_IN = [
    pl.BlockSpec((256, D), lambda i, s: (jnp.minimum(i, 1), 0)),
    pl.BlockSpec((256, D), lambda i, s: (jnp.maximum(i - 2, 0), 0)),
]
CENTS_IN = [pl.BlockSpec((512, D), lambda i, s, k=k: (s[k], 0)) for k in range(4)]
WHOLE_STAT = pl.BlockSpec((8, 512), lambda i, s: (0, 0))
WHOLE_NORMS = pl.BlockSpec((2048, 128), lambda i, s: (0, 0))


def scores_near(idx, embeddings, cents):
    return pl.pallas_call(
        scores_near_kernel,
        grid_spec=pltpu.PrefetchScalarGridSpec(
            num_scalar_prefetch=1,
            grid=(4,),
            in_specs=[pl.BlockSpec((256, D), lambda i, s: (s[8 + i // 2] * 2 + i % 2, 0))] + CENTS_IN,
            out_specs=[
                pl.BlockSpec((2048, 256), lambda i, s: (0, i)),
                pl.BlockSpec((256, D), lambda i, s: (i, 0)),
                WHOLE_STAT,
                WHOLE_NORMS,
            ],
            scratch_shapes=[pltpu.VMEM((2048, 256), F32)],
        ),
        out_shape=[
            shape((2048, 2048), F32),
            shape((2048, D), BF),
            shape((8, 512), F32),
            shape((2048, 128), F32),
        ],
        cost_estimate=pl.CostEstimate(
            flops=2 * 2048 * 1024 * D, transcendentals=2048 * 1024, bytes_accessed=24 << 20
        ),
        name="scores_near",
    )(idx, embeddings, cents, cents, cents, cents)


def scores_far(idx, a, b, cents, norms, near, p, x):
    return pl.pallas_call(
        scores_far_kernel,
        grid_spec=pltpu.PrefetchScalarGridSpec(
            num_scalar_prefetch=1,
            grid=(4,),
            in_specs=ROW_IN + CENTS_IN + [WHOLE_NORMS, WHOLE_STAT, ANY, ANY],
            out_specs=[
                pl.BlockSpec((2048, 256), lambda i, s: (0, 4 + i)),
                pl.BlockSpec((256, D), lambda i, s: (4 + i, 0)),
                WHOLE_STAT,
            ],
            scratch_shapes=[pltpu.VMEM((2048, 256), F32)],
        ),
        out_shape=[shape((2048, 2048), F32), shape((2048, D), BF), shape((8, 512), F32)],
        input_output_aliases={9: 0, 10: 1},
        name="scores_far",
    )(idx, a, b, cents, cents, cents, cents, norms, near, p, x)


def merge_all(stats):
    m = stats[0][0:4]
    for t in stats[1:]:
        m = jnp.maximum(m, t[0:4])
    total = None
    for t in stats:
        part = t[4:8] * jnp.exp(t[0:4] - m)
        total = part if total is None else total + part
    return m, total


def merge_cores(local, other):
    def kernel(a, b, o_ref):
        m, total = merge_all([a[...], b[...]])
        both = jnp.concatenate([m, total], axis=0)
        for i in range(16):
            o_ref[i] = both

    return pl.pallas_call(
        kernel, in_specs=[VMEM] * 2, out_shape=shape((16, 8, 512), F32), name="merge_cores"
    )(local, other)


def merge_last(idx, stats, local):
    def kernel(idx_ref, s_ref, l_ref, f_ref, tmp):
        m, total = merge_all([s_ref[i] for i in range(16)])
        tmp[0:4, :] = jnp.exp(l_ref[0:4, :] - m) / total
        for r in range(4):
            f_ref[:, r * 512 : (r + 1) * 512] = tmp[pl.ds(idx_ref[4 + r], 1), :]

    return pl.pallas_call(
        kernel,
        in_specs=[SMEM] + [VMEM] * 2,
        scratch_shapes=[pltpu.VMEM((8, 512), F32)],
        out_shape=shape((1, 2048), F32),
        name="merge_last",
    )(idx, stats, local)


def sums_far(p, factor, x, blocks, half):
    first, step = blocks[0], blocks[-1] - blocks[0]

    def kernel(p_ref, f_ref, x_ref, *refs):
        w = (p_ref[...] * f_ref[...]).astype(BF)
        sums = nn(w, x_ref[...]).astype(BF)
        packed = mass_rows(as_row(lane_sums(w))).astype(BF)
        for q in range(len(blocks)):

            @pl.when(pl.program_id(0) == q)
            def _(q=q):
                refs[q][0:256, :] = sums
                refs[q][256:272, 0:256] = packed
                refs[q][256:272, 256:D] = jnp.zeros((16, D - 256), BF)

    return pl.pallas_call(
        kernel,
        grid=(len(blocks),),
        in_specs=[
            pl.BlockSpec((256, 2048), lambda j: ((first + step * j) * 2 + half, 0)),
            pl.BlockSpec((1, 2048), lambda j: (0, 0)),
            pl.BlockSpec((2048, D), lambda j: (0, 0)),
        ],
        out_specs=[pl.BlockSpec((272, D), lambda j: (0, 0)) for k in blocks],
        out_shape=[shape((272, D), BF) for k in blocks],
        name="sums_far",
    )(p, factor, x)


def sums_rest(p, factor, x):
    def kernel(p_ref, f_ref, x_ref, g2, g1, g3, own_ref, m_ref):
        w = (p_ref[...] * f_ref[...]).astype(BF)
        sums = nn(w, x_ref[...])
        mass = as_row(lane_sums(w))
        j = pl.program_id(0)
        for q, ref in enumerate((g2, g1, g3)):

            @pl.when(j == q)
            def _(ref=ref):
                ref[0:256, :] = sums.astype(BF)
                ref[256:272, 0:256] = mass_rows(mass).astype(BF)
                ref[256:272, 256:D] = jnp.zeros((16, D - 256), BF)

        @pl.when(j >= 3)
        def _():
            own_ref[...] = sums
            m_ref[...] = mass

    return pl.pallas_call(
        kernel,
        grid=(5,),
        in_specs=[
            pl.BlockSpec((256, 2048), lambda j: (jnp.where(j < 3, (2 - j + 3 * (j // 2)) * 2 + 1, j - 3), 0)),
            pl.BlockSpec((1, 2048), lambda j: (0, 0)),
            pl.BlockSpec((2048, D), lambda j: (0, 0)),
        ],
        out_specs=[pl.BlockSpec((272, D), lambda j: (0, 0))] * 3
        + [
            pl.BlockSpec((256, D), lambda j: (jnp.maximum(j - 3, 0), 0)),
            pl.BlockSpec((1, 256), lambda j: (0, jnp.maximum(j - 3, 0))),
        ],
        out_shape=[shape((272, D), BF)] * 3 + [shape((512, D), F32), shape((1, 512), F32)],
        name="sums_rest",
    )(p, factor, x)


def finish_one(idx, own, own_mass, got, cents, half):
    def kernel(idx_ref, own_ref, m_ref, g1, g2, g3, cents_ref, pts_ref, mass_ref):
        total = m_ref[...]
        num = own_ref[...] + PRIOR * cents_ref[...].astype(F32)
        for g in (g1, g2, g3):
            extra = g[256:272, 0:256].astype(F32)
            total = total + (extra[0:1] + extra[1:2] + extra[2:3])
            num = num + g[0:256, :].astype(F32)
        mass_ref[...] = total
        pts_ref[...] = (num / (as_column(total) + PRIOR)).astype(BF)

    return pl.pallas_call(
        kernel,
        grid_spec=pltpu.PrefetchScalarGridSpec(
            num_scalar_prefetch=1,
            grid=(1,),
            in_specs=[
                pl.BlockSpec((256, D), lambda i, s: (half, 0)),
                pl.BlockSpec((1, 256), lambda i, s: (0, half)),
            ]
            + [pl.BlockSpec((272, D), lambda i, s: (0, 0))] * 3
            + [pl.BlockSpec((256, D), lambda i, s: (s[0] * 2 + half, 0))],
            out_specs=[pl.BlockSpec((256, D), lambda i, s: (0, 0)), pl.BlockSpec((1, 256), lambda i, s: (0, 0))],
        ),
        out_shape=[shape((256, D), BF), shape((1, 256), F32)],
        name="finish_one",
    )(idx, own, own_mass, *got, cents)


def turn_points(owners, points, masses):
    def kernel(owners_ref, p0, p1, m0, m1, keep_ref, give_ref, tall):
        for h, p_ref in enumerate((p0, p1)):
            for at in range(0, D, 128):
                tall[pl.ds(at, 128), h * 256 : h * 256 + 256] = p_ref[:, pl.ds(at, 128)].astype(F32).T.astype(BF)
        packed = mass_rows(jnp.concatenate([m0[...], m1[...]], axis=1)).astype(BF)
        for r in range(8):
            ref = (keep_ref, give_ref)[r // 4]
            ref[r % 4, 0:96, :] = tall[pl.ds(pl.multiple_of(owners_ref[r] * 96, 32), 96), :]
            ref[r % 4, 96:112, :] = packed

    return pl.pallas_call(
        kernel,
        in_specs=[SMEM] + [VMEM] * 4,
        scratch_shapes=[pltpu.VMEM((D, 512), BF)],
        out_shape=[shape((4, 112, 512), BF)] * 2,
        name="turn_points",
    )(owners, *points, *masses)


def pair_pieces(keep, take):
    def kernel(k_ref, t_ref, *refs):
        for k, ref in enumerate(refs, 1):
            ref[0] = k_ref[k]
            ref[1] = t_ref[k]

    return pl.pallas_call(
        kernel, in_specs=[VMEM] * 2, out_shape=[shape((2, 112, 512), BF)] * 3, name="pair_pieces"
    )(keep, take)


def gather_one(sources, keep, take, pieces):
    def kernel(sources_ref, k_ref, t_ref, r1, r2, r3, o_ref, m_ref):
        for r in range(8):
            b, k = r // 4, r % 4
            piece = (r1, r2, r3)[k - 1].at[b] if k else (k_ref, t_ref)[b].at[0]
            block = sources_ref[r]
            o_ref[:, pl.ds(pl.multiple_of(block * 512, 512), 512)] = piece[0:96, :].astype(F32)
            t = piece[96:112, :].astype(F32)
            m_ref[:, pl.ds(pl.multiple_of(block * 512, 512), 512)] = t[0:1] + t[1:2] + t[2:3]

    return pl.pallas_call(
        kernel,
        in_specs=[SMEM] + [VMEM] * 5,
        out_shape=[shape((96, 4096), F32), shape((1, 4096), F32)],
        name="gather_one",
    )(sources, keep, take, *pieces)


def join_two(a, b, rows):
    def kernel(a_ref, b_ref, o_ref, n_ref):
        if rows > 512:
            o_ref[512:rows, 512:D] = jnp.zeros((rows - 512, D - 512), BF)
        for at, ref in ((0, a_ref), (256, b_ref)):
            block = ref[...]
            n = square_norms(block)
            o_ref[at : at + 256, :] = block
            n_ref[at : at + 256, :] = jnp.broadcast_to(n, (256, 128))
            if rows > 512:
                o_ref[512:rows, at : at + 256] = mass_rows(as_row(n)).astype(BF)

    return pl.pallas_call(
        kernel,
        in_specs=[VMEM] * 2,
        out_shape=[shape((rows, D), BF), shape((512, 128), F32)],
        name="join_two",
    )(a, b)


def norms_of(block):
    def kernel(c_ref, n_ref):
        n_ref[...] = jnp.broadcast_to(square_norms(c_ref[...]), (512, 128))

    return pl.pallas_call(
        kernel, in_specs=[VMEM], out_shape=shape((512, 128), F32), name="norms_of"
    )(block)


def scores_two(places, own, theirs, two, norms, half, old=()):
    def kernel(places_ref, a_ref, b_ref, *refs):
        cents, ns = refs[0:4], (*refs[4:7], refs[-1])
        p_ref, stat_ref, scores, far_norms = refs[-4:]
        i = pl.program_id(0)

        @pl.when(i == 0)
        def _():
            row = cents[3][512:528, 0:512].astype(F32)
            row = row[0:1] + row[1:2] + row[2:3]
            far_norms[...] = jnp.broadcast_to(row, (128, 512)).T

        twice = jnp.where(i == 0, a_ref[...], b_ref[...]) * 2
        top = None
        for slot in range(8):
            here = pl.ds((slot % 2) * 256, 256)
            n = ns[slot // 2][here, :]
            s = nt(cents[slot // 2][here, :], twice) - jnp.concatenate([n, n], axis=1)
            scores[pl.ds(slot * 256, 256), :] = s
            t = fold_rows(s, jnp.maximum)
            top = t if top is None else jnp.maximum(top, t)
        m = jnp.max(top, axis=0, keepdims=True)
        total = None
        for slot in range(8):
            e = jnp.exp(scores[pl.ds(slot * 256, 256), :] - m)
            p_ref[pl.ds(pl.multiple_of(places_ref[slot] * 256, 256), 256), :] = e
            t = fold_rows(e, jnp.add)
            total = t if total is None else total + t

        @pl.when(i == 0)
        def _():
            stat_ref[...] = refs[8][...] if old else jnp.zeros_like(stat_ref)

        cols = pl.ds(pl.multiple_of((half * 2 + i) * 256, 256), 256)
        stat_ref[0:1, cols] = m
        stat_ref[1:2, cols] = jnp.sum(total, axis=0, keepdims=True)

    whole = lambda r, c: pl.BlockSpec((r, c), lambda i, s: (0, 0))
    return pl.pallas_call(
        kernel,
        grid_spec=pltpu.PrefetchScalarGridSpec(
            num_scalar_prefetch=1,
            grid=(2,),
            in_specs=[whole(256, D)] * 2 + [whole(t.shape[0], D) for t in two] + [whole(512, 128)] * 3
            + ([ANY, whole(2, 1024)] if old else []),
            out_specs=[pl.BlockSpec((2048, 256), lambda i, s: (0, half * 2 + i)), whole(2, 1024)],
            scratch_shapes=[pltpu.VMEM((2048, 256), F32), pltpu.VMEM((512, 128), F32)],
        ),
        out_shape=[shape((2048, 1024), F32), shape((2, 1024), F32)],
        input_output_aliases={10: 0} if old else {},
        name="scores_two",
    )(places, own, theirs, *two, *norms, *old)


def sums_two(p, stat, other, points):
    def kernel(p_ref, s_ref, r_ref, x0, x1, x2, x3, o_ref, rows, factor):
        @pl.when(pl.program_id(0) == 0)
        def _():
            for at, ref in zip(range(0, 1024, 256), (x0, x1, x2, x3)):
                rows[at : at + 256, :] = ref[...]
            theirs = jnp.concatenate([r_ref[:, at : at + 256] for at in (256, 0, 768, 512)], axis=1)
            mine = s_ref[...]
            m = jnp.maximum(mine[0:1], theirs[0:1])
            near = jnp.exp(mine[0:1] - m)
            total = mine[1:2] * near + theirs[1:2] * jnp.exp(theirs[0:1] - m)
            factor[0:1, :] = near / total

        w = (p_ref[...] * factor[0:1, :]).astype(BF)
        num = nn(w, rows[...])
        packed = mass_rows(as_row(lane_sums(w)))
        for q in range(32):
            for j in range(6):
                o_ref[q, j * 32 : j * 32 + 32, :] = num[q * 32 : q * 32 + 32, j * 128 : j * 128 + 128].astype(BF)
            lanes = packed[:, (q // 4) * 128 : (q // 4) * 128 + 128]
            turn = (128 - (q % 4) * 32) % 128
            o_ref[q, 192:TALL, :] = (pltpu.roll(lanes, turn, 1) if turn else lanes).astype(BF)

    whole = lambda r, c: pl.BlockSpec((r, c), lambda i: (0, 0))
    return pl.pallas_call(
        kernel,
        grid=(2,),
        in_specs=[pl.BlockSpec((1024, 1024), lambda i: (i, 0)), whole(2, 1024), whole(2, 1024)] + [whole(256, D)] * 4,
        out_specs=pl.BlockSpec((32, TALL, 128), lambda i: (i, 0, 0)),
        scratch_shapes=[pltpu.VMEM((1024, D), BF), pltpu.VMEM((8, 1024), F32)],
        out_shape=shape((64, TALL, 128), BF),
        name="sums_two",
    )(p, stat, other, *points)


def finish_two(total, cents):
    def kernel(x_ref, c_ref, o_ref):
        mass = x_ref[192:193, :] + x_ref[193:194, :] + x_ref[194:195, :]
        column = as_column(mass)[0:32] + PRIOR
        packed = mass_rows(mass).astype(BF)
        for j in range(6):
            num = x_ref[j * 32 : j * 32 + 32, :] + PRIOR * c_ref[:, j * 128 : j * 128 + 128].astype(F32)
            new = (num / column).astype(BF)
            for q in range(8):
                o_ref[q, j * 32 : j * 32 + 32, :] = new
        for q in range(8):
            o_ref[q, 192:TALL, :] = packed

    return pl.pallas_call(
        kernel, in_specs=[VMEM] * 2, out_shape=shape((8, TALL, 128), BF), name="finish_two"
    )(total, cents)


def gather_two(core, mine, theirs):
    def kernel(core_ref, a_ref, b_ref, o_ref, m_ref):
        lane = lax.broadcasted_iota(jnp.int32, (16, 128), 1)
        for ref, half in ((a_ref, core_ref[0]), (b_ref, 1 - core_ref[0])):
            start = pl.multiple_of(half * 256, 256)
            for q in range(8):
                for j in range(6):
                    o_ref[pl.ds(start + q * 32, 32), j * 128 : j * 128 + 128] = ref[q, j * 32 : j * 32 + 32, :].astype(F32)
            for g in range(2):
                row = None
                for r in range(4):
                    t = ref[g * 4 + r, 192:TALL, :].astype(F32)
                    t = pltpu.roll(t, r * 32, 1) if r else t
                    row = t if row is None else jnp.where(lane >= r * 32, t, row)
                m_ref[:, pl.ds(start + g * 128, 128)] = row[0:1] + row[1:2] + row[2:3]

    return pl.pallas_call(
        kernel,
        in_specs=[SMEM] + [VMEM] * 2,
        out_shape=[shape((512, D), F32), shape((1, 512), F32)],
        name="gather_two",
    )(core, mine, theirs)


def shift_y(x, k):
    return lax.ppermute(x, "y", [(i, (i + k) % 4) for i in range(4)])


def shift_z(x, k):
    return lax.ppermute(x, "z", [(i, (i + k) % 4) for i in range(4)])


def flip(x, axis):
    return lax.ppermute(x, axis, [(0, 1), (1, 0)])


def flip_x(x):
    return lax.ppermute(x, ("xh", "xl"), [(0, 3), (1, 2), (2, 1), (3, 0)])


def after(x, *others):
    return lax.optimization_barrier((x,) + others)[0]


def body(embeddings, cents_one, cents_two):
    y = lax.axis_index("y").astype(jnp.int32)
    xh = lax.axis_index("xh").astype(jnp.int32)
    z = lax.axis_index("z").astype(jnp.int32)
    xl = lax.axis_index("xl").astype(jnp.int32)
    c = lax.axis_index("c").astype(jnp.int32)
    halves = jnp.stack([xh * 2 + c, xh * 2 + 1 - c, 2 - xh * 2 + c, 3 - xh * 2 - c])
    idx = jnp.concatenate([xh * 4 + (y + jnp.arange(4, dtype=jnp.int32)) % 4, halves, jnp.stack([c, 1 - c])])
    slot = jnp.arange(8, dtype=jnp.int32)
    places = (y - slot) % 4 * 2 + (xh ^ (slot // 4))

    mine = lax.dynamic_slice_in_dim(embeddings, c * 512, 512, 0).astype(BF)
    far_mine = flip_x(mine)
    half_two = lax.dynamic_slice_in_dim(cents_two, c * 256, 256, 0)
    around = [shift_y(half_two, k) for k in (1, 2, 3)]

    p, x, near, norms = scores_near(idx, embeddings, cents_one)
    near_a, norms_a = join_two(after(half_two, near), around[0], 512)
    far_mine = after(far_mine, near, norms_a, around[2])
    far_other = flip(far_mine, "c")
    far_a = flip_x(after(near_a, far_mine))
    p, x, local = scores_far(idx, far_mine, far_other, cents_one, norms, near, p, x)

    spread = merge_cores(local, flip(local, "c"))
    stats = lax.all_to_all(spread, ("xh", "z", "xl"), 0, 0, tiled=True)
    near_b, norms_b = join_two(after(around[1], spread), around[2], 528)
    norms_c = norms_of(after(far_a, spread))
    factor = merge_last(idx, stats, after(local, norms_b, norms_c))

    parts_0 = sums_far(p, factor, x, (2,), 0)
    parts_0 += sums_far(p, after(factor, parts_0[0]), x, (1, 3), 0)
    got_0 = [shift_y(part, k) for part, k in zip(parts_0, (2, 1, 3))]
    far_b = flip_x(after(near_b, parts_0[1]))
    *parts_1, own, own_mass = sums_rest(p, after(factor, parts_0[1]), x)
    got_1 = [shift_y(part, k) for part, k in zip(parts_1, (2, 1, 3))]
    two = (near_a, near_b, far_a, far_b)
    norms_two = (norms_a, norms_b, norms_c)

    points_0, mass_0 = finish_one(idx, own, own_mass, got_0, cents_one, 0)
    theirs_0 = flip(points_0, "c")
    old = scores_two(places, points_0, theirs_0, two, norms_two, 0)
    points_1, mass_1 = finish_one(idx, own, after(own_mass, old[1]), got_1, cents_one, 1)
    theirs_1 = flip(points_1, "c")
    owners = (y + slot) % 4 * 2 + (xh ^ (slot // 4))
    sources = (y - slot) % 4 + (xh ^ (slot // 4)) * 4
    keep, give = turn_points(owners, (points_0, points_1), (mass_0, mass_1))
    take = flip(give, "xh")

    p2, stat2 = scores_two(places, after(points_1, give), theirs_1, two, norms_two, 1, tuple(old))
    packed = sums_two(p2, stat2, flip(stat2, "c"), (points_0, theirs_0, points_1, theirs_1))
    packed = after(packed, take)
    parts = lax.all_to_all(packed, ("y", "xh", "z", "xl"), 0, 0, tiled=True)
    pairs = pair_pieces(after(keep, packed), take)
    total = jnp.sum(after(parts, pairs[0]).astype(F32), axis=0)
    rows = lax.dynamic_slice_in_dim(cents_two, c * 256 + z * 64 + xl * 32, 32, 0)
    spread = finish_two(total, rows)
    pieces = [shift_y(after(t, spread), k) for t, k in zip(pairs, (1, 2, 3))]
    turned_one, mass_one = gather_one(sources, keep, take, pieces)
    block = after(lax.all_to_all(spread, ("z", "xl"), 0, 0, tiled=True), *pieces)
    updated_two, mass_two = gather_two(c[None], block, flip(block, "c"))
    return turned_one.T, mass_one.reshape(4096), updated_two, mass_two.reshape(512)


def solution(mesh):
    fine = Mesh(mesh.devices.reshape(4, 2, 4, 2, 2), ("y", "xh", "z", "xl", "c"))
    dp, cent = ("y", "xh"), ("z", "xl", "c")
    return jax.shard_map(
        body,
        mesh=fine,
        in_specs=(P(dp, None), P(cent, None), P(dp, None)),
        out_specs=(P(cent, dp), P(cent), P(dp, None), P(dp)),
        check_vma=False,
    )
```

```python
import jax
import jax.numpy as jnp
from jax import lax
from jax.experimental import pallas as pl
from jax.experimental.pallas import tpu as pltpu
from jax.sharding import Mesh, PartitionSpec as P

PRIOR = 0.5
BF = jnp.bfloat16
F32 = jnp.float32
D = 768
TALL = 208
SMEM = pl.BlockSpec(memory_space=pltpu.SMEM)
VMEM = pl.BlockSpec(memory_space=pltpu.VMEM)


def nt(left, right):
    return lax.dot_general(left, right, (((1,), (1,)), ((), ())), preferred_element_type=F32)


def nn(left, right):
    return lax.dot_general(left, right, (((1,), (0,)), ((), ())), preferred_element_type=F32)


def shape(dims, dtype):
    return jax.ShapeDtypeStruct(dims, dtype)


def square_norms(block):
    wide = block.astype(F32)
    return jnp.sum(wide * wide, axis=1, keepdims=True)


def fold_rows(block, op):
    parts = [block[i : i + 8] for i in range(0, block.shape[0], 8)]
    while len(parts) > 1:
        parts = [op(parts[i], parts[i + 1]) for i in range(0, len(parts) - 1, 2)] + (
            [parts[-1]] if len(parts) % 2 else []
        )
    return parts[0]


def lane_sums(w):
    wide = w.astype(F32)
    part = wide[:, 0:128]
    for j in range(128, wide.shape[1], 128):
        part = part + wide[:, j : j + 128]
    return jnp.sum(part, axis=1, keepdims=True)


def as_row(column):
    return jnp.broadcast_to(column, (column.shape[0], 128)).T[0:1, :]


def as_column(row):
    return jnp.broadcast_to(row, (128, row.shape[1])).T[:, 0:1]


def mass_rows(row):
    t = jnp.broadcast_to(row, (16, row.shape[1]))
    hi = t.astype(BF).astype(F32)
    mid = (t - hi).astype(BF).astype(F32)
    low = t - hi - mid
    at = lax.broadcasted_iota(jnp.int32, t.shape, 0)
    return jnp.where(at == 0, hi, jnp.where(at == 1, mid, jnp.where(at == 2, low, 0.0)))


def scores_step(cents, twice, norms, p_ref, scores):
    top = None
    for k in range(4):
        for h in range(2):
            at = k * 512 + h * 256
            n = norms[pl.ds(at, 256), :]
            s = nt(cents[k][pl.ds(h * 256, 256), :], twice) - jnp.concatenate([n, n], axis=1)
            scores[pl.ds(at, 256), :] = s
            t = fold_rows(s, jnp.maximum)
            top = t if top is None else jnp.maximum(top, t)
    m = jnp.max(top, axis=0, keepdims=True)
    total = None
    for at in range(0, 2048, 256):
        e = jnp.exp(scores[pl.ds(at, 256), :] - m)
        p_ref[pl.ds(at, 256), :] = e
        t = fold_rows(e, jnp.add)
        total = t if total is None else total + t
    return m, jnp.sum(total, axis=0, keepdims=True)


def put_stats(stat_ref, row, i, m, l):
    cols = pl.ds(pl.multiple_of(lax.rem(i, 2) * 256, 256), 256)
    stat_ref[pl.ds(row, 1), cols] = m
    stat_ref[pl.ds(4 + row, 1), cols] = l


def scores_near_kernel(idx, e_ref, c0, c1, c2, c3, p_ref, x_ref, stat_ref, norms_ref, scores):
    i = pl.program_id(0)
    cents = (c0, c1, c2, c3)

    @pl.when(i == 0)
    def _():
        stat_ref[...] = jnp.zeros_like(stat_ref)
        for k in range(4):
            for h in range(2):
                n = square_norms(cents[k][pl.ds(h * 256, 256), :])
                norms_ref[pl.ds(k * 512 + h * 256, 256), :] = jnp.broadcast_to(n, (256, 128))

    x = e_ref[...].astype(BF)
    x_ref[...] = x
    m, l = scores_step(cents, x * 2, norms_ref, p_ref, scores)
    put_stats(stat_ref, idx[4 + i // 2], i, m, l)


def scores_far_kernel(idx, a_ref, b_ref, c0, c1, c2, c3, norms_ref, near_ref, p_old, x_old, p_ref, x_ref, stat_ref, scores):
    i = pl.program_id(0)

    @pl.when(i == 0)
    def _():
        stat_ref[...] = near_ref[...]

    x = jnp.where(i < 2, a_ref[...], b_ref[...])
    x_ref[...] = x
    m, l = scores_step((c0, c1, c2, c3), x * 2, norms_ref, p_ref, scores)
    put_stats(stat_ref, idx[6 + i // 2], i, m, l)


ANY = pl.BlockSpec(memory_space=pl.ANY)
ROW_IN = [
    pl.BlockSpec((256, D), lambda i, s: (jnp.minimum(i, 1), 0)),
    pl.BlockSpec((256, D), lambda i, s: (jnp.maximum(i - 2, 0), 0)),
]
CENTS_IN = [pl.BlockSpec((512, D), lambda i, s, k=k: (s[k], 0)) for k in range(4)]
WHOLE_STAT = pl.BlockSpec((8, 512), lambda i, s: (0, 0))
WHOLE_NORMS = pl.BlockSpec((2048, 128), lambda i, s: (0, 0))


def scores_near(idx, embeddings, cents):
    return pl.pallas_call(
        scores_near_kernel,
        grid_spec=pltpu.PrefetchScalarGridSpec(
            num_scalar_prefetch=1,
            grid=(4,),
            in_specs=[pl.BlockSpec((256, D), lambda i, s: (s[8 + i // 2] * 2 + i % 2, 0))] + CENTS_IN,
            out_specs=[
                pl.BlockSpec((2048, 256), lambda i, s: (0, i)),
                pl.BlockSpec((256, D), lambda i, s: (i, 0)),
                WHOLE_STAT,
                WHOLE_NORMS,
            ],
            scratch_shapes=[pltpu.VMEM((2048, 256), F32)],
        ),
        out_shape=[
            shape((2048, 2048), F32),
            shape((2048, D), BF),
            shape((8, 512), F32),
            shape((2048, 128), F32),
        ],
        cost_estimate=pl.CostEstimate(
            flops=2 * 2048 * 1024 * D, transcendentals=2048 * 1024, bytes_accessed=24 << 20
        ),
        name="scores_near",
    )(idx, embeddings, cents, cents, cents, cents)


def scores_far(idx, a, b, cents, norms, near, p, x):
    return pl.pallas_call(
        scores_far_kernel,
        grid_spec=pltpu.PrefetchScalarGridSpec(
            num_scalar_prefetch=1,
            grid=(4,),
            in_specs=ROW_IN + CENTS_IN + [WHOLE_NORMS, WHOLE_STAT, ANY, ANY],
            out_specs=[
                pl.BlockSpec((2048, 256), lambda i, s: (0, 4 + i)),
                pl.BlockSpec((256, D), lambda i, s: (4 + i, 0)),
                WHOLE_STAT,
            ],
            scratch_shapes=[pltpu.VMEM((2048, 256), F32)],
        ),
        out_shape=[shape((2048, 2048), F32), shape((2048, D), BF), shape((8, 512), F32)],
        input_output_aliases={9: 0, 10: 1},
        name="scores_far",
    )(idx, a, b, cents, cents, cents, cents, norms, near, p, x)


def merge_all(stats):
    m = stats[0][0:4]
    for t in stats[1:]:
        m = jnp.maximum(m, t[0:4])
    total = None
    for t in stats:
        part = t[4:8] * jnp.exp(t[0:4] - m)
        total = part if total is None else total + part
    return m, total


def merge_cores(local, other):
    def kernel(a, b, o_ref):
        m, total = merge_all([a[...], b[...]])
        both = jnp.concatenate([m, total], axis=0)
        for i in range(16):
            o_ref[i] = both

    return pl.pallas_call(
        kernel, in_specs=[VMEM] * 2, out_shape=shape((16, 8, 512), F32), name="merge_cores"
    )(local, other)


def merge_last(idx, stats, local):
    def kernel(idx_ref, s_ref, l_ref, f_ref, tmp):
        m, total = merge_all([s_ref[i] for i in range(16)])
        tmp[0:4, :] = jnp.exp(l_ref[0:4, :] - m) / total
        for r in range(4):
            f_ref[:, r * 512 : (r + 1) * 512] = tmp[pl.ds(idx_ref[4 + r], 1), :]

    return pl.pallas_call(
        kernel,
        in_specs=[SMEM] + [VMEM] * 2,
        scratch_shapes=[pltpu.VMEM((8, 512), F32)],
        out_shape=shape((1, 2048), F32),
        name="merge_last",
    )(idx, stats, local)


def sums_far(p, factor, x, blocks, half):
    first, step = blocks[0], blocks[-1] - blocks[0]

    def kernel(p_ref, f_ref, x_ref, *refs):
        w = (p_ref[...] * f_ref[...]).astype(BF)
        sums = nn(w, x_ref[...]).astype(BF)
        packed = mass_rows(as_row(lane_sums(w))).astype(BF)
        for q in range(len(blocks)):

            @pl.when(pl.program_id(0) == q)
            def _(q=q):
                refs[q][0:256, :] = sums
                refs[q][256:272, 0:256] = packed
                refs[q][256:272, 256:D] = jnp.zeros((16, D - 256), BF)

    return pl.pallas_call(
        kernel,
        grid=(len(blocks),),
        in_specs=[
            pl.BlockSpec((256, 2048), lambda j: ((first + step * j) * 2 + half, 0)),
            pl.BlockSpec((1, 2048), lambda j: (0, 0)),
            pl.BlockSpec((2048, D), lambda j: (0, 0)),
        ],
        out_specs=[pl.BlockSpec((272, D), lambda j: (0, 0)) for k in blocks],
        out_shape=[shape((272, D), BF) for k in blocks],
        name="sums_far",
    )(p, factor, x)


def sums_rest(p, factor, x):
    def kernel(p_ref, f_ref, x_ref, g2, g1, g3, own_ref, m_ref):
        w = (p_ref[...] * f_ref[...]).astype(BF)
        sums = nn(w, x_ref[...])
        mass = as_row(lane_sums(w))
        j = pl.program_id(0)
        for q, ref in enumerate((g2, g1, g3)):

            @pl.when(j == q)
            def _(ref=ref):
                ref[0:256, :] = sums.astype(BF)
                ref[256:272, 0:256] = mass_rows(mass).astype(BF)
                ref[256:272, 256:D] = jnp.zeros((16, D - 256), BF)

        @pl.when(j >= 3)
        def _():
            own_ref[...] = sums
            m_ref[...] = mass

    return pl.pallas_call(
        kernel,
        grid=(5,),
        in_specs=[
            pl.BlockSpec((256, 2048), lambda j: (jnp.where(j < 3, (2 - j + 3 * (j // 2)) * 2 + 1, j - 3), 0)),
            pl.BlockSpec((1, 2048), lambda j: (0, 0)),
            pl.BlockSpec((2048, D), lambda j: (0, 0)),
        ],
        out_specs=[pl.BlockSpec((272, D), lambda j: (0, 0))] * 3
        + [
            pl.BlockSpec((256, D), lambda j: (jnp.maximum(j - 3, 0), 0)),
            pl.BlockSpec((1, 256), lambda j: (0, jnp.maximum(j - 3, 0))),
        ],
        out_shape=[shape((272, D), BF)] * 3 + [shape((512, D), F32), shape((1, 512), F32)],
        name="sums_rest",
    )(p, factor, x)


def finish_one(idx, own, own_mass, got, cents, half):
    def kernel(idx_ref, own_ref, m_ref, g1, g2, g3, cents_ref, pts_ref, mass_ref):
        total = m_ref[...]
        num = own_ref[...] + PRIOR * cents_ref[...].astype(F32)
        for g in (g1, g2, g3):
            extra = g[256:272, 0:256].astype(F32)
            total = total + (extra[0:1] + extra[1:2] + extra[2:3])
            num = num + g[0:256, :].astype(F32)
        mass_ref[...] = total
        pts_ref[...] = (num / (as_column(total) + PRIOR)).astype(BF)

    return pl.pallas_call(
        kernel,
        grid_spec=pltpu.PrefetchScalarGridSpec(
            num_scalar_prefetch=1,
            grid=(1,),
            in_specs=[
                pl.BlockSpec((256, D), lambda i, s: (half, 0)),
                pl.BlockSpec((1, 256), lambda i, s: (0, half)),
            ]
            + [pl.BlockSpec((272, D), lambda i, s: (0, 0))] * 3
            + [pl.BlockSpec((256, D), lambda i, s: (s[0] * 2 + half, 0))],
            out_specs=[pl.BlockSpec((256, D), lambda i, s: (0, 0)), pl.BlockSpec((1, 256), lambda i, s: (0, 0))],
        ),
        out_shape=[shape((256, D), BF), shape((1, 256), F32)],
        name="finish_one",
    )(idx, own, own_mass, *got, cents)


def turn_points(owners, points, masses):
    def kernel(owners_ref, p0, p1, m0, m1, keep_ref, give_ref, tall):
        for h, p_ref in enumerate((p0, p1)):
            for at in range(0, D, 128):
                tall[pl.ds(at, 128), h * 256 : h * 256 + 256] = p_ref[:, pl.ds(at, 128)].astype(F32).T.astype(BF)
        packed = mass_rows(jnp.concatenate([m0[...], m1[...]], axis=1)).astype(BF)
        for r in range(8):
            ref = (keep_ref, give_ref)[r // 4]
            ref[r % 4, 0:96, :] = tall[pl.ds(pl.multiple_of(owners_ref[r] * 96, 32), 96), :]
            ref[r % 4, 96:112, :] = packed

    return pl.pallas_call(
        kernel,
        in_specs=[SMEM] + [VMEM] * 4,
        scratch_shapes=[pltpu.VMEM((D, 512), BF)],
        out_shape=[shape((4, 112, 512), BF)] * 2,
        name="turn_points",
    )(owners, *points, *masses)


def pair_pieces(keep, take):
    def kernel(k_ref, t_ref, *refs):
        for k, ref in enumerate(refs, 1):
            ref[0] = k_ref[k]
            ref[1] = t_ref[k]

    return pl.pallas_call(
        kernel, in_specs=[VMEM] * 2, out_shape=[shape((2, 112, 512), BF)] * 3, name="pair_pieces"
    )(keep, take)


def gather_one(sources, keep, take, pieces):
    def kernel(sources_ref, k_ref, t_ref, r1, r2, r3, o_ref, m_ref):
        for r in range(8):
            b, k = r // 4, r % 4
            piece = (r1, r2, r3)[k - 1].at[b] if k else (k_ref, t_ref)[b].at[0]
            block = sources_ref[r]
            o_ref[:, pl.ds(pl.multiple_of(block * 512, 512), 512)] = piece[0:96, :].astype(F32)
            t = piece[96:112, :].astype(F32)
            m_ref[:, pl.ds(pl.multiple_of(block * 512, 512), 512)] = t[0:1] + t[1:2] + t[2:3]

    return pl.pallas_call(
        kernel,
        in_specs=[SMEM] + [VMEM] * 5,
        out_shape=[shape((96, 4096), F32), shape((1, 4096), F32)],
        name="gather_one",
    )(sources, keep, take, *pieces)


def join_two(a, b, rows):
    def kernel(a_ref, b_ref, o_ref, n_ref):
        if rows > 512:
            o_ref[512:rows, 512:D] = jnp.zeros((rows - 512, D - 512), BF)
        for at, ref in ((0, a_ref), (256, b_ref)):
            block = ref[...]
            n = square_norms(block)
            o_ref[at : at + 256, :] = block
            n_ref[at : at + 256, :] = jnp.broadcast_to(n, (256, 128))
            if rows > 512:
                o_ref[512:rows, at : at + 256] = mass_rows(as_row(n)).astype(BF)

    return pl.pallas_call(
        kernel,
        in_specs=[VMEM] * 2,
        out_shape=[shape((rows, D), BF), shape((512, 128), F32)],
        name="join_two",
    )(a, b)


def norms_of(block):
    def kernel(c_ref, n_ref):
        n_ref[...] = jnp.broadcast_to(square_norms(c_ref[...]), (512, 128))

    return pl.pallas_call(
        kernel, in_specs=[VMEM], out_shape=shape((512, 128), F32), name="norms_of"
    )(block)


def scores_two(places, own, theirs, two, norms, half, old=()):
    def kernel(places_ref, a_ref, b_ref, *refs):
        cents, ns = refs[0:4], (*refs[4:7], refs[-1])
        p_ref, stat_ref, scores, far_norms = refs[-4:]
        i = pl.program_id(0)

        @pl.when(i == 0)
        def _():
            row = cents[3][512:528, 0:512].astype(F32)
            row = row[0:1] + row[1:2] + row[2:3]
            far_norms[...] = jnp.broadcast_to(row, (128, 512)).T

        twice = jnp.where(i == 0, a_ref[...], b_ref[...]) * 2
        top = None
        for slot in range(8):
            here = pl.ds((slot % 2) * 256, 256)
            n = ns[slot // 2][here, :]
            s = nt(cents[slot // 2][here, :], twice) - jnp.concatenate([n, n], axis=1)
            scores[pl.ds(slot * 256, 256), :] = s
            t = fold_rows(s, jnp.maximum)
            top = t if top is None else jnp.maximum(top, t)
        m = jnp.max(top, axis=0, keepdims=True)
        total = None
        for slot in range(8):
            e = jnp.exp(scores[pl.ds(slot * 256, 256), :] - m)
            p_ref[pl.ds(pl.multiple_of(places_ref[slot] * 256, 256), 256), :] = e
            t = fold_rows(e, jnp.add)
            total = t if total is None else total + t

        @pl.when(i == 0)
        def _():
            stat_ref[...] = refs[8][...] if old else jnp.zeros_like(stat_ref)

        cols = pl.ds(pl.multiple_of((half * 2 + i) * 256, 256), 256)
        stat_ref[0:1, cols] = m
        stat_ref[1:2, cols] = jnp.sum(total, axis=0, keepdims=True)

    whole = lambda r, c: pl.BlockSpec((r, c), lambda i, s: (0, 0))
    return pl.pallas_call(
        kernel,
        grid_spec=pltpu.PrefetchScalarGridSpec(
            num_scalar_prefetch=1,
            grid=(2,),
            in_specs=[whole(256, D)] * 2 + [whole(t.shape[0], D) for t in two] + [whole(512, 128)] * 3
            + ([ANY, whole(2, 1024)] if old else []),
            out_specs=[pl.BlockSpec((2048, 256), lambda i, s: (0, half * 2 + i)), whole(2, 1024)],
            scratch_shapes=[pltpu.VMEM((2048, 256), F32), pltpu.VMEM((512, 128), F32)],
        ),
        out_shape=[shape((2048, 1024), F32), shape((2, 1024), F32)],
        input_output_aliases={10: 0} if old else {},
        name="scores_two",
    )(places, own, theirs, *two, *norms, *old)


def sums_two(p, stat, other, points):
    def kernel(p_ref, s_ref, r_ref, x0, x1, x2, x3, o_ref, rows, factor):
        @pl.when(pl.program_id(0) == 0)
        def _():
            for at, ref in zip(range(0, 1024, 256), (x0, x1, x2, x3)):
                rows[at : at + 256, :] = ref[...]
            theirs = jnp.concatenate([r_ref[:, at : at + 256] for at in (256, 0, 768, 512)], axis=1)
            mine = s_ref[...]
            m = jnp.maximum(mine[0:1], theirs[0:1])
            near = jnp.exp(mine[0:1] - m)
            total = mine[1:2] * near + theirs[1:2] * jnp.exp(theirs[0:1] - m)
            factor[0:1, :] = near / total

        w = (p_ref[...] * factor[0:1, :]).astype(BF)
        num = nn(w, rows[...])
        packed = mass_rows(as_row(lane_sums(w)))
        for q in range(32):
            for j in range(6):
                o_ref[q, j * 32 : j * 32 + 32, :] = num[q * 32 : q * 32 + 32, j * 128 : j * 128 + 128].astype(BF)
            lanes = packed[:, (q // 4) * 128 : (q // 4) * 128 + 128]
            turn = (128 - (q % 4) * 32) % 128
            o_ref[q, 192:TALL, :] = (pltpu.roll(lanes, turn, 1) if turn else lanes).astype(BF)

    whole = lambda r, c: pl.BlockSpec((r, c), lambda i: (0, 0))
    return pl.pallas_call(
        kernel,
        grid=(2,),
        in_specs=[pl.BlockSpec((1024, 1024), lambda i: (i, 0)), whole(2, 1024), whole(2, 1024)] + [whole(256, D)] * 4,
        out_specs=pl.BlockSpec((32, TALL, 128), lambda i: (i, 0, 0)),
        scratch_shapes=[pltpu.VMEM((1024, D), BF), pltpu.VMEM((8, 1024), F32)],
        out_shape=shape((64, TALL, 128), BF),
        name="sums_two",
    )(p, stat, other, *points)


def finish_two(total, cents):
    def kernel(x_ref, c_ref, o_ref):
        mass = x_ref[192:193, :] + x_ref[193:194, :] + x_ref[194:195, :]
        column = as_column(mass)[0:32] + PRIOR
        packed = mass_rows(mass).astype(BF)
        for j in range(6):
            num = x_ref[j * 32 : j * 32 + 32, :] + PRIOR * c_ref[:, j * 128 : j * 128 + 128].astype(F32)
            new = (num / column).astype(BF)
            for q in range(8):
                o_ref[q, j * 32 : j * 32 + 32, :] = new
        for q in range(8):
            o_ref[q, 192:TALL, :] = packed

    return pl.pallas_call(
        kernel, in_specs=[VMEM] * 2, out_shape=shape((8, TALL, 128), BF), name="finish_two"
    )(total, cents)


def gather_two(core, mine, theirs):
    def kernel(core_ref, a_ref, b_ref, o_ref, m_ref):
        lane = lax.broadcasted_iota(jnp.int32, (16, 128), 1)
        for ref, half in ((a_ref, core_ref[0]), (b_ref, 1 - core_ref[0])):
            start = pl.multiple_of(half * 256, 256)
            for q in range(8):
                for j in range(6):
                    o_ref[pl.ds(start + q * 32, 32), j * 128 : j * 128 + 128] = ref[q, j * 32 : j * 32 + 32, :].astype(F32)
            for g in range(2):
                row = None
                for r in range(4):
                    t = ref[g * 4 + r, 192:TALL, :].astype(F32)
                    t = pltpu.roll(t, r * 32, 1) if r else t
                    row = t if row is None else jnp.where(lane >= r * 32, t, row)
                m_ref[:, pl.ds(start + g * 128, 128)] = row[0:1] + row[1:2] + row[2:3]

    return pl.pallas_call(
        kernel,
        in_specs=[SMEM] + [VMEM] * 2,
        out_shape=[shape((512, D), F32), shape((1, 512), F32)],
        name="gather_two",
    )(core, mine, theirs)


def shift_y(x, k):
    return lax.ppermute(x, "y", [(i, (i + k) % 4) for i in range(4)])


def shift_z(x, k):
    return lax.ppermute(x, "z", [(i, (i + k) % 4) for i in range(4)])


def flip(x, axis):
    return lax.ppermute(x, axis, [(0, 1), (1, 0)])


def flip_x(x):
    return lax.ppermute(x, ("xh", "xl"), [(0, 3), (1, 2), (2, 1), (3, 0)])


def after(x, *others):
    return lax.optimization_barrier((x,) + others)[0]


def body(embeddings, cents_one, cents_two):
    y = lax.axis_index("y").astype(jnp.int32)
    xh = lax.axis_index("xh").astype(jnp.int32)
    z = lax.axis_index("z").astype(jnp.int32)
    xl = lax.axis_index("xl").astype(jnp.int32)
    c = lax.axis_index("c").astype(jnp.int32)
    halves = jnp.stack([xh * 2 + c, xh * 2 + 1 - c, 2 - xh * 2 + c, 3 - xh * 2 - c])
    idx = jnp.concatenate([xh * 4 + (y + jnp.arange(4, dtype=jnp.int32)) % 4, halves, jnp.stack([c, 1 - c])])
    slot = jnp.arange(8, dtype=jnp.int32)
    places = (y - slot) % 4 * 2 + (xh ^ (slot // 4))

    mine = lax.dynamic_slice_in_dim(embeddings, c * 512, 512, 0).astype(BF)
    far_mine = flip_x(mine)
    half_two = lax.dynamic_slice_in_dim(cents_two, c * 256, 256, 0)
    around = [shift_y(half_two, k) for k in (1, 2, 3)]

    p, x, near, norms = scores_near(idx, embeddings, cents_one)
    near_a, norms_a = join_two(after(half_two, near), around[0], 512)
    far_mine = after(far_mine, near, norms_a, around[2])
    far_other = flip(far_mine, "c")
    far_a = flip_x(after(near_a, far_mine))
    p, x, local = scores_far(idx, far_mine, far_other, cents_one, norms, near, p, x)

    spread = merge_cores(local, flip(local, "c"))
    stats = lax.all_to_all(spread, ("xh", "z", "xl"), 0, 0, tiled=True)
    near_b, norms_b = join_two(after(around[1], spread), around[2], 528)
    norms_c = norms_of(after(far_a, spread))
    factor = merge_last(idx, stats, after(local, norms_b, norms_c))

    parts_0 = sums_far(p, factor, x, (2,), 0)
    parts_0 += sums_far(p, after(factor, parts_0[0]), x, (1, 3), 0)
    got_0 = [shift_y(part, k) for part, k in zip(parts_0, (2, 1, 3))]
    far_b = flip_x(after(near_b, parts_0[1]))
    *parts_1, own, own_mass = sums_rest(p, after(factor, parts_0[1]), x)
    got_1 = [shift_y(part, k) for part, k in zip(parts_1, (2, 1, 3))]
    two = (near_a, near_b, far_a, far_b)
    norms_two = (norms_a, norms_b, norms_c)

    points_0, mass_0 = finish_one(idx, own, own_mass, got_0, cents_one, 0)
    theirs_0 = flip(points_0, "c")
    old = scores_two(places, points_0, theirs_0, two, norms_two, 0)
    points_1, mass_1 = finish_one(idx, own, after(own_mass, old[1]), got_1, cents_one, 1)
    theirs_1 = flip(points_1, "c")
    owners = (y + slot) % 4 * 2 + (xh ^ (slot // 4))
    sources = (y - slot) % 4 + (xh ^ (slot // 4)) * 4
    keep, give = turn_points(owners, (points_0, points_1), (mass_0, mass_1))
    take = flip(give, "xh")

    p2, stat2 = scores_two(places, after(points_1, give), theirs_1, two, norms_two, 1, tuple(old))
    packed = sums_two(p2, stat2, flip(stat2, "c"), (points_0, theirs_0, points_1, theirs_1))
    packed = after(packed, take)
    parts = lax.all_to_all(packed, ("y", "xh", "z", "xl"), 0, 0, tiled=True)
    pairs = pair_pieces(after(keep, packed), take)
    total = jnp.sum(after(parts, pairs[0]).astype(F32), axis=0)
    rows = lax.dynamic_slice_in_dim(cents_two, c * 256 + z * 64 + xl * 32, 32, 0)
    far_step = shift_y(pairs[1], 2)
    spread = finish_two(total, after(rows, far_step))
    pieces = [shift_y(after(pairs[0], spread), 1), far_step, shift_y(after(pairs[2], spread), 3)]
    turned_one, mass_one = gather_one(sources, keep, take, pieces)
    block = after(lax.all_to_all(spread, ("z", "xl"), 0, 0, tiled=True), *pieces)
    updated_two, mass_two = gather_two(c[None], block, flip(block, "c"))
    return turned_one.T, mass_one.reshape(4096), updated_two, mass_two.reshape(512)


def solution(mesh):
    fine = Mesh(mesh.devices.reshape(4, 2, 4, 2, 2), ("y", "xh", "z", "xl", "c"))
    dp, cent = ("y", "xh"), ("z", "xl", "c")
    return jax.shard_map(
        body,
        mesh=fine,
        in_specs=(P(dp, None), P(cent, None), P(dp, None)),
        out_specs=(P(cent, dp), P(cent), P(dp, None), P(dp)),
        check_vma=False,
    )
```

```python
import jax
import jax.numpy as jnp
from jax import lax
from jax.experimental import pallas as pl
from jax.experimental.pallas import tpu as pltpu
from jax.sharding import Mesh, PartitionSpec as P

PRIOR = 0.5
BF = jnp.bfloat16
F32 = jnp.float32
D = 768
TALL = 208
SMEM = pl.BlockSpec(memory_space=pltpu.SMEM)
VMEM = pl.BlockSpec(memory_space=pltpu.VMEM)


def nt(left, right):
    return lax.dot_general(left, right, (((1,), (1,)), ((), ())), preferred_element_type=F32)


def nn(left, right):
    return lax.dot_general(left, right, (((1,), (0,)), ((), ())), preferred_element_type=F32)


def shape(dims, dtype):
    return jax.ShapeDtypeStruct(dims, dtype)


def square_norms(block):
    wide = block.astype(F32)
    return jnp.sum(wide * wide, axis=1, keepdims=True)


def fold_rows(block, op):
    parts = [block[i : i + 8] for i in range(0, block.shape[0], 8)]
    while len(parts) > 1:
        parts = [op(parts[i], parts[i + 1]) for i in range(0, len(parts) - 1, 2)] + (
            [parts[-1]] if len(parts) % 2 else []
        )
    return parts[0]


def lane_sums(w):
    wide = w.astype(F32)
    part = wide[:, 0:128]
    for j in range(128, wide.shape[1], 128):
        part = part + wide[:, j : j + 128]
    return jnp.sum(part, axis=1, keepdims=True)


def as_row(column):
    return jnp.broadcast_to(column, (column.shape[0], 128)).T[0:1, :]


def as_column(row):
    return jnp.broadcast_to(row, (128, row.shape[1])).T[:, 0:1]


def mass_rows(row):
    t = jnp.broadcast_to(row, (16, row.shape[1]))
    hi = t.astype(BF).astype(F32)
    mid = (t - hi).astype(BF).astype(F32)
    low = t - hi - mid
    at = lax.broadcasted_iota(jnp.int32, t.shape, 0)
    return jnp.where(at == 0, hi, jnp.where(at == 1, mid, jnp.where(at == 2, low, 0.0)))


def scores_step(cents, twice, norms, p_ref, scores):
    top = None
    for k in range(4):
        for h in range(2):
            at = k * 512 + h * 256
            n = norms[pl.ds(at, 256), :]
            s = nt(cents[k][pl.ds(h * 256, 256), :], twice) - jnp.concatenate([n, n], axis=1)
            scores[pl.ds(at, 256), :] = s
            t = fold_rows(s, jnp.maximum)
            top = t if top is None else jnp.maximum(top, t)
    m = jnp.max(top, axis=0, keepdims=True)
    total = None
    for at in range(0, 2048, 256):
        e = jnp.exp(scores[pl.ds(at, 256), :] - m)
        p_ref[pl.ds(at, 256), :] = e
        t = fold_rows(e, jnp.add)
        total = t if total is None else total + t
    return m, jnp.sum(total, axis=0, keepdims=True)


def put_stats(stat_ref, row, i, m, l):
    cols = pl.ds(pl.multiple_of(lax.rem(i, 2) * 256, 256), 256)
    stat_ref[pl.ds(row, 1), cols] = m
    stat_ref[pl.ds(4 + row, 1), cols] = l


def scores_near_kernel(idx, e_ref, c0, c1, c2, c3, p_ref, x_ref, stat_ref, norms_ref, scores):
    i = pl.program_id(0)
    cents = (c0, c1, c2, c3)

    @pl.when(i == 0)
    def _():
        stat_ref[...] = jnp.zeros_like(stat_ref)
        for k in range(4):
            for h in range(2):
                n = square_norms(cents[k][pl.ds(h * 256, 256), :])
                norms_ref[pl.ds(k * 512 + h * 256, 256), :] = jnp.broadcast_to(n, (256, 128))

    x = e_ref[...].astype(BF)
    x_ref[...] = x
    m, l = scores_step(cents, x * 2, norms_ref, p_ref, scores)
    put_stats(stat_ref, idx[4 + i // 2], i, m, l)


def scores_far_kernel(idx, a_ref, b_ref, c0, c1, c2, c3, norms_ref, near_ref, p_old, x_old, p_ref, x_ref, stat_ref, scores):
    i = pl.program_id(0)

    @pl.when(i == 0)
    def _():
        stat_ref[...] = near_ref[...]

    x = jnp.where(i < 2, a_ref[...], b_ref[...])
    x_ref[...] = x
    m, l = scores_step((c0, c1, c2, c3), x * 2, norms_ref, p_ref, scores)
    put_stats(stat_ref, idx[6 + i // 2], i, m, l)


ANY = pl.BlockSpec(memory_space=pl.ANY)
ROW_IN = [
    pl.BlockSpec((256, D), lambda i, s: (jnp.minimum(i, 1), 0)),
    pl.BlockSpec((256, D), lambda i, s: (jnp.maximum(i - 2, 0), 0)),
]
CENTS_IN = [pl.BlockSpec((512, D), lambda i, s, k=k: (s[k], 0)) for k in range(4)]
WHOLE_STAT = pl.BlockSpec((8, 512), lambda i, s: (0, 0))
WHOLE_NORMS = pl.BlockSpec((2048, 128), lambda i, s: (0, 0))


def scores_near(idx, embeddings, cents):
    return pl.pallas_call(
        scores_near_kernel,
        grid_spec=pltpu.PrefetchScalarGridSpec(
            num_scalar_prefetch=1,
            grid=(4,),
            in_specs=[pl.BlockSpec((256, D), lambda i, s: (s[8 + i // 2] * 2 + i % 2, 0))] + CENTS_IN,
            out_specs=[
                pl.BlockSpec((2048, 256), lambda i, s: (0, i)),
                pl.BlockSpec((256, D), lambda i, s: (i, 0)),
                WHOLE_STAT,
                WHOLE_NORMS,
            ],
            scratch_shapes=[pltpu.VMEM((2048, 256), F32)],
        ),
        out_shape=[
            shape((2048, 2048), F32),
            shape((2048, D), BF),
            shape((8, 512), F32),
            shape((2048, 128), F32),
        ],
        cost_estimate=pl.CostEstimate(
            flops=2 * 2048 * 1024 * D, transcendentals=2048 * 1024, bytes_accessed=24 << 20
        ),
        name="scores_near",
    )(idx, embeddings, cents, cents, cents, cents)


def scores_far(idx, a, b, cents, norms, near, p, x):
    return pl.pallas_call(
        scores_far_kernel,
        grid_spec=pltpu.PrefetchScalarGridSpec(
            num_scalar_prefetch=1,
            grid=(4,),
            in_specs=ROW_IN + CENTS_IN + [WHOLE_NORMS, WHOLE_STAT, ANY, ANY],
            out_specs=[
                pl.BlockSpec((2048, 256), lambda i, s: (0, 4 + i)),
                pl.BlockSpec((256, D), lambda i, s: (4 + i, 0)),
                WHOLE_STAT,
            ],
            scratch_shapes=[pltpu.VMEM((2048, 256), F32)],
        ),
        out_shape=[shape((2048, 2048), F32), shape((2048, D), BF), shape((8, 512), F32)],
        input_output_aliases={9: 0, 10: 1},
        name="scores_far",
    )(idx, a, b, cents, cents, cents, cents, norms, near, p, x)


def merge_all(stats):
    m = stats[0][0:4]
    for t in stats[1:]:
        m = jnp.maximum(m, t[0:4])
    total = None
    for t in stats:
        part = t[4:8] * jnp.exp(t[0:4] - m)
        total = part if total is None else total + part
    return m, total


def merge_cores(local, other):
    def kernel(a, b, o_ref):
        m, total = merge_all([a[...], b[...]])
        both = jnp.concatenate([m, total], axis=0)
        for i in range(16):
            o_ref[i] = both

    return pl.pallas_call(
        kernel, in_specs=[VMEM] * 2, out_shape=shape((16, 8, 512), F32), name="merge_cores"
    )(local, other)


def merge_last(idx, stats, local):
    def kernel(idx_ref, s_ref, l_ref, f_ref, tmp):
        m, total = merge_all([s_ref[i] for i in range(16)])
        tmp[0:4, :] = jnp.exp(l_ref[0:4, :] - m) / total
        for r in range(4):
            f_ref[:, r * 512 : (r + 1) * 512] = tmp[pl.ds(idx_ref[4 + r], 1), :]

    return pl.pallas_call(
        kernel,
        in_specs=[SMEM] + [VMEM] * 2,
        scratch_shapes=[pltpu.VMEM((8, 512), F32)],
        out_shape=shape((1, 2048), F32),
        name="merge_last",
    )(idx, stats, local)


def sums_far(p, factor, x, blocks, half):
    first, step = blocks[0], blocks[-1] - blocks[0]

    def kernel(p_ref, f_ref, x_ref, *refs):
        w = (p_ref[...] * f_ref[...]).astype(BF)
        sums = nn(w, x_ref[...]).astype(BF)
        packed = mass_rows(as_row(lane_sums(w))).astype(BF)
        for q in range(len(blocks)):

            @pl.when(pl.program_id(0) == q)
            def _(q=q):
                refs[q][0:256, :] = sums
                refs[q][256:272, 0:256] = packed
                refs[q][256:272, 256:D] = jnp.zeros((16, D - 256), BF)

    return pl.pallas_call(
        kernel,
        grid=(len(blocks),),
        in_specs=[
            pl.BlockSpec((256, 2048), lambda j: ((first + step * j) * 2 + half, 0)),
            pl.BlockSpec((1, 2048), lambda j: (0, 0)),
            pl.BlockSpec((2048, D), lambda j: (0, 0)),
        ],
        out_specs=[pl.BlockSpec((272, D), lambda j: (0, 0)) for k in blocks],
        out_shape=[shape((272, D), BF) for k in blocks],
        name="sums_far",
    )(p, factor, x)


def sums_rest(p, factor, x):
    def kernel(p_ref, f_ref, x_ref, g2, g1, g3, own_ref, m_ref):
        w = (p_ref[...] * f_ref[...]).astype(BF)
        sums = nn(w, x_ref[...])
        mass = as_row(lane_sums(w))
        j = pl.program_id(0)
        for q, ref in enumerate((g2, g1, g3)):

            @pl.when(j == q)
            def _(ref=ref):
                ref[0:256, :] = sums.astype(BF)
                ref[256:272, 0:256] = mass_rows(mass).astype(BF)
                ref[256:272, 256:D] = jnp.zeros((16, D - 256), BF)

        @pl.when(j >= 3)
        def _():
            own_ref[...] = sums
            m_ref[...] = mass

    return pl.pallas_call(
        kernel,
        grid=(5,),
        in_specs=[
            pl.BlockSpec((256, 2048), lambda j: (jnp.where(j < 3, (2 - j + 3 * (j // 2)) * 2 + 1, j - 3), 0)),
            pl.BlockSpec((1, 2048), lambda j: (0, 0)),
            pl.BlockSpec((2048, D), lambda j: (0, 0)),
        ],
        out_specs=[pl.BlockSpec((272, D), lambda j: (0, 0))] * 3
        + [
            pl.BlockSpec((256, D), lambda j: (jnp.maximum(j - 3, 0), 0)),
            pl.BlockSpec((1, 256), lambda j: (0, jnp.maximum(j - 3, 0))),
        ],
        out_shape=[shape((272, D), BF)] * 3 + [shape((512, D), F32), shape((1, 512), F32)],
        name="sums_rest",
    )(p, factor, x)


def finish_one(idx, own, own_mass, got, cents, half):
    def kernel(idx_ref, own_ref, m_ref, g1, g2, g3, cents_ref, pts_ref, mass_ref):
        total = m_ref[...]
        num = own_ref[...] + PRIOR * cents_ref[...].astype(F32)
        for g in (g1, g2, g3):
            extra = g[256:272, 0:256].astype(F32)
            total = total + (extra[0:1] + extra[1:2] + extra[2:3])
            num = num + g[0:256, :].astype(F32)
        mass_ref[...] = total
        pts_ref[...] = (num / (as_column(total) + PRIOR)).astype(BF)

    return pl.pallas_call(
        kernel,
        grid_spec=pltpu.PrefetchScalarGridSpec(
            num_scalar_prefetch=1,
            grid=(1,),
            in_specs=[
                pl.BlockSpec((256, D), lambda i, s: (half, 0)),
                pl.BlockSpec((1, 256), lambda i, s: (0, half)),
            ]
            + [pl.BlockSpec((272, D), lambda i, s: (0, 0))] * 3
            + [pl.BlockSpec((256, D), lambda i, s: (s[0] * 2 + half, 0))],
            out_specs=[pl.BlockSpec((256, D), lambda i, s: (0, 0)), pl.BlockSpec((1, 256), lambda i, s: (0, 0))],
        ),
        out_shape=[shape((256, D), BF), shape((1, 256), F32)],
        name="finish_one",
    )(idx, own, own_mass, *got, cents)


def turn_points(owners, points, masses):
    def kernel(owners_ref, p0, p1, m0, m1, keep_ref, give_ref, tall):
        for h, p_ref in enumerate((p0, p1)):
            for at in range(0, D, 128):
                tall[pl.ds(at, 128), h * 256 : h * 256 + 256] = p_ref[:, pl.ds(at, 128)].astype(F32).T.astype(BF)
        packed = mass_rows(jnp.concatenate([m0[...], m1[...]], axis=1)).astype(BF)
        for r in range(8):
            ref = (keep_ref, give_ref)[r // 4]
            ref[r % 4, 0:96, :] = tall[pl.ds(pl.multiple_of(owners_ref[r] * 96, 32), 96), :]
            ref[r % 4, 96:112, :] = packed

    return pl.pallas_call(
        kernel,
        in_specs=[SMEM] + [VMEM] * 4,
        scratch_shapes=[pltpu.VMEM((D, 512), BF)],
        out_shape=[shape((4, 112, 512), BF)] * 2,
        name="turn_points",
    )(owners, *points, *masses)


def pair_pieces(keep, take):
    def kernel(k_ref, t_ref, *refs):
        for k, ref in enumerate(refs, 1):
            ref[0] = k_ref[k]
            ref[1] = t_ref[k]

    return pl.pallas_call(
        kernel, in_specs=[VMEM] * 2, out_shape=[shape((2, 112, 512), BF)] * 3, name="pair_pieces"
    )(keep, take)


def gather_one(sources, keep, take, pieces):
    def kernel(sources_ref, k_ref, t_ref, r1, r2, r3, o_ref, m_ref):
        for r in range(8):
            b, k = r // 4, r % 4
            piece = (r1, r2, r3)[k - 1].at[b] if k else (k_ref, t_ref)[b].at[0]
            block = sources_ref[r]
            o_ref[:, pl.ds(pl.multiple_of(block * 512, 512), 512)] = piece[0:96, :].astype(F32)
            t = piece[96:112, :].astype(F32)
            m_ref[:, pl.ds(pl.multiple_of(block * 512, 512), 512)] = t[0:1] + t[1:2] + t[2:3]

    return pl.pallas_call(
        kernel,
        in_specs=[SMEM] + [VMEM] * 5,
        out_shape=[shape((96, 4096), F32), shape((1, 4096), F32)],
        name="gather_one",
    )(sources, keep, take, *pieces)


def join_two(a, b, rows):
    def kernel(a_ref, b_ref, o_ref, n_ref):
        if rows > 512:
            o_ref[512:rows, 512:D] = jnp.zeros((rows - 512, D - 512), BF)
        for at, ref in ((0, a_ref), (256, b_ref)):
            block = ref[...]
            n = square_norms(block)
            o_ref[at : at + 256, :] = block
            n_ref[at : at + 256, :] = jnp.broadcast_to(n, (256, 128))
            if rows > 512:
                o_ref[512:rows, at : at + 256] = mass_rows(as_row(n)).astype(BF)

    return pl.pallas_call(
        kernel,
        in_specs=[VMEM] * 2,
        out_shape=[shape((rows, D), BF), shape((512, 128), F32)],
        name="join_two",
    )(a, b)


def norms_of(block):
    def kernel(c_ref, n_ref):
        n_ref[...] = jnp.broadcast_to(square_norms(c_ref[...]), (512, 128))

    return pl.pallas_call(
        kernel, in_specs=[VMEM], out_shape=shape((512, 128), F32), name="norms_of"
    )(block)


def scores_two(places, own, theirs, two, norms, half, old=()):
    def kernel(places_ref, a_ref, b_ref, *refs):
        cents, ns = refs[0:4], (*refs[4:7], refs[-1])
        p_ref, stat_ref, scores, far_norms = refs[-4:]
        i = pl.program_id(0)

        @pl.when(i == 0)
        def _():
            row = cents[3][512:528, 0:512].astype(F32)
            row = row[0:1] + row[1:2] + row[2:3]
            far_norms[...] = jnp.broadcast_to(row, (128, 512)).T

        twice = jnp.where(i == 0, a_ref[...], b_ref[...]) * 2
        top = None
        for slot in range(8):
            here = pl.ds((slot % 2) * 256, 256)
            n = ns[slot // 2][here, :]
            s = nt(cents[slot // 2][here, :], twice) - jnp.concatenate([n, n], axis=1)
            scores[pl.ds(slot * 256, 256), :] = s
            t = fold_rows(s, jnp.maximum)
            top = t if top is None else jnp.maximum(top, t)
        m = jnp.max(top, axis=0, keepdims=True)
        total = None
        for slot in range(8):
            e = jnp.exp(scores[pl.ds(slot * 256, 256), :] - m)
            p_ref[pl.ds(pl.multiple_of(places_ref[slot] * 256, 256), 256), :] = e
            t = fold_rows(e, jnp.add)
            total = t if total is None else total + t

        @pl.when(i == 0)
        def _():
            stat_ref[...] = refs[8][...] if old else jnp.zeros_like(stat_ref)

        cols = pl.ds(pl.multiple_of((half * 2 + i) * 256, 256), 256)
        stat_ref[0:1, cols] = m
        stat_ref[1:2, cols] = jnp.sum(total, axis=0, keepdims=True)

    whole = lambda r, c: pl.BlockSpec((r, c), lambda i, s: (0, 0))
    return pl.pallas_call(
        kernel,
        grid_spec=pltpu.PrefetchScalarGridSpec(
            num_scalar_prefetch=1,
            grid=(2,),
            in_specs=[whole(256, D)] * 2 + [whole(t.shape[0], D) for t in two] + [whole(512, 128)] * 3
            + ([ANY, whole(2, 1024)] if old else []),
            out_specs=[pl.BlockSpec((2048, 256), lambda i, s: (0, half * 2 + i)), whole(2, 1024)],
            scratch_shapes=[pltpu.VMEM((2048, 256), F32), pltpu.VMEM((512, 128), F32)],
        ),
        out_shape=[shape((2048, 1024), F32), shape((2, 1024), F32)],
        input_output_aliases={10: 0} if old else {},
        name="scores_two",
    )(places, own, theirs, *two, *norms, *old)


def sums_two(p, stat, other, points):
    def kernel(p_ref, s_ref, r_ref, x0, x1, x2, x3, o_ref, rows, factor):
        @pl.when(pl.program_id(0) == 0)
        def _():
            for at, ref in zip(range(0, 1024, 256), (x0, x1, x2, x3)):
                rows[at : at + 256, :] = ref[...]
            theirs = jnp.concatenate([r_ref[:, at : at + 256] for at in (256, 0, 768, 512)], axis=1)
            mine = s_ref[...]
            m = jnp.maximum(mine[0:1], theirs[0:1])
            near = jnp.exp(mine[0:1] - m)
            total = mine[1:2] * near + theirs[1:2] * jnp.exp(theirs[0:1] - m)
            factor[0:1, :] = near / total

        w = (p_ref[...] * factor[0:1, :]).astype(BF)
        num = nn(w, rows[...])
        packed = mass_rows(as_row(lane_sums(w)))
        for q in range(32):
            for j in range(6):
                o_ref[q, j * 32 : j * 32 + 32, :] = num[q * 32 : q * 32 + 32, j * 128 : j * 128 + 128].astype(BF)
            lanes = packed[:, (q // 4) * 128 : (q // 4) * 128 + 128]
            turn = (128 - (q % 4) * 32) % 128
            o_ref[q, 192:TALL, :] = (pltpu.roll(lanes, turn, 1) if turn else lanes).astype(BF)

    whole = lambda r, c: pl.BlockSpec((r, c), lambda i: (0, 0))
    return pl.pallas_call(
        kernel,
        grid=(2,),
        in_specs=[pl.BlockSpec((1024, 1024), lambda i: (i, 0)), whole(2, 1024), whole(2, 1024)] + [whole(256, D)] * 4,
        out_specs=pl.BlockSpec((32, TALL, 128), lambda i: (i, 0, 0)),
        scratch_shapes=[pltpu.VMEM((1024, D), BF), pltpu.VMEM((8, 1024), F32)],
        out_shape=shape((64, TALL, 128), BF),
        name="sums_two",
    )(p, stat, other, *points)


def finish_two(total, cents):
    def kernel(x_ref, c_ref, o_ref):
        mass = x_ref[192:193, :] + x_ref[193:194, :] + x_ref[194:195, :]
        column = as_column(mass)[0:32] + PRIOR
        packed = mass_rows(mass).astype(BF)
        for j in range(6):
            num = x_ref[j * 32 : j * 32 + 32, :] + PRIOR * c_ref[:, j * 128 : j * 128 + 128].astype(F32)
            new = (num / column).astype(BF)
            for q in range(8):
                o_ref[q, j * 32 : j * 32 + 32, :] = new
        for q in range(8):
            o_ref[q, 192:TALL, :] = packed

    return pl.pallas_call(
        kernel, in_specs=[VMEM] * 2, out_shape=shape((8, TALL, 128), BF), name="finish_two"
    )(total, cents)


def gather_two(core, mine, theirs):
    def kernel(core_ref, a_ref, b_ref, o_ref, m_ref):
        lane = lax.broadcasted_iota(jnp.int32, (16, 128), 1)
        for ref, half in ((a_ref, core_ref[0]), (b_ref, 1 - core_ref[0])):
            start = pl.multiple_of(half * 256, 256)
            for q in range(8):
                for j in range(6):
                    o_ref[pl.ds(start + q * 32, 32), j * 128 : j * 128 + 128] = ref[q, j * 32 : j * 32 + 32, :].astype(F32)
            for g in range(2):
                row = None
                for r in range(4):
                    t = ref[g * 4 + r, 192:TALL, :].astype(F32)
                    t = pltpu.roll(t, r * 32, 1) if r else t
                    row = t if row is None else jnp.where(lane >= r * 32, t, row)
                m_ref[:, pl.ds(start + g * 128, 128)] = row[0:1] + row[1:2] + row[2:3]

    return pl.pallas_call(
        kernel,
        in_specs=[SMEM] + [VMEM] * 2,
        out_shape=[shape((512, D), F32), shape((1, 512), F32)],
        name="gather_two",
    )(core, mine, theirs)


def shift_y(x, k):
    return lax.ppermute(x, "y", [(i, (i + k) % 4) for i in range(4)])


def shift_z(x, k):
    return lax.ppermute(x, "z", [(i, (i + k) % 4) for i in range(4)])


def flip(x, axis):
    return lax.ppermute(x, axis, [(0, 1), (1, 0)])


def flip_x(x):
    return lax.ppermute(x, ("xh", "xl"), [(0, 3), (1, 2), (2, 1), (3, 0)])


def after(x, *others):
    return lax.optimization_barrier((x,) + others)[0]


def body(embeddings, cents_one, cents_two):
    y = lax.axis_index("y").astype(jnp.int32)
    xh = lax.axis_index("xh").astype(jnp.int32)
    z = lax.axis_index("z").astype(jnp.int32)
    xl = lax.axis_index("xl").astype(jnp.int32)
    c = lax.axis_index("c").astype(jnp.int32)
    halves = jnp.stack([xh * 2 + c, xh * 2 + 1 - c, 2 - xh * 2 + c, 3 - xh * 2 - c])
    idx = jnp.concatenate([xh * 4 + (y + jnp.arange(4, dtype=jnp.int32)) % 4, halves, jnp.stack([c, 1 - c])])
    slot = jnp.arange(8, dtype=jnp.int32)
    places = (y - slot) % 4 * 2 + (xh ^ (slot // 4))

    mine = lax.dynamic_slice_in_dim(embeddings, c * 512, 512, 0).astype(BF)
    far_mine = flip_x(mine)
    half_two = lax.dynamic_slice_in_dim(cents_two, c * 256, 256, 0)
    around = [shift_y(half_two, k) for k in (1, 2, 3)]

    p, x, near, norms = scores_near(idx, embeddings, cents_one)
    near_a, norms_a = join_two(after(half_two, near), around[0], 512)
    far_mine = after(far_mine, near, norms_a, around[2])
    far_other = flip(far_mine, "c")
    far_a = flip_x(after(near_a, far_mine))
    p, x, local = scores_far(idx, far_mine, far_other, cents_one, norms, near, p, x)

    spread = merge_cores(local, flip(local, "c"))
    stats = lax.all_to_all(spread, ("xh", "z", "xl"), 0, 0, tiled=True)
    near_b, norms_b = join_two(after(around[1], spread), around[2], 528)
    norms_c = norms_of(after(far_a, spread))
    factor = merge_last(idx, stats, after(local, norms_b, norms_c))

    parts_0 = sums_far(p, factor, x, (2,), 0)
    parts_0 += sums_far(p, after(factor, parts_0[0]), x, (1, 3), 0)
    got_0 = [shift_y(part, k) for part, k in zip(parts_0, (2, 1, 3))]
    far_b = flip_x(after(near_b, parts_0[1]))
    *parts_1, own, own_mass = sums_rest(p, after(factor, parts_0[1]), x)
    got_1 = [shift_y(part, k) for part, k in zip(parts_1, (2, 1, 3))]
    two = (near_a, near_b, far_a, far_b)
    norms_two = (norms_a, norms_b, norms_c)

    points_0, mass_0 = finish_one(idx, own, own_mass, got_0, cents_one, 0)
    theirs_0 = flip(points_0, "c")
    old = scores_two(places, points_0, theirs_0, two, norms_two, 0)
    points_1, mass_1 = finish_one(idx, own, after(own_mass, old[1]), got_1, cents_one, 1)
    theirs_1 = flip(points_1, "c")
    owners = (y + slot) % 4 * 2 + (xh ^ (slot // 4))
    sources = (y - slot) % 4 + (xh ^ (slot // 4)) * 4
    keep, give = turn_points(owners, (points_0, points_1), (mass_0, mass_1))
    take = flip(give, "xh")

    p2, stat2 = scores_two(places, after(points_1, give), theirs_1, two, norms_two, 1, tuple(old))
    packed = sums_two(p2, stat2, flip(stat2, "c"), (points_0, theirs_0, points_1, theirs_1))
    packed = after(packed, take)
    parts = lax.all_to_all(packed, ("y", "xh", "z", "xl"), 0, 0, tiled=True)
    pairs = pair_pieces(after(keep, packed), take)
    total = jnp.sum(after(parts, pairs[0]).astype(F32), axis=0)
    rows = lax.dynamic_slice_in_dim(cents_two, c * 256 + z * 64 + xl * 32, 32, 0)
    one_up, one_down = shift_y(pairs[0], 1), shift_y(pairs[2], 3)
    spread = finish_two(total, after(rows, one_up, one_down))
    pieces = [one_up, shift_y(after(pairs[1], spread), 2), one_down]
    turned_one, mass_one = gather_one(sources, keep, take, pieces)
    block = after(lax.all_to_all(spread, ("z", "xl"), 0, 0, tiled=True), *pieces)
    updated_two, mass_two = gather_two(c[None], block, flip(block, "c"))
    return turned_one.T, mass_one.reshape(4096), updated_two, mass_two.reshape(512)


def solution(mesh):
    fine = Mesh(mesh.devices.reshape(4, 2, 4, 2, 2), ("y", "xh", "z", "xl", "c"))
    dp, cent = ("y", "xh"), ("z", "xl", "c")
    return jax.shard_map(
        body,
        mesh=fine,
        in_specs=(P(dp, None), P(cent, None), P(dp, None)),
        out_specs=(P(cent, dp), P(cent), P(dp, None), P(dp)),
        check_vma=False,
    )
```
